32 devices in a mesh: wide: 16 (over z, y, x), narrow: 2 (over core).
Axes of the slice: x: 2, y: 2, z: 4, core: 2. Of those that a mesh axis runs over, the one named last changes fastest.
Arguments:
- activations: bfloat16 [16384, 1024], P(('wide', 'narrow')), may hold values from -6 to 6
- segment_ids: int32 [16384], P(('wide', 'narrow')), may hold values from -1 to 511, as said below
- cotangent: bfloat16 [16384, 1024], P(('wide', 'narrow')), may hold values from -6 to 6
- querymat: bfloat16 [1024, 1024], P(('wide', 'narrow')), may hold values from -0.1875 to 0.1875
- keymat: bfloat16 [1024, 1024], P(('wide', 'narrow')), may hold values from -0.1875 to 0.1875
- valuemat: bfloat16 [1024, 1024], P(('wide', 'narrow')), may hold values from -0.1875 to 0.1875
- outmat: bfloat16 [1024, 1024], P(('wide', 'narrow')), may hold values from -0.1875 to 0.1875
- upmatrix: bfloat16 [1024, 4096], P(('wide', 'narrow')), may hold values from -0.1875 to 0.1875
- downmatrix: bfloat16 [4096, 1024], P(('wide', 'narrow')), may hold values from -0.09375 to 0.09375
- querybias: bfloat16 [1024], P(('wide', 'narrow')), may hold values from -3 to 3
- keybias: bfloat16 [1024], P(('wide', 'narrow')), may hold values from -3 to 3
- valuebias: bfloat16 [1024], P(('wide', 'narrow')), may hold values from -3 to 3
- outbias: bfloat16 [1024], P(('wide', 'narrow')), may hold values from -3 to 3
- upbias: bfloat16 [4096], P(('wide', 'narrow')), may hold values from -3 to 3
- downbias: bfloat16 [1024], P(('wide', 'narrow')), may hold values from -3 to 3
- firstgain: bfloat16 [1024], P(('wide', 'narrow')), may hold values from 0.099609375 to 1.8984375
- secondgain: bfloat16 [1024], P(('wide', 'narrow')), may hold values from 0.099609375 to 1.8984375
- thirdgain: bfloat16 [1024], P(('wide', 'narrow')), may hold values from 0.099609375 to 1.8984375
- fourthgain: bfloat16 [1024], P(('wide', 'narrow')), may hold values from 0.099609375 to 1.8984375
Outputs:
- layer_out: bfloat16 [16384, 1024], P(('wide', 'narrow'))
- input_gradient: float32 [16384, 1024], P(('wide', 'narrow'))
- querymat_gradient: float32 [1024, 1024], P(('wide', 'narrow'))
- keymat_gradient: float32 [1024, 1024], P(('wide', 'narrow'))
- valuemat_gradient: float32 [1024, 1024], P(('wide', 'narrow'))
- outmat_gradient: float32 [1024, 1024], P(('wide', 'narrow'))
- upmatrix_gradient: float32 [1024, 4096], P(('wide', 'narrow'))
- downmatrix_gradient: float32 [4096, 1024], P(('wide', 'narrow'))
- querybias_gradient: float32 [1024], P(('wide', 'narrow'))
- keybias_gradient: float32 [1024], P(('wide', 'narrow'))
- valuebias_gradient: float32 [1024], P(('wide', 'narrow'))
- outbias_gradient: float32 [1024], P(('wide', 'narrow'))
- upbias_gradient: float32 [4096], P(('wide', 'narrow'))
- downbias_gradient: float32 [1024], P(('wide', 'narrow'))
- firstgain_gradient: float32 [1024], P(('wide', 'narrow'))
- secondgain_gradient: float32 [1024], P(('wide', 'narrow'))
- thirdgain_gradient: float32 [1024], P(('wide', 'narrow'))
- fourthgain_gradient: float32 [1024], P(('wide', 'narrow'))
- output_power: float32 [], replicated
The draws below stay inside these ranges and needn't reach their ends.
Inputs may be any that keep to these rules, and one draw needn't show every extreme that they name: `segment_ids`: in each packed row of 512 slots the ids of the used slots start at 0 and never fall, each sequence being a run of equal ids; the used slots come first, 128 or more of them, and the rest hold -1; some row holds one sequence of 512 tokens, and some row holds 512 sequences of one token.
All inputs are finite; a program needn't handle non-finite values.
Results may differ from the reference program's by a relative error of at most 0.019.
Values may be sent and summed in bfloat16 or wider, within the bound.
No kernel may reach another device: no remote copies, remote signals or barrier semaphores. Data moves between devices by JAX's collectives and lax.ppermute only.
A program may use at most 256 MiB of HBM per device.

```python
import jax
import jax.numpy as jnp
from jax import lax

D = 1024
HEADS = 16
HEAD = 64
FF = 4096
TOK_DEV = 512
BLOCKS = 32
TOKENS = 16384


def draw_segment_ids(key, part):
    keys = jax.random.split(jax.random.fold_in(key, 17), 4)
    exponent = jax.random.randint(keys[0], (BLOCKS, 1), 5, 10)
    random_bits = jax.random.randint(keys[1], (BLOCKS, TOK_DEV), 0, 1 << 20)
    flags = random_bits % jnp.left_shift(jnp.int32(1), exponent) == 0
    used = jax.random.randint(keys[2], (BLOCKS, 1), TOK_DEV // 4, TOK_DEV + 1)
    chosen = jax.random.randint(keys[3], (), 0, BLOCKS)
    single = (chosen + 1) % BLOCKS
    rowsidx = jnp.arange(BLOCKS)[:, None]
    places = jnp.arange(TOK_DEV)[None, :]
    flags = flags & (rowsidx != chosen) & (places > 0) | (rowsidx == single) & (places > 0)
    used = jnp.where(rowsidx == chosen, TOK_DEV, used)
    used = jnp.where(rowsidx == single, TOK_DEV, used)
    labels = jnp.cumsum(flags.astype(jnp.int32), axis=1)
    labels = jnp.where(places < used, labels, -1)
    return labels.reshape(-1).astype(jnp.int32)


def level_of(rng, shape, pieces, low, top_value):
    factor_of, own = 1.0, jax.random.fold_in(rng, 6)
    for axis_at, blocks in pieces:
        heights = jnp.exp(jax.random.uniform(jax.random.fold_in(own, axis_at), (blocks,), jnp.float32, low / len(pieces), top_value / len(pieces)))
        factor_of = factor_of * jnp.repeat(heights, shape[axis_at] // blocks).reshape([-1 if axis == axis_at else 1 for axis in range(len(shape))])
    return factor_of


def normal_values(key, shape, width, bound, pieces=(), kind=jnp.bfloat16):
    level = level_of(key, shape, pieces, -0.22, 0.18) if pieces else 1.0
    entries = jax.random.normal(key, shape, jnp.float32) * width * level
    return jnp.minimum(jnp.maximum(entries, -bound), bound).astype(kind)


def setup_inputs(seed: int = 0) -> dict:
    streams_of = jax.random.split(jax.random.key(seed), 20)
    return {
        "activations": normal_values(streams_of[0], (TOKENS, D), 1.0, 6.0, ((0, 32),)),
        "segment_ids": draw_segment_ids(jax.random.fold_in(streams_of[19], 71), 0),
        "cotangent": normal_values(streams_of[2], (TOKENS, D), 1.0, 6.0, ((0, 32),)),
        "querymat": normal_values(streams_of[3], (D, D), D ** -0.5, 0.1875, ((0, 32),)),
        "keymat": normal_values(streams_of[4], (D, D), D ** -0.5, 0.1875, ((0, 32),)),
        "valuemat": normal_values(streams_of[5], (D, D), D ** -0.5, 0.1875, ((0, 32),)),
        "outmat": normal_values(streams_of[6], (D, D), D ** -0.5, 0.1875, ((0, 32),)),
        "upmatrix": normal_values(streams_of[7], (D, FF), D ** -0.5, 0.1875, ((0, 32),)),
        "downmatrix": normal_values(streams_of[8], (FF, D), FF ** -0.5, 0.09375, ((0, 32),)),
        "querybias": normal_values(streams_of[9], (D,), 0.5, 3.0, ((0, 32),)),
        "keybias": normal_values(streams_of[10], (D,), 0.5, 3.0, ((0, 32),)),
        "valuebias": normal_values(streams_of[11], (D,), 0.5, 3.0, ((0, 32),)),
        "outbias": normal_values(streams_of[12], (D,), 0.5, 3.0, ((0, 32),)),
        "upbias": normal_values(streams_of[13], (FF,), 0.5, 3.0, ((0, 32),)),
        "downbias": normal_values(streams_of[14], (D,), 0.5, 3.0, ((0, 32),)),
        "firstgain": jnp.clip(1.0 + 0.18 * jax.random.normal(streams_of[15], (D,), jnp.float32), 0.099609375, 1.8984375).astype(jnp.bfloat16),
        "secondgain": jnp.clip(1.0 + 0.18 * jax.random.normal(streams_of[16], (D,), jnp.float32), 0.099609375, 1.8984375).astype(jnp.bfloat16),
        "thirdgain": jnp.clip(1.0 + 0.18 * jax.random.normal(streams_of[17], (D,), jnp.float32), 0.099609375, 1.8984375).astype(jnp.bfloat16),
        "fourthgain": jnp.clip(1.0 + 0.18 * jax.random.normal(streams_of[18], (D,), jnp.float32), 0.099609375, 1.8984375).astype(jnp.bfloat16),
    }


@jax.custom_vjp
def low(v):
    return lax.optimization_barrier(v.astype(jnp.bfloat16)).astype(jnp.float32)

@jax.custom_vjp
def low_back(v):
    return v

def low_keep(v):
    return (low(v), None)

def low_pass(kept, grad):
    return (grad,)

def back_keep(v):
    return (v, None)

def back_low(kept, grad):
    return (low(grad),)
low.defvjp(low_keep, low_pass)
low_back.defvjp(back_keep, back_low)

def matmul_high(left, right):
    return jnp.dot(left, right, precision=lax.Precision.HIGHEST)

def rms_norm(values, gain):
    return values * lax.rsqrt(lax.optimization_barrier(jnp.mean(values * values, axis=-1, keepdims=True)) + 1e-06) * gain

def rotate(values, cosine, sine):
    midpoint = values.shape[-1] // 2
    first_half = values[..., :midpoint]
    second_half = values[..., midpoint:]
    return jnp.concatenate([first_half * cosine - second_half * sine, first_half * sine + second_half * cosine], axis=-1)

def positions_of(segment):
    places = jnp.arange(segment.shape[0])
    matching = segment[:, None] == segment[None, :]
    earlier = places[None, :] < places[:, None]
    return lax.optimization_barrier(jnp.sum(jnp.logical_and(matching, earlier).astype(jnp.int32), axis=1))

def angle_tables(segment):
    places = positions_of(segment).astype(jnp.float32)
    midpoint = HEAD // 2
    inverse = 10000.0 ** (-jnp.arange(midpoint).astype(jnp.float32) * 2.0 / HEAD)
    angles = places[:, None] * inverse[None, :]
    return (jnp.cos(angles)[:, None, :], jnp.sin(angles)[:, None, :])

def key_mask(segment):
    places = jnp.arange(segment.shape[0])
    matching = segment[:, None] == segment[None, :]
    allowed = matching & (segment[None, :] >= 0) & (places[None, :] <= places[:, None])
    return allowed | (places[None, :] == places[:, None])

def block_forward(params, inputs, segment):
    querymat, keymat, valuemat, outmat, upmatrix, downmatrix, querybias, keybias, valuebias, outbias, upbias, downbias, firstgain, secondgain, thirdgain, fourthgain = params
    length = inputs.shape[0]
    cosine, sine = angle_tables(segment)
    allowed = key_mask(segment)
    normed_in = low(rms_norm(inputs, firstgain))
    queries = low_back(matmul_high(normed_in, querymat) + querybias)
    keys_pre = low_back(matmul_high(normed_in, keymat) + keybias)
    values = low(low_back(matmul_high(normed_in, valuemat) + valuebias)).reshape(length, HEADS, HEAD)
    query_rot = low(rotate(queries.reshape(length, HEADS, HEAD), cosine, sine))
    key_rot = low(rotate(keys_pre.reshape(length, HEADS, HEAD), cosine, sine))
    scores = low_back(jnp.einsum('qhd,khd->hqk', query_rot, key_rot, precision=lax.Precision.HIGHEST) * 0.125)
    scores = jnp.where(allowed[None], scores, -1e+30)
    probs = jax.nn.softmax(scores, axis=-1)
    mixed = jnp.einsum('hqk,khd->qhd', low(probs), values, precision=lax.Precision.HIGHEST)
    mixed = low(low_back(mixed.reshape(length, D)))
    attended = low_back(matmul_high(mixed, outmat) + outbias)
    middle = inputs + rms_norm(attended, secondgain)
    normed_mid = low(rms_norm(middle, thirdgain))
    expanded = low_back(matmul_high(normed_mid, upmatrix) + upbias)
    activated = low(jax.nn.gelu(expanded))
    contracted = low_back(matmul_high(activated, downmatrix) + downbias)
    valid = (segment >= 0).astype(jnp.float32)
    power = jnp.sum(valid * lax.optimization_barrier(jnp.mean(contracted * contracted, axis=-1)))
    return (middle + rms_norm(contracted, fourthgain), power)

def reference(activations, segment_ids, cotangent, querymat, keymat, valuemat, outmat, upmatrix, downmatrix, querybias, keybias, valuebias, outbias, upbias, downbias, firstgain, secondgain, thirdgain, fourthgain):
    params = tuple((member.astype(jnp.float32) for member in (querymat, keymat, valuemat, outmat, upmatrix, downmatrix, querybias, keybias, valuebias, outbias, upbias, downbias, firstgain, secondgain, thirdgain, fourthgain)))
    inputs_all = activations.astype(jnp.float32).reshape(BLOCKS, TOK_DEV, D)
    segments_all = segment_ids.reshape(BLOCKS, TOK_DEV)
    seeds_all = cotangent.astype(jnp.float32).reshape(BLOCKS, TOK_DEV, D)

    def step(carried, blocked):
        totals, power_total = carried
        inputs, segment, seeds = blocked

        def forward(param_set, values):
            return block_forward(param_set, values, segment)
        outputs, pullback, power = jax.vjp(forward, params, inputs, has_aux=True)
        valid = (segment >= 0).astype(jnp.float32)[:, None]
        param_grads, input_grads = pullback(seeds * valid)
        totals = jax.tree.map(jnp.add, totals, param_grads)
        return ((totals, power_total + power), (outputs.astype(jnp.bfloat16), input_grads))
    zeros = jax.tree.map(jnp.zeros_like, params)
    (totals, power_total), (outputs, input_grads) = lax.scan(step, (zeros, jnp.zeros((), jnp.float32)), (inputs_all, segments_all, seeds_all))
    layer_out = outputs.reshape(TOKENS, D)
    input_gradient = input_grads.reshape(TOKENS, D)
    output_power = power_total / TOKENS
    return (layer_out, input_gradient, totals[0], totals[1], totals[2], totals[3], totals[4], totals[5], totals[6], totals[7], totals[8], totals[9], totals[10], totals[11], totals[12], totals[13], totals[14], totals[15], output_power)
```

```python
import jax
import jax.numpy as jnp
from jax import lax
from jax.sharding import PartitionSpec as P

HEAD = 64
AXES = ("wide", "narrow")


def rms_norm(values, gain):
    return values * lax.rsqrt(jnp.mean(values * values, axis=-1, keepdims=True) + 1e-06) * gain


def rotate(values, cosine, sine):
    midpoint = values.shape[-1] // 2
    first_half = values[..., :midpoint]
    second_half = values[..., midpoint:]
    return jnp.concatenate(
        [first_half * cosine - second_half * sine, first_half * sine + second_half * cosine],
        axis=-1,
    )


def positions_of(segment):
    places = jnp.arange(segment.shape[0])
    matching = segment[:, None] == segment[None, :]
    earlier = places[None, :] < places[:, None]
    return jnp.sum(jnp.logical_and(matching, earlier).astype(jnp.int32), axis=1)


def angle_tables(segment):
    places = positions_of(segment).astype(jnp.float32)
    midpoint = HEAD // 2
    inverse = 10000.0 ** (-jnp.arange(midpoint).astype(jnp.float32) * 2.0 / HEAD)
    angles = places[:, None] * inverse[None, :]
    return (jnp.cos(angles)[:, None, :], jnp.sin(angles)[:, None, :])


def key_mask(segment):
    places = jnp.arange(segment.shape[0])
    matching = segment[:, None] == segment[None, :]
    allowed = matching & (segment[None, :] >= 0) & (places[None, :] <= places[:, None])
    return allowed | (places[None, :] == places[:, None])


def contract_rows(left, right):
    return lax.dot_general(
        left, right, (((0,), (0,)), ((), ())), preferred_element_type=jnp.float32
    )


def times_transpose(left, right):
    return lax.dot_general(
        left, right, (((1,), (1,)), ((), ())), preferred_element_type=jnp.float32
    )


def product(left, right):
    return jnp.dot(left, right, preferred_element_type=jnp.float32)


def column_sums(values):
    return jnp.sum(values.astype(jnp.float32), axis=0)


def masked_scores(query_rot, key_rot, allowed):
    scores = (
        jnp.einsum("qhd,khd->hqk", query_rot, key_rot, preferred_element_type=jnp.float32) * 0.125
    )
    return jnp.where(allowed[None], scores, -1e30)


class Net:
    def __init__(self, wide):
        self.wide = wide
        self.me = lax.axis_index("wide")
        self.core = lax.axis_index("narrow")
        outer = []
        mask = wide // 2
        while mask > 2:
            outer.append(mask)
            mask //= 2
        self.outer = outer

    def swap(self, value, mask):
        pairs = [(d, d ^ mask) for d in range(self.wide)]
        return lax.ppermute(value, "wide", pairs)

    def sibling(self, value):
        return lax.ppermute(value, "narrow", [(0, 1), (1, 0)])

    def bit(self, mask):
        return (self.me & mask) != 0

    def grow(self, value, mask, axis):
        other = self.swap(value, mask)
        bit = self.bit(mask)
        low = jnp.where(bit, other, value)
        high = jnp.where(bit, value, other)
        return jnp.stack([low, high], axis=axis)

    def shrink(self, value, mask, axis):
        bit = self.bit(mask).astype(jnp.int32)
        mine = lax.dynamic_index_in_dim(value, bit, axis, keepdims=False)
        theirs = lax.dynamic_index_in_dim(value, 1 - bit, axis, keepdims=False)
        other = self.swap(theirs, mask)
        return (mine.astype(jnp.float32) + other.astype(jnp.float32)).astype(jnp.bfloat16)

    def gather(self, first, second):
        r, c = first.shape
        both = jnp.stack([first, second])[None]
        for mask in self.outer:
            both = self.grow(both, mask, 1).reshape(-1, 2, r, c)
        outer = both.shape[0]
        a = self.grow(both[:, 0], 1, 1)
        a = self.grow(a, 2, 1)
        b = self.grow(both[:, 1], 2, 1)
        b = self.grow(b, 1, 2)
        return jnp.stack([a, b], axis=3).reshape(outer * 4 * 2 * r, c)

    def scatter(self, full):
        rows, c = full.shape
        r = rows // (self.wide * 2)
        outer = self.wide // 4
        parts = full.reshape(outer, 2, 2, 2, r, c)
        a, b = parts[:, :, :, 0], parts[:, :, :, 1]
        a = self.shrink(self.shrink(a, 2, 1), 1, 1)
        b = self.shrink(self.shrink(b, 1, 2), 2, 1)
        both = jnp.stack([a, b], axis=1)
        for mask in reversed(self.outer):
            count = both.shape[0] // 2
            both = self.shrink(both.reshape(count, 2, 2, r, c), mask, 1)
        return both[0, 0], both[0, 1]

    def gather_small(self, value):
        other = self.sibling(value)
        core = self.core == 1
        buf = jnp.stack([jnp.where(core, other, value), jnp.where(core, value, other)])[None]
        for mask in [1, 2] + self.outer[::-1]:
            buf = self.grow(buf, mask, 0).reshape(1, -1, *value.shape)
        return buf[0]

    def total(self, value):
        value = value + self.sibling(value)
        for mask in [1, 2] + self.outer[::-1]:
            value = value + self.swap(value, mask)
        return value

    def pick(self, value, axis):
        mine = lax.dynamic_index_in_dim(value, self.core, axis, keepdims=False)
        theirs = lax.dynamic_index_in_dim(value, 1 - self.core, axis, keepdims=False)
        return mine, theirs

    def halves(self, mine, theirs):
        core = self.core == 1
        return jnp.where(core, theirs, mine), jnp.where(core, mine, theirs)

    def columns_in(self, shard):
        mine, theirs = self.pick(shard, 1)
        return self.halves(mine, self.sibling(theirs))

    def columns_out(self, first, second):
        mine, theirs = self.pick(jnp.stack([first, second]), 0)
        other = self.sibling(theirs)
        left, right = self.halves(mine, other)
        return jnp.stack([left, right], axis=1)


def shards(
    activations,
    segment_ids,
    cotangent,
    querymat,
    keymat,
    valuemat,
    outmat,
    upmatrix,
    downmatrix,
    querybias,
    keybias,
    valuebias,
    outbias,
    upbias,
    downbias,
    firstgain,
    secondgain,
    thirdgain,
    fourthgain,
):
    wide = lax.axis_size("wide")
    net = Net(wide)
    core = net.core
    length, width = activations.shape
    rows = querymat.shape[0]
    hidden = upmatrix.shape[1]
    block = hidden // (2 * wide)
    half = width // 2
    heads = width // HEAD
    f32 = jnp.float32
    bf16 = jnp.bfloat16

    nine = [querybias, keybias, valuebias, outbias, downbias, firstgain, secondgain, thirdgain, fourthgain]
    small = jnp.concatenate([jnp.concatenate(nine), upbias])
    qkv_shard = jnp.concatenate(
        [m.reshape(rows, 2, half) for m in (querymat, keymat, valuemat)], axis=2
    )
    up_shard = upmatrix.reshape(rows, wide, 2, block).transpose(0, 2, 1, 3).reshape(rows, 2, hidden // 2)
    out_shard = outmat.reshape(rows, 2, half)
    small_all = net.gather_small(small)
    qkv_mine = net.gather(*net.columns_in(qkv_shard))
    out_mine = net.gather(*net.columns_in(out_shard))
    up_mine = net.gather(*net.columns_in(up_shard))
    down_rows = downmatrix.shape[0]
    down_mine = net.gather(downmatrix[: down_rows // 2], downmatrix[down_rows // 2 :])
    qkv_theirs, out_theirs, up_theirs, down_theirs = map(
        net.sibling, (qkv_mine, out_mine, up_mine, down_mine)
    )

    vectors = small_all[:, : 9 * rows].reshape(-1, 9, rows).transpose(1, 0, 2).reshape(9, width)
    vectors = vectors.astype(f32)
    bias_query, bias_key, bias_value, bias_output, bias_down = (vectors[i] for i in range(5))
    gain_first, gain_second, gain_third, gain_fourth = (vectors[i] for i in range(5, 9))
    bias_up_pair = small_all[:, 9 * rows :].reshape(wide, 2, block).astype(f32)
    bias_up_mine, bias_up_theirs = (v.reshape(-1) for v in net.pick(bias_up_pair, 1))

    def natural(mine, theirs):
        return jnp.where(
            core == 1,
            jnp.concatenate([theirs, mine], axis=-1),
            jnp.concatenate([mine, theirs], axis=-1),
        )

    inputs = activations.astype(f32)
    cosine, sine = angle_tables(segment_ids)
    allowed = key_mask(segment_ids)
    valid_row = (segment_ids >= 0).astype(f32)
    normed_in, pull_first = jax.vjp(rms_norm, inputs, gain_first)
    normed_low = normed_in.astype(bf16)
    normed_low_theirs = net.sibling(normed_low)
    qkv_m = product(normed_low, qkv_mine)
    qkv_t = product(normed_low, qkv_theirs)
    queries, keys_pre, values_pre = (
        natural(qkv_m[:, i * half : (i + 1) * half], qkv_t[:, i * half : (i + 1) * half]) + b
        for i, b in enumerate((bias_query, bias_key, bias_value))
    )
    query_rot = rotate(queries.reshape(length, heads, HEAD), cosine, sine).astype(bf16)
    key_rot = rotate(keys_pre.reshape(length, heads, HEAD), cosine, sine).astype(bf16)
    value_low = values_pre.reshape(length, heads, HEAD).astype(bf16)
    scores = masked_scores(query_rot, key_rot, allowed)
    peak = jnp.max(scores, axis=-1, keepdims=True)
    exponent = jnp.exp(scores - peak)
    totals = jnp.sum(exponent, axis=-1, keepdims=True)
    logsum = peak + jnp.log(totals)
    probs = exponent / totals
    mixed = jnp.einsum(
        "hqk,khd->qhd", probs.astype(bf16), value_low, preferred_element_type=f32
    )
    mixed_low = mixed.reshape(length, width).astype(bf16)
    mixed_low_theirs = net.sibling(mixed_low)
    attended = natural(product(mixed_low, out_mine), product(mixed_low, out_theirs)) + bias_output
    normed_att, pull_second = jax.vjp(rms_norm, attended, gain_second)
    middle = inputs + normed_att
    normed_mid, pull_third = jax.vjp(rms_norm, middle, gain_third)
    normed_mid_low = normed_mid.astype(bf16)
    normed_mid_low_theirs = net.sibling(normed_mid_low)
    act_m_f, pull_gelu_m = jax.vjp(jax.nn.gelu, product(normed_mid_low, up_mine) + bias_up_mine)
    act_t_f, pull_gelu_t = jax.vjp(jax.nn.gelu, product(normed_mid_low, up_theirs) + bias_up_theirs)
    act_m = act_m_f.astype(bf16)
    act_t = act_t_f.astype(bf16)
    act_other = net.sibling(act_t)
    contracted = product(act_m, down_mine) + product(act_t, down_theirs) + bias_down
    local_power = jnp.sum(valid_row * jnp.mean(contracted * contracted, axis=-1))
    normed_out, pull_fourth = jax.vjp(rms_norm, contracted, gain_fourth)
    layer_out = (middle + normed_out).astype(bf16)

    seed = cotangent.astype(f32) * valid_row[:, None]
    d_contracted_f, fourth_slope = pull_fourth(seed)
    d_contracted = d_contracted_f.astype(bf16)
    d_contracted_theirs = net.sibling(d_contracted)
    down_bias_slope = column_sums(d_contracted)
    d_exp_m = pull_gelu_m(times_transpose(d_contracted, down_mine))[0].astype(bf16)
    d_exp_t = pull_gelu_t(times_transpose(d_contracted, down_theirs))[0].astype(bf16)
    d_exp_other = net.sibling(d_exp_t)

    def both_rows(a, b):
        return jnp.concatenate([a, b], axis=0)

    down_slope = contract_rows(
        both_rows(act_m, act_other), both_rows(d_contracted, d_contracted_theirs)
    ).astype(bf16)
    down_sum = net.scatter(down_slope)
    up_slope = contract_rows(
        both_rows(normed_mid_low, normed_mid_low_theirs), both_rows(d_exp_m, d_exp_other)
    ).astype(bf16)
    up_sum = net.scatter(up_slope)
    up_bias_m, up_bias_t = column_sums(d_exp_m), column_sums(d_exp_t)
    d_normed_mid = times_transpose(d_exp_m, up_mine) + times_transpose(d_exp_t, up_theirs)
    d_middle_part, third_slope = pull_third(d_normed_mid)
    d_middle = seed + d_middle_part
    d_attended_f, second_slope = pull_second(d_middle)
    d_attended = d_attended_f.astype(bf16)
    output_bias_slope = column_sums(d_attended)
    d_att_m, d_att_t = net.pick(d_attended.reshape(length, 2, half), 1)
    d_att_other = net.sibling(d_att_t)
    out_slope = contract_rows(
        both_rows(mixed_low, mixed_low_theirs), both_rows(d_att_m, d_att_other)
    ).astype(bf16)
    out_sum = net.scatter(out_slope)
    d_mixed = (
        (times_transpose(d_att_m, out_mine) + times_transpose(d_att_t, out_theirs))
        .astype(bf16)
        .reshape(length, heads, HEAD)
    )
    probs_again = jnp.exp(masked_scores(query_rot, key_rot, allowed) - logsum)
    d_values = jnp.einsum(
        "hqk,qhd->khd", probs_again.astype(bf16), d_mixed, preferred_element_type=f32
    )
    d_probs = jnp.einsum("qhd,khd->hqk", d_mixed, value_low, preferred_element_type=f32)
    row_terms = jnp.sum(probs_again * d_probs, axis=-1, keepdims=True)
    d_scores = (probs_again * (d_probs - row_terms)).astype(bf16)
    d_query_rot = (
        jnp.einsum("hqk,khd->qhd", d_scores, key_rot, preferred_element_type=f32) * 0.125
    )
    d_key_rot = (
        jnp.einsum("hqk,qhd->khd", d_scores, query_rot, preferred_element_type=f32) * 0.125
    )
    d_queries = rotate(d_query_rot, cosine, -sine).reshape(length, width).astype(bf16)
    d_keys = rotate(d_key_rot, cosine, -sine).reshape(length, width).astype(bf16)
    d_values_low = d_values.reshape(length, width).astype(bf16)
    pairs = [net.pick(v.reshape(length, 2, half), 1) for v in (d_queries, d_keys, d_values_low)]
    d_qkv_m = jnp.concatenate([p[0] for p in pairs], axis=1)
    d_qkv_t = jnp.concatenate([p[1] for p in pairs], axis=1)
    d_qkv_other = net.sibling(d_qkv_t)
    qkv_slope = contract_rows(
        both_rows(normed_low, normed_low_theirs), both_rows(d_qkv_m, d_qkv_other)
    ).astype(bf16)
    qkv_sum = net.scatter(qkv_slope)
    d_normed = times_transpose(d_qkv_m, qkv_mine) + times_transpose(d_qkv_t, qkv_theirs)
    d_inputs_part, first_slope = pull_first(d_normed)
    input_gradient = d_middle + d_inputs_part

    up_bias_low = jnp.where(core == 1, up_bias_t, up_bias_m).reshape(wide, 1, block)
    up_bias_high = jnp.where(core == 1, up_bias_m, up_bias_t).reshape(wide, 1, block)
    up_bias_slope = jnp.concatenate([up_bias_low, up_bias_high], axis=1).reshape(-1)
    small_slopes = jnp.concatenate(
        [
            column_sums(d_queries),
            column_sums(d_keys),
            column_sums(d_values_low),
            output_bias_slope,
            down_bias_slope,
            first_slope,
            second_slope,
            third_slope,
            fourth_slope,
            up_bias_slope,
            jnp.full((128,), local_power, f32),
        ]
    )
    sums = net.total(small_slopes)
    output_power = sums[-1] / (length * wide * 2)
    device = net.me * 2 + core
    own = lax.dynamic_slice_in_dim(sums[: 9 * width].reshape(9, width), device * rows, rows, 1)
    own_up = lax.dynamic_slice_in_dim(sums[9 * width : 9 * width + hidden], device * 2 * block // 2, block, 0)

    qkv_grad = net.columns_out(*qkv_sum).astype(f32)
    out_grad = net.columns_out(*out_sum).astype(f32).reshape(rows, width)
    up_grad = net.columns_out(*up_sum).astype(f32)
    up_grad = up_grad.reshape(rows, 2, wide, block).transpose(0, 2, 1, 3).reshape(rows, hidden)
    down_grad = jnp.concatenate(down_sum, axis=0).astype(f32)
    q_grad, k_grad, v_grad = (
        qkv_grad[:, :, i * half : (i + 1) * half].reshape(rows, width) for i in range(3)
    )
    return (
        layer_out,
        input_gradient,
        q_grad,
        k_grad,
        v_grad,
        out_grad,
        up_grad,
        down_grad,
        own[0],
        own[1],
        own[2],
        own[3],
        own_up,
        own[4],
        own[5],
        own[6],
        own[7],
        own[8],
        output_power,
    )


def solution(mesh):
    matrix = P(AXES, None)
    vector = P(AXES)
    return jax.shard_map(
        shards,
        mesh=mesh,
        in_specs=(matrix, vector, matrix) + (matrix,) * 6 + (vector,) * 10,
        out_specs=(matrix,) * 8 + (vector,) * 10 + (P(),),
        check_vma=False,
    )
```

```python
import jax
import jax.numpy as jnp
import functools

from jax import lax
from jax.experimental import pallas as pl
from jax.experimental.pallas import tpu as pltpu
from jax.sharding import PartitionSpec as P

HEAD = 64
AXES = ("wide", "narrow")


def rms_norm(values, gain):
    return values * lax.rsqrt(jnp.mean(values * values, axis=-1, keepdims=True) + 1e-06) * gain


def rotate(values, cosine, sine):
    midpoint = values.shape[-1] // 2
    first_half = values[..., :midpoint]
    second_half = values[..., midpoint:]
    return jnp.concatenate(
        [first_half * cosine - second_half * sine, first_half * sine + second_half * cosine],
        axis=-1,
    )


def positions_of(segment):
    places = jnp.arange(segment.shape[0])
    matching = segment[:, None] == segment[None, :]
    earlier = places[None, :] < places[:, None]
    return jnp.sum(jnp.logical_and(matching, earlier).astype(jnp.int32), axis=1)


def angle_tables(segment):
    places = positions_of(segment).astype(jnp.float32)
    midpoint = HEAD // 2
    inverse = 10000.0 ** (-jnp.arange(midpoint).astype(jnp.float32) * 2.0 / HEAD)
    angles = places[:, None] * inverse[None, :]
    return (jnp.cos(angles)[:, None, :], jnp.sin(angles)[:, None, :])


def key_mask(segment):
    places = jnp.arange(segment.shape[0])
    matching = segment[:, None] == segment[None, :]
    allowed = matching & (segment[None, :] >= 0) & (places[None, :] <= places[:, None])
    return allowed | (places[None, :] == places[:, None])


def contract_rows(left, right):
    return lax.dot_general(
        left, right, (((0,), (0,)), ((), ())), preferred_element_type=jnp.float32
    )


def times_transpose(left, right):
    return lax.dot_general(
        left, right, (((1,), (1,)), ((), ())), preferred_element_type=jnp.float32
    )


def product(left, right):
    return jnp.dot(left, right, preferred_element_type=jnp.float32)


def column_sums(values):
    return jnp.sum(values.astype(jnp.float32), axis=0)


def masked_scores(query_rot, key_rot, allowed):
    scores = (
        jnp.einsum("qhd,khd->hqk", query_rot, key_rot, preferred_element_type=jnp.float32) * 0.125
    )
    return jnp.where(allowed[None], scores, -1e30)


class Net:
    def __init__(self, wide):
        self.wide = wide
        self.me = lax.axis_index("wide")
        self.core = lax.axis_index("narrow")
        outer = []
        mask = wide // 2
        while mask > 2:
            outer.append(mask)
            mask //= 2
        self.outer = outer

    def swap(self, value, mask):
        pairs = [(d, d ^ mask) for d in range(self.wide)]
        return lax.ppermute(value, "wide", pairs)

    def sibling(self, value):
        return lax.ppermute(value, "narrow", [(0, 1), (1, 0)])

    def bit(self, mask):
        return (self.me & mask) != 0

    def grow(self, value, mask, axis):
        other = self.swap(value, mask)
        bit = self.bit(mask)
        low = jnp.where(bit, other, value)
        high = jnp.where(bit, value, other)
        return jnp.stack([low, high], axis=axis)

    def shrink(self, value, mask, axis):
        bit = self.bit(mask).astype(jnp.int32)
        mine = lax.dynamic_index_in_dim(value, bit, axis, keepdims=False)
        theirs = lax.dynamic_index_in_dim(value, 1 - bit, axis, keepdims=False)
        other = self.swap(theirs, mask)
        return (mine.astype(jnp.float32) + other.astype(jnp.float32)).astype(jnp.bfloat16)

    def gather(self, first, second):
        r, c = first.shape
        both = jnp.stack([first, second])[None]
        for mask in self.outer:
            both = self.grow(both, mask, 1).reshape(-1, 2, r, c)
        outer = both.shape[0]
        a = self.grow(both[:, 0], 1, 1)
        a = self.grow(a, 2, 1)
        b = self.grow(both[:, 1], 2, 1)
        b = self.grow(b, 1, 2)
        return jnp.stack([a, b], axis=3).reshape(outer * 4 * 2 * r, c)

    def scatter(self, full):
        rows, c = full.shape
        r = rows // (self.wide * 2)
        outer = self.wide // 4
        parts = full.reshape(outer, 2, 2, 2, r, c)
        a, b = parts[:, :, :, 0], parts[:, :, :, 1]
        a = self.shrink(self.shrink(a, 2, 1), 1, 1)
        b = self.shrink(self.shrink(b, 1, 2), 2, 1)
        both = jnp.stack([a, b], axis=1)
        for mask in reversed(self.outer):
            count = both.shape[0] // 2
            both = self.shrink(both.reshape(count, 2, 2, r, c), mask, 1)
        return both[0, 0], both[0, 1]

    def gather_small(self, value):
        other = self.sibling(value)
        core = self.core == 1
        buf = jnp.stack([jnp.where(core, other, value), jnp.where(core, value, other)])[None]
        for mask in [1, 2] + self.outer[::-1]:
            buf = self.grow(buf, mask, 0).reshape(1, -1, *value.shape)
        return buf[0]

    def total(self, value):
        value = value + self.sibling(value)
        for mask in [1, 2] + self.outer[::-1]:
            value = value + self.swap(value, mask)
        return value

    def pick(self, value, axis):
        mine = lax.dynamic_index_in_dim(value, self.core, axis, keepdims=False)
        theirs = lax.dynamic_index_in_dim(value, 1 - self.core, axis, keepdims=False)
        return mine, theirs

    def halves(self, mine, theirs):
        core = self.core == 1
        return jnp.where(core, theirs, mine), jnp.where(core, mine, theirs)

    def columns_in(self, shard):
        mine, theirs = self.pick(shard, 1)
        return self.halves(mine, self.sibling(theirs))

    def columns_out(self, first, second):
        mine, theirs = self.pick(jnp.stack([first, second]), 0)
        other = self.sibling(theirs)
        left, right = self.halves(mine, other)
        return jnp.stack([left, right], axis=1)


def shards_any(
    activations,
    segment_ids,
    cotangent,
    querymat,
    keymat,
    valuemat,
    outmat,
    upmatrix,
    downmatrix,
    querybias,
    keybias,
    valuebias,
    outbias,
    upbias,
    downbias,
    firstgain,
    secondgain,
    thirdgain,
    fourthgain,
):
    wide = lax.axis_size("wide")
    net = Net(wide)
    core = net.core
    length, width = activations.shape
    rows = querymat.shape[0]
    hidden = upmatrix.shape[1]
    block = hidden // (2 * wide)
    half = width // 2
    heads = width // HEAD
    f32 = jnp.float32
    bf16 = jnp.bfloat16

    nine = [querybias, keybias, valuebias, outbias, downbias, firstgain, secondgain, thirdgain, fourthgain]
    small = jnp.concatenate([jnp.concatenate(nine), upbias])
    qkv_shard = jnp.concatenate(
        [m.reshape(rows, 2, half) for m in (querymat, keymat, valuemat)], axis=2
    )
    up_shard = upmatrix.reshape(rows, wide, 2, block).transpose(0, 2, 1, 3).reshape(rows, 2, hidden // 2)
    out_shard = outmat.reshape(rows, 2, half)
    small_all = net.gather_small(small)
    qkv_mine = net.gather(*net.columns_in(qkv_shard))
    out_mine = net.gather(*net.columns_in(out_shard))
    up_mine = net.gather(*net.columns_in(up_shard))
    down_rows = downmatrix.shape[0]
    down_mine = net.gather(downmatrix[: down_rows // 2], downmatrix[down_rows // 2 :])
    qkv_theirs, out_theirs, up_theirs, down_theirs = map(
        net.sibling, (qkv_mine, out_mine, up_mine, down_mine)
    )

    vectors = small_all[:, : 9 * rows].reshape(-1, 9, rows).transpose(1, 0, 2).reshape(9, width)
    vectors = vectors.astype(f32)
    bias_query, bias_key, bias_value, bias_output, bias_down = (vectors[i] for i in range(5))
    gain_first, gain_second, gain_third, gain_fourth = (vectors[i] for i in range(5, 9))
    bias_up_pair = small_all[:, 9 * rows :].reshape(wide, 2, block).astype(f32)
    bias_up_mine, bias_up_theirs = (v.reshape(-1) for v in net.pick(bias_up_pair, 1))

    def natural(mine, theirs):
        return jnp.where(
            core == 1,
            jnp.concatenate([theirs, mine], axis=-1),
            jnp.concatenate([mine, theirs], axis=-1),
        )

    inputs = activations.astype(f32)
    cosine, sine = angle_tables(segment_ids)
    allowed = key_mask(segment_ids)
    valid_row = (segment_ids >= 0).astype(f32)
    normed_in, pull_first = jax.vjp(rms_norm, inputs, gain_first)
    normed_low = normed_in.astype(bf16)
    normed_low_theirs = net.sibling(normed_low)
    qkv_m = product(normed_low, qkv_mine)
    qkv_t = product(normed_low, qkv_theirs)
    queries, keys_pre, values_pre = (
        natural(qkv_m[:, i * half : (i + 1) * half], qkv_t[:, i * half : (i + 1) * half]) + b
        for i, b in enumerate((bias_query, bias_key, bias_value))
    )
    query_rot = rotate(queries.reshape(length, heads, HEAD), cosine, sine).astype(bf16)
    key_rot = rotate(keys_pre.reshape(length, heads, HEAD), cosine, sine).astype(bf16)
    value_low = values_pre.reshape(length, heads, HEAD).astype(bf16)
    scores = masked_scores(query_rot, key_rot, allowed)
    peak = jnp.max(scores, axis=-1, keepdims=True)
    exponent = jnp.exp(scores - peak)
    totals = jnp.sum(exponent, axis=-1, keepdims=True)
    logsum = peak + jnp.log(totals)
    probs = exponent / totals
    mixed = jnp.einsum(
        "hqk,khd->qhd", probs.astype(bf16), value_low, preferred_element_type=f32
    )
    mixed_low = mixed.reshape(length, width).astype(bf16)
    mixed_low_theirs = net.sibling(mixed_low)
    attended = natural(product(mixed_low, out_mine), product(mixed_low, out_theirs)) + bias_output
    normed_att, pull_second = jax.vjp(rms_norm, attended, gain_second)
    middle = inputs + normed_att
    normed_mid, pull_third = jax.vjp(rms_norm, middle, gain_third)
    normed_mid_low = normed_mid.astype(bf16)
    normed_mid_low_theirs = net.sibling(normed_mid_low)
    act_m_f, pull_gelu_m = jax.vjp(jax.nn.gelu, product(normed_mid_low, up_mine) + bias_up_mine)
    act_t_f, pull_gelu_t = jax.vjp(jax.nn.gelu, product(normed_mid_low, up_theirs) + bias_up_theirs)
    act_m = act_m_f.astype(bf16)
    act_t = act_t_f.astype(bf16)
    act_other = net.sibling(act_t)
    contracted = product(act_m, down_mine) + product(act_t, down_theirs) + bias_down
    local_power = jnp.sum(valid_row * jnp.mean(contracted * contracted, axis=-1))
    normed_out, pull_fourth = jax.vjp(rms_norm, contracted, gain_fourth)
    layer_out = (middle + normed_out).astype(bf16)

    seed = cotangent.astype(f32) * valid_row[:, None]
    d_contracted_f, fourth_slope = pull_fourth(seed)
    d_contracted = d_contracted_f.astype(bf16)
    d_contracted_theirs = net.sibling(d_contracted)
    down_bias_slope = column_sums(d_contracted)
    d_exp_m = pull_gelu_m(times_transpose(d_contracted, down_mine))[0].astype(bf16)
    d_exp_t = pull_gelu_t(times_transpose(d_contracted, down_theirs))[0].astype(bf16)
    d_exp_other = net.sibling(d_exp_t)

    def both_rows(a, b):
        return jnp.concatenate([a, b], axis=0)

    down_slope = contract_rows(
        both_rows(act_m, act_other), both_rows(d_contracted, d_contracted_theirs)
    ).astype(bf16)
    down_sum = net.scatter(down_slope)
    up_slope = contract_rows(
        both_rows(normed_mid_low, normed_mid_low_theirs), both_rows(d_exp_m, d_exp_other)
    ).astype(bf16)
    up_sum = net.scatter(up_slope)
    up_bias_m, up_bias_t = column_sums(d_exp_m), column_sums(d_exp_t)
    d_normed_mid = times_transpose(d_exp_m, up_mine) + times_transpose(d_exp_t, up_theirs)
    d_middle_part, third_slope = pull_third(d_normed_mid)
    d_middle = seed + d_middle_part
    d_attended_f, second_slope = pull_second(d_middle)
    d_attended = d_attended_f.astype(bf16)
    output_bias_slope = column_sums(d_attended)
    d_att_m, d_att_t = net.pick(d_attended.reshape(length, 2, half), 1)
    d_att_other = net.sibling(d_att_t)
    out_slope = contract_rows(
        both_rows(mixed_low, mixed_low_theirs), both_rows(d_att_m, d_att_other)
    ).astype(bf16)
    out_sum = net.scatter(out_slope)
    d_mixed = (
        (times_transpose(d_att_m, out_mine) + times_transpose(d_att_t, out_theirs))
        .astype(bf16)
        .reshape(length, heads, HEAD)
    )
    probs_again = jnp.exp(masked_scores(query_rot, key_rot, allowed) - logsum)
    d_values = jnp.einsum(
        "hqk,qhd->khd", probs_again.astype(bf16), d_mixed, preferred_element_type=f32
    )
    d_probs = jnp.einsum("qhd,khd->hqk", d_mixed, value_low, preferred_element_type=f32)
    row_terms = jnp.sum(probs_again * d_probs, axis=-1, keepdims=True)
    d_scores = (probs_again * (d_probs - row_terms)).astype(bf16)
    d_query_rot = (
        jnp.einsum("hqk,khd->qhd", d_scores, key_rot, preferred_element_type=f32) * 0.125
    )
    d_key_rot = (
        jnp.einsum("hqk,qhd->khd", d_scores, query_rot, preferred_element_type=f32) * 0.125
    )
    d_queries = rotate(d_query_rot, cosine, -sine).reshape(length, width).astype(bf16)
    d_keys = rotate(d_key_rot, cosine, -sine).reshape(length, width).astype(bf16)
    d_values_low = d_values.reshape(length, width).astype(bf16)
    pairs = [net.pick(v.reshape(length, 2, half), 1) for v in (d_queries, d_keys, d_values_low)]
    d_qkv_m = jnp.concatenate([p[0] for p in pairs], axis=1)
    d_qkv_t = jnp.concatenate([p[1] for p in pairs], axis=1)
    d_qkv_other = net.sibling(d_qkv_t)
    qkv_slope = contract_rows(
        both_rows(normed_low, normed_low_theirs), both_rows(d_qkv_m, d_qkv_other)
    ).astype(bf16)
    qkv_sum = net.scatter(qkv_slope)
    d_normed = times_transpose(d_qkv_m, qkv_mine) + times_transpose(d_qkv_t, qkv_theirs)
    d_inputs_part, first_slope = pull_first(d_normed)
    input_gradient = d_middle + d_inputs_part

    up_bias_low = jnp.where(core == 1, up_bias_t, up_bias_m).reshape(wide, 1, block)
    up_bias_high = jnp.where(core == 1, up_bias_m, up_bias_t).reshape(wide, 1, block)
    up_bias_slope = jnp.concatenate([up_bias_low, up_bias_high], axis=1).reshape(-1)
    small_slopes = jnp.concatenate(
        [
            column_sums(d_queries),
            column_sums(d_keys),
            column_sums(d_values_low),
            output_bias_slope,
            down_bias_slope,
            first_slope,
            second_slope,
            third_slope,
            fourth_slope,
            up_bias_slope,
            jnp.full((128,), local_power, f32),
        ]
    )
    sums = net.total(small_slopes)
    output_power = sums[-1] / (length * wide * 2)
    device = net.me * 2 + core
    own = lax.dynamic_slice_in_dim(sums[: 9 * width].reshape(9, width), device * rows, rows, 1)
    own_up = lax.dynamic_slice_in_dim(sums[9 * width : 9 * width + hidden], device * 2 * block // 2, block, 0)

    qkv_grad = net.columns_out(*qkv_sum).astype(f32)
    out_grad = net.columns_out(*out_sum).astype(f32).reshape(rows, width)
    up_grad = net.columns_out(*up_sum).astype(f32)
    up_grad = up_grad.reshape(rows, 2, wide, block).transpose(0, 2, 1, 3).reshape(rows, hidden)
    down_grad = jnp.concatenate(down_sum, axis=0).astype(f32)
    q_grad, k_grad, v_grad = (
        qkv_grad[:, :, i * half : (i + 1) * half].reshape(rows, width) for i in range(3)
    )
    return (
        layer_out,
        input_gradient,
        q_grad,
        k_grad,
        v_grad,
        out_grad,
        up_grad,
        down_grad,
        own[0],
        own[1],
        own[2],
        own[3],
        own_up,
        own[4],
        own[5],
        own[6],
        own[7],
        own[8],
        output_power,
    )


F32 = jnp.float32
BF16 = jnp.bfloat16
I32 = jnp.int32
EPS = 1e-06
VMEM_LIMIT = 60 * 1024 * 1024
LANES = 128
GELU_A = 0.7978845608028654
GELU_B = 0.044715


def whole_spec():
    return pl.BlockSpec(memory_space=pltpu.VMEM)


def hbm_spec():
    return pl.BlockSpec(memory_space=pl.ANY)


def smem_spec():
    return pl.BlockSpec(memory_space=pltpu.SMEM)


def params():
    return pltpu.CompilerParams(vmem_limit_bytes=VMEM_LIMIT)


def shape(dims, dtype):
    return jax.ShapeDtypeStruct(dims, dtype)


def cost(flops, bytes_accessed):
    return pl.CostEstimate(flops=flops, bytes_accessed=bytes_accessed, transcendentals=0)


def dot(a, b):
    return lax.dot_general(a, b, (((1,), (0,)), ((), ())), preferred_element_type=F32)


def dot_t(a, b):
    return lax.dot_general(a, b, (((1,), (1,)), ((), ())), preferred_element_type=F32)


def t_dot(a, b):
    return lax.dot_general(a, b, (((0,), (0,)), ((), ())), preferred_element_type=F32)


def pair_mask(place):
    return place // 4 + 4 * (place % 4)


def stack_rows(refs):
    return jnp.concatenate([ref[...].reshape(-1, ref.shape[-1]) for ref in refs], axis=0)


def inverse_rms(v):
    return lax.rsqrt(jnp.mean(v * v, axis=-1, keepdims=True) + EPS)


def rms_back(v, r, gain, e):
    ge = gain * e
    return r * ge - v * (r * r * r) * jnp.mean(v * ge, axis=-1, keepdims=True)


def row_sum(v):
    return jnp.sum(v, axis=0, keepdims=True)


def turn(v, cosine, sine):
    lane = lax.broadcasted_iota(I32, v.shape, 1)
    swapped = jnp.where((lane & 63) < 32, pltpu.roll(v, 96, 1), pltpu.roll(v, 32, 1))
    return v * cosine + swapped * sine


def project_kernel(rope, x_own, x_sib, *refs):
    own, sib = refs[:5], refs[5:10]
    bias = refs[10]
    out = refs[-1]
    y = dot(x_own[...], stack_rows(own)) + dot(x_sib[...], stack_rows(sib)) + bias[...]
    if rope:
        cosine, sine = refs[11][...], refs[12][...]
        scale = jnp.where(pl.program_id(0) == 0, 0.125, 1.0)
        for c in range(0, y.shape[1], LANES):
            out[:, c : c + LANES] = (turn(y[:, c : c + LANES], cosine, sine) * scale).astype(BF16)
    else:
        out[...] = y.astype(BF16)


def project(x_own, x_sib, pieces, first, tiles, bias, tables=()):
    t, half = x_own.shape
    tn = 1024
    weights = [
        pl.BlockSpec((*p.shape[:2], tn), lambda i, f=first: (0, 0, i + f)) for p in pieces
    ]
    return pl.pallas_call(
        functools.partial(project_kernel, bool(tables)),
        grid=(tiles,),
        in_specs=[pl.BlockSpec((t, half), lambda i: (0, 0))] * 2
        + weights
        + [pl.BlockSpec((1, tn), lambda i: (0, i))]
        + [pl.BlockSpec((t, LANES), lambda i: (0, 0))] * len(tables),
        out_specs=pl.BlockSpec((t, tn), lambda i: (0, i)),
        out_shape=shape((t, tiles * tn), BF16),
        compiler_params=params(),
        cost_estimate=cost(4 * t * half * tiles * tn, 2 * tiles * 2 * half * tn),
        name="project",
    )(x_own, x_sib, *pieces, bias, *tables)


def attend_kernel(q_ref, k_ref, v_ref, col_ref, row_ref, out_ref, lse_ref, open_ref):
    t = q_ref.shape[0]
    tile = 128

    @pl.when(pl.program_id(0) == 0)
    def _():
        rows = lax.broadcasted_iota(I32, (t, t), 0)
        cols = lax.broadcasted_iota(I32, (t, t), 1)
        ok = (col_ref[...] == row_ref[...]) & (cols <= rows)
        open_ref[...] = jnp.where(ok, 0.0, -1e30)

    for i in range(t // tile):
        rows = slice(i * tile, (i + 1) * tile)
        seen = (i + 1) * tile
        outs, sums = [], []
        for h in range(2):
            lanes = slice(h * HEAD, (h + 1) * HEAD)
            s = dot_t(q_ref[rows, lanes], k_ref[:seen, lanes]) + open_ref[rows, :seen]
            peak = jnp.max(s, axis=-1, keepdims=True)
            e = jnp.exp(s - peak)
            total = jnp.sum(e, axis=-1, keepdims=True)
            outs.append(dot(e.astype(BF16), v_ref[:seen, lanes]) / total)
            sums.append(jnp.broadcast_to(peak + jnp.log(total), (tile, HEAD)))
        out_ref[rows, :] = jnp.concatenate(outs, axis=1).astype(BF16)
        lse_ref[rows, :] = jnp.concatenate(sums, axis=1)


def attend(qk, v, col, row):
    t, width = v.shape
    steps = width // LANES
    block = lambda f: pl.BlockSpec((t, LANES), f)
    return pl.pallas_call(
        attend_kernel,
        grid=(steps,),
        in_specs=[
            block(lambda i: (0, i)),
            block(lambda i: (0, i + steps)),
            block(lambda i: (0, i)),
            pl.BlockSpec((t, 1), lambda i: (0, 0)),
            pl.BlockSpec((1, t), lambda i: (0, 0)),
        ],
        out_specs=[block(lambda i: (0, i))] * 2,
        out_shape=[shape((t, width), BF16), shape((t, width), F32)],
        scratch_shapes=[pltpu.VMEM((t, t), F32)],
        compiler_params=params(),
        cost_estimate=cost(4 * t * t * width, 10 * t * width),
        name="attend",
    )(qk, qk, v, col, row)


def attend_back_kernel(
    q_ref, k_ref, v_ref, dm_ref, lse_ref, col_ref, row_ref, cos_ref, sin_ref,
    dq_ref, dk_ref, dv_ref, sum_ref, open_ref, ak_ref, av_ref,
):
    t = q_ref.shape[0]
    tile = 128

    @pl.when(pl.program_id(0) == 0)
    def _():
        rows = lax.broadcasted_iota(I32, (t, t), 0)
        cols = lax.broadcasted_iota(I32, (t, t), 1)
        ok = (col_ref[...] == row_ref[...]) & (cols <= rows)
        open_ref[...] = jnp.where(ok, 0.0, -1e30)

    total_q = jnp.zeros((1, LANES), F32)
    for i in reversed(range(t // tile)):
        rows = slice(i * tile, (i + 1) * tile)
        seen = (i + 1) * tile
        dqs, dks, dvs = [], [], []
        for h in range(2):
            lanes = slice(h * HEAD, (h + 1) * HEAD)
            q = q_ref[rows, lanes]
            k = k_ref[:seen, lanes]
            dm = dm_ref[rows, lanes]
            s = dot_t(q, k) + open_ref[rows, :seen]
            p = jnp.exp(s - lse_ref[rows, h * HEAD : h * HEAD + 1])
            dp = dot_t(dm, v_ref[:seen, lanes])
            delta = jnp.sum(p * dp, axis=-1, keepdims=True)
            ds = (p * (dp - delta)).astype(BF16)
            dqs.append(dot(ds, k))
            dks.append(t_dot(ds, q))
            dvs.append(t_dot(p.astype(BF16), dm))
        dq = turn(jnp.concatenate(dqs, axis=1) * 0.125, cos_ref[rows, :], -sin_ref[rows, :])
        dq = dq.astype(BF16)
        dq_ref[rows, :] = dq
        total_q += row_sum(dq.astype(F32))
        dk = jnp.concatenate(dks, axis=1)
        dv = jnp.concatenate(dvs, axis=1)
        if seen == t:
            ak_ref[...] = dk
            av_ref[...] = dv
        else:
            ak_ref[:seen, :] += dk
            av_ref[:seen, :] += dv
    dk = turn(ak_ref[...], cos_ref[...], -sin_ref[...]).astype(BF16)
    dv = av_ref[...].astype(BF16)
    dk_ref[...] = dk
    dv_ref[...] = dv
    sum_ref[0:1, :] = total_q
    sum_ref[1:2, :] = row_sum(dk.astype(F32))
    sum_ref[2:3, :] = row_sum(dv.astype(F32))


def attend_back(qk, v, dm, lse, col, row, cosine, sine, first, steps):
    t, width = v.shape
    key = width // LANES
    part = steps * LANES
    block = lambda f: pl.BlockSpec((t, LANES), f)
    fixed = lambda a: pl.BlockSpec(a.shape, lambda i: (0, 0))
    here = block(lambda i: (0, i))
    read = block(lambda i: (0, i + first))
    return pl.pallas_call(
        attend_back_kernel,
        grid=(steps,),
        in_specs=[read, block(lambda i: (0, i + first + key)), read, read, read]
        + [fixed(a) for a in (col, row, cosine, sine)],
        out_specs=[here, here, here, pl.BlockSpec((8, LANES), lambda i: (0, i))],
        out_shape=[shape((t, part), BF16)] * 3 + [shape((8, part), F32)],
        scratch_shapes=[
            pltpu.VMEM((t, t), F32),
            pltpu.VMEM((t, LANES), F32),
            pltpu.VMEM((t, LANES), F32),
        ],
        compiler_params=params(),
        cost_estimate=cost(10 * t * t * part, 18 * t * part),
        name="attend_back",
    )(qk, qk, v, dm, lse, col, row, cosine, sine)


def out_kernel(mixed, order, x, bias, g2, g3, *refs):
    own, sib = refs[:5], refs[5:10]
    m_own, m_sib, att_ref, mid_ref, n_ref, n_own, n_sib = refs[10:]
    half = m_own.shape[1]
    turned = dot(mixed[...], order[...]).astype(BF16)
    m_own[...] = turned[:, :half]
    m_sib[...] = turned[:, half:]
    att = dot(turned[:, :half], stack_rows(own)) + dot(turned[:, half:], stack_rows(sib))
    att = att + bias[...]
    att_ref[...] = att
    mid = x[...].astype(F32) + att * inverse_rms(att) * g2[...]
    mid_ref[...] = mid
    normed = (mid * inverse_rms(mid) * g3[...]).astype(BF16)
    n_ref[...] = normed
    turned = dot(normed, order[...]).astype(BF16)
    n_own[...] = turned[:, :half]
    n_sib[...] = turned[:, half:]


def out_project(mixed, order, x, bias, g2, g3, pieces):
    t, width = mixed.shape
    half = width // 2
    tm = 256
    rows = lambda c: pl.BlockSpec((tm, c), lambda i: (i, 0))
    vec = pl.BlockSpec((1, width), lambda i: (0, 0))
    halves = [shape((t, half), BF16)] * 2
    return pl.pallas_call(
        out_kernel,
        grid=(t // tm,),
        in_specs=[rows(width), pl.BlockSpec((width, width), lambda i: (0, 0)), rows(width), vec, vec, vec]
        + [pl.BlockSpec((*p.shape[:2], width), lambda i: (0, 0, 1)) for p in pieces],
        out_specs=[rows(half)] * 2 + [rows(width)] * 3 + [rows(half)] * 2,
        out_shape=halves + [shape((t, width), F32)] * 2 + [shape((t, width), BF16)] + halves,
        compiler_params=params(),
        cost_estimate=cost(6 * t * width * width, 16 * t * width),
        name="out_project",
    )(mixed, order, x, bias, g2, g3, *pieces)


def up_kernel(where, x, bias, w_ref, a_own, a_sib, s_own, s_sib):
    first = where[1] == 0
    width = x.shape[1]
    for j in range(w_ref.shape[3] // 256):
        cols = slice(j * 256, (j + 1) * 256)
        y = dot(x[...], w_ref[:, 0, :, cols].reshape(width, 256)) + bias[:, cols]
        yy = y * y
        t = jnp.tanh(y * (GELU_A + (GELU_A * GELU_B) * yy))
        h = 0.5 * t + 0.5
        act = (y * h).astype(BF16)
        slope = h + (0.5 * y) * (1.0 - t * t) * (GELU_A + (3 * GELU_A * GELU_B) * yy)
        slope = slope.astype(BF16)
        dst = slice(j * 128, (j + 1) * 128)
        a0, a1, s0, s1 = act[:, :128], act[:, 128:], slope[:, :128], slope[:, 128:]
        a_own[:, dst] = jnp.where(first, a0, a1)
        a_sib[:, dst] = jnp.where(first, a1, a0)
        s_own[:, dst] = jnp.where(first, s0, s1)
        s_sib[:, dst] = jnp.where(first, s1, s0)


def up_project(where, x, bias, ffn):
    t, width = x.shape
    hidden = bias.shape[1]
    tn = ffn.shape[3]
    return pl.pallas_call(
        up_kernel,
        grid=(hidden // tn,),
        in_specs=[
            smem_spec(),
            pl.BlockSpec((t, width), lambda i: (0, 0)),
            pl.BlockSpec((1, tn), lambda i: (0, i)),
            pl.BlockSpec((ffn.shape[0], 1, ffn.shape[2], tn), lambda i: (0, i, 0, 0)),
        ],
        out_specs=[pl.BlockSpec((t, tn // 2), lambda i: (0, i))] * 4,
        out_shape=[shape((t, hidden // 2), BF16)] * 4,
        compiler_params=params(),
        cost_estimate=cost(2 * t * width * hidden, 2 * width * hidden + 4 * t * hidden),
        name="up_project",
    )(where, x, bias, ffn)


def block_at(ref, where, place):
    chip = where[0] ^ pair_mask(place)
    return ref[:, pl.ds(pl.multiple_of(chip * LANES, LANES), LANES)]


def down_copies(where, ffn, wbuf, sems):
    copies = []
    for e in range(2):
        for g in range(4):
            src = ffn.at[pl.ds(g * 4, 4), where[1] ^ e, pl.ds(4, 4)]
            copies.append(pltpu.make_async_copy(src, wbuf.at[e, g], sems.at[e * 4 + g]))
    for copy in copies:
        copy.start()
    return copies


def down_kernel(
    where, a_own, a_sib, bias, mid, cot, valid, g4, ffn,
    out_ref, dc_ref, sums_ref, power_ref, wbuf, acc, sems,
):
    copies = down_copies(where, ffn, wbuf, sems)
    width = acc.shape[1]
    for e, act in enumerate((a_own, a_sib)):
        for g in range(4):
            copies[e * 4 + g].wait()
            y = dot(act[:, g * 512 : (g + 1) * 512], wbuf[e, g].reshape(512, width))
            if e + g == 0:
                acc[...] = y + bias[...]
            else:
                acc[...] += y
    t = acc.shape[0]
    tile = 128
    power = jnp.zeros((1, 1), F32)
    gain_sum = jnp.zeros((1, acc.shape[1]), F32)
    bias_sum = jnp.zeros((1, acc.shape[1]), F32)
    gain = g4[...]
    for i in range(t // tile):
        rows = slice(i * tile, (i + 1) * tile)
        v = acc[rows, :]
        ok = valid[rows, :]
        mean = jnp.mean(v * v, axis=-1, keepdims=True)
        power += row_sum(mean * ok)
        r = lax.rsqrt(mean + EPS)
        out_ref[rows, :] = (mid[rows, :] + v * r * gain).astype(BF16)
        seed = cot[rows, :].astype(F32) * ok
        gain_sum += row_sum(v * r * seed)
        dc = rms_back(v, r, gain, seed).astype(BF16)
        dc_ref[rows, :] = dc
        bias_sum += row_sum(dc.astype(F32))
    sums_ref[0:1, :] = gain_sum
    sums_ref[1:2, :] = bias_sum
    power_ref[...] = jnp.broadcast_to(power, power_ref.shape)


def down_buffers(ffn):
    return [pltpu.VMEM((2, 4, 4, 4, ffn.shape[3], ffn.shape[4]), BF16)]


def down_project(where, a_own, a_sib, bias, mid, cot, valid, g4, ffn):
    t, width = mid.shape
    hidden = 2 * a_own.shape[1]
    return pl.pallas_call(
        down_kernel,
        in_specs=[smem_spec()] + [whole_spec()] * 7 + [hbm_spec()],
        out_specs=[whole_spec()] * 4,
        out_shape=[shape((t, width), BF16)] * 2 + [shape((8, width), F32), shape((1, LANES), F32)],
        scratch_shapes=down_buffers(ffn)
        + [pltpu.VMEM((t, width), F32), pltpu.SemaphoreType.DMA((8,))],
        compiler_params=params(),
        cost_estimate=cost(2 * t * hidden * width, 2 * hidden * width + 10 * t * width),
        name="down_project",
    )(where, a_own, a_sib, bias, mid, cot, valid, g4, ffn)


def down_back_kernel(where, dc, s_own, s_sib, ffn, de_ref, sums_ref, wbuf, sems):
    copies = down_copies(where, ffn, wbuf, sems)
    for e, slope in enumerate((s_own, s_sib)):
        for g in range(4):
            copies[e * 4 + g].wait()
            y = dot_t(dc[...], wbuf[e, g].reshape(512, -1))
            for j in range(4):
                chip = g * 4 + j
                d = y[:, j * LANES : (j + 1) * LANES] * slope[:, chip * LANES : (chip + 1) * LANES].astype(F32)
                d = d.astype(BF16)
                at = (chip * 2 + (where[1] ^ e)) * LANES
                at = pl.ds(pl.multiple_of(at, LANES), LANES)
                de_ref[:, at] = d
                sums_ref[:, at] = row_sum(d.astype(F32))


def down_back(where, dc, s_own, s_sib, ffn):
    t, width = dc.shape
    hidden = 2 * s_own.shape[1]
    return pl.pallas_call(
        down_back_kernel,
        in_specs=[smem_spec()] + [whole_spec()] * 3 + [hbm_spec()],
        out_specs=[whole_spec()] * 2,
        out_shape=[shape((t, hidden), BF16), shape((1, hidden), F32)],
        scratch_shapes=down_buffers(ffn) + [pltpu.SemaphoreType.DMA((8,))],
        compiler_params=params(),
        cost_estimate=cost(2 * t * hidden * width, 2 * hidden * width),
        name="down_back",
    )(where, dc, s_own, s_sib, ffn)


GRAD_PLACES = {
    "to_x": (14, 15, 6, 7),
    "to_y": (12, 13, 8, 9),
    "x01": (4, 5),
    "y23": (10, 11),
    "f": (0, 1, 2, 3),
}


def runs_of(places):
    return [(at, places[at : at + 2]) for at in range(0, len(places), 2)]


def slope_kernel(parts, x_own, x_oth, *refs):
    dy_own, dy_oth = refs[:parts], refs[parts : 2 * parts]
    outs = refs[2 * parts :]
    for places, out in zip(GRAD_PLACES.values(), outs):
        r = out.shape[1]
        if places == (0, 1, 2, 3):
            runs = [(0, places)]
        else:
            runs = runs_of(places)
        for at, run in runs:
            cols = slice(run[0] * r, (run[-1] + 1) * r)
            for i in range(parts):
                n = dy_own[i].shape[1]
                y = t_dot(x_own[:, cols], dy_own[i][...]) + t_dot(x_oth[:, cols], dy_oth[i][...])
                out[at : at + len(run), :, i * n : (i + 1) * n] = y.astype(BF16).reshape(len(run), r, n)


def row_slopes(x_own, x_oth, dy_own, dy_oth, tiles):
    t, half = x_own.shape
    r = half // 16
    parts = len(dy_own)
    n = dy_own[0].shape[1] // tiles
    total = n * tiles * parts
    fixed = pl.BlockSpec((t, half), lambda i: (0, 0))
    return pl.pallas_call(
        functools.partial(slope_kernel, parts),
        grid=(tiles,),
        in_specs=[fixed] * 2 + [pl.BlockSpec((t, n), lambda i: (0, i))] * (2 * parts),
        out_specs=[
            pl.BlockSpec((len(p), r, n * parts), lambda i: (0, 0, i)) for p in GRAD_PLACES.values()
        ],
        out_shape=[shape((len(p), r, total), BF16) for p in GRAD_PLACES.values()],
        compiler_params=params(),
        cost_estimate=cost(4 * t * half * total, 8 * t * total + 2 * half * total),
        name="row_slopes",
    )(x_own, x_oth, *dy_own, *dy_oth)


def block_slope_kernel(where, a_own, a_oth, dy_own, dy_oth, *outs):
    for places, out in zip(GRAD_PLACES.values(), outs):
        for at, run in runs_of(places):
            mine = jnp.concatenate([block_at(a_own, where, p) for p in run], axis=1)
            other = jnp.concatenate([block_at(a_oth, where, p) for p in run], axis=1)
            y = t_dot(mine, dy_own[...]) + t_dot(other, dy_oth[...])
            out[at : at + 2] = y.astype(BF16).reshape(2, LANES, y.shape[1])


def block_slopes(where, a_own, a_oth, dy_own, dy_oth):
    t, half = a_own.shape
    width = dy_own.shape[1]
    return pl.pallas_call(
        block_slope_kernel,
        in_specs=[smem_spec()] + [whole_spec()] * 4,
        out_specs=[whole_spec()] * 5,
        out_shape=[shape((len(p), LANES, width), BF16) for p in GRAD_PLACES.values()],
        compiler_params=params(),
        cost_estimate=cost(4 * t * half * width, 4 * t * (half + width) + 2 * half * width),
        name="block_slopes",
    )(where, a_own, a_oth, dy_own, dy_oth)


def to_natural(v, order):
    high = v.astype(BF16)
    low = (v - high.astype(F32)).astype(BF16)
    return dot_t(high, order) + dot_t(low, order)


def up_back_kernel(de, order, mid_ref, att_ref, cot, valid, g2_ref, g3_ref, w_ref, *refs):
    out_own, out_sib = refs[:5], refs[5:10]
    dmid_ref, datt_ref, dmix_ref, sums_ref, acc = refs[10:]
    step = pl.program_id(0)
    width = acc.shape[1]
    y = dot_t(de[...], w_ref[:, 0].reshape(width, -1))

    @pl.when(step == 0)
    def _():
        acc[...] = y

    @pl.when(step > 0)
    def _():
        acc[...] += y

    @pl.when(step == pl.num_programs(0) - 1)
    def _():
        tile = 256
        g2, g3 = g2_ref[...], g3_ref[...]
        w_own, w_sib = stack_rows(out_own), stack_rows(out_sib)
        sums = [jnp.zeros((1, width), F32)] * 3
        for i in range(acc.shape[0] // tile):
            rows = slice(i * tile, (i + 1) * tile)
            e = acc[rows, :]
            mid = mid_ref[rows, :]
            r3 = inverse_rms(mid)
            dmid = cot[rows, :].astype(F32) * valid[rows, :] + rms_back(mid, r3, g3, e)
            dmid_ref[rows, :] = dmid
            att = att_ref[rows, :]
            r2 = inverse_rms(att)
            datt = rms_back(att, r2, g2, dmid).astype(BF16)
            datt_ref[rows, :] = datt
            sums[0] += row_sum(mid * r3 * e)
            sums[1] += row_sum(att * r2 * dmid)
            sums[2] += row_sum(datt.astype(F32))
            turned = jnp.concatenate([dot_t(datt, w_own), dot_t(datt, w_sib)], axis=1)
            dmix_ref[rows, :] = dot_t(turned.astype(BF16), order[...]).astype(BF16)
        for i in range(3):
            sums_ref[i : i + 1, :] = sums[i]


def up_back(de, order, mid, att, cot, valid, g2, g3, ffn, out_pieces):
    t, width = mid.shape
    hidden = de.shape[1]
    tk = ffn.shape[3]
    fixed = lambda a: pl.BlockSpec(a.shape, lambda i: (0, 0))
    return pl.pallas_call(
        up_back_kernel,
        grid=(hidden // tk,),
        in_specs=[pl.BlockSpec((t, tk), lambda i: (0, i))]
        + [fixed(a) for a in (order, mid, att, cot, valid, g2, g3)]
        + [pl.BlockSpec((ffn.shape[0], 1, ffn.shape[2], tk), lambda i: (0, i, 0, 0))]
        + [pl.BlockSpec((*p.shape[:2], width), lambda i: (0, 0, 1)) for p in out_pieces],
        out_specs=[pl.BlockSpec((t, width), lambda i: (0, 0))] * 3
        + [pl.BlockSpec((8, width), lambda i: (0, 0))],
        out_shape=[shape((t, width), F32), shape((t, width), BF16), shape((t, width), BF16), shape((8, width), F32)],
        scratch_shapes=[pltpu.VMEM((t, width), F32)],
        compiler_params=params(),
        cost_estimate=cost(2 * t * width * hidden, 2 * width * hidden + 2 * t * hidden),
        name="up_back",
    )(de, order, mid, att, cot, valid, g2, g3, ffn, *out_pieces)


def in_back_kernel(dqa, dka, dva, dqb, dkb, dvb, order, x_ref, dmid_ref, g1_ref, *refs):
    qk_own, qk_sib, v_own, v_sib = refs[:5], refs[5:10], refs[10:15], refs[15:20]
    out_ref, sums_ref = refs[20:]
    width = x_ref.shape[1]
    half = width // 2
    halves = []
    for qk, v in ((qk_own, v_own), (qk_sib, v_sib)):
        w = stack_rows(qk)
        wv = stack_rows(v)
        y = dot_t(dqa[...], w[:, :half]) + dot_t(dqb[...], w[:, half:width])
        y = y + dot_t(dka[...], w[:, width : width + half]) + dot_t(dkb[...], w[:, width + half :])
        halves.append(y + dot_t(dva[...], wv[:, :half]) + dot_t(dvb[...], wv[:, half:]))
    turned = jnp.concatenate(halves, axis=1)
    gain = g1_ref[...]
    tile = 256
    total = jnp.zeros((1, width), F32)
    for i in range(x_ref.shape[0] // tile):
        rows = slice(i * tile, (i + 1) * tile)
        e = to_natural(turned[rows, :], order[...])
        x = x_ref[rows, :].astype(F32)
        r = inverse_rms(x)
        out_ref[rows, :] = dmid_ref[rows, :] + rms_back(x, r, gain, e)
        total += row_sum(x * r * e)
    sums_ref[...] = total


def in_back(d_a, d_b, order, x, dmid, g1, qk_pieces, vo_pieces):
    t, width = x.shape
    fixed = lambda a: pl.BlockSpec(a.shape, lambda i: (0, 0))
    return pl.pallas_call(
        in_back_kernel,
        grid=(1,),
        in_specs=[fixed(a) for a in (*d_a, *d_b, order, x, dmid, g1)]
        + [pl.BlockSpec(p.shape, lambda i: (0, 0, 0)) for p in qk_pieces]
        + [pl.BlockSpec((*p.shape[:2], width), lambda i: (0, 0, 0)) for p in vo_pieces],
        out_specs=[pl.BlockSpec((t, width), lambda i: (0, 0)), pl.BlockSpec((1, width), lambda i: (0, 0))],
        out_shape=[shape((t, width), F32), shape((1, width), F32)],
        compiler_params=params(),
        cost_estimate=cost(6 * t * width * width, 6 * width * width),
        name="in_back",
    )(*d_a, *d_b, order, x, dmid, g1, *qk_pieces, *vo_pieces)


def after(*values):
    return lax.optimization_barrier(values)


def add(*values):
    total = values[0].astype(F32)
    for v in values[1:]:
        total = total + v.astype(F32)
    return total


class Gather:
    def __init__(self, net, shard):
        self.net = net
        self.line = [shard] + [net.swap(shard, 4 * m) for m in (1, 2, 3)]

    def spread(self, line):
        net = self.net
        self.lines = jnp.stack(line)
        self.x = net.swap(self.lines, 1)
        self.y = net.swap(self.lines, 2)
        self.sib = [net.sibling(self.lines)]

    def corner(self, x, y):
        net = self.net
        self.x, self.y = x, y
        self.d01 = net.swap(x[:2], 2)
        self.d23 = net.swap(y[2:], 1)
        self.sib += [net.sibling(x), net.sibling(y)]

    def finish(self, d01, d23):
        net = self.net
        self.d01, self.d23 = d01, d23
        self.sib += [net.sibling(d01), net.sibling(d23)]

    def pieces(self):
        return [self.lines, self.x, self.y, self.d01, self.d23] + self.sib


class Scatter:
    def __init__(self, net, pieces):
        self.net = net
        to_x, to_y, self.x01, self.y23, self.f = pieces
        self.from_x = net.swap(to_x, 1)
        self.from_y = net.swap(to_y, 2)

    def second(self, from_x, from_y):
        net = self.net
        self.x23, self.y01 = from_x[2:], from_y[2:]
        self.rx01 = net.swap(add(self.x01, from_y[:2]).astype(BF16), 1)
        self.ry23 = net.swap(add(self.y23, from_x[:2]).astype(BF16), 2)

    def third(self, rx01, ry23):
        net = self.net
        low = add(self.f[:2], rx01, self.y01)
        high = add(self.f[2:], ry23, self.x23)
        self.low = low
        self.far = net.swap(high.astype(BF16), 8)

    def fourth(self, far):
        net = self.net
        low = self.low + far.astype(F32)
        self.own = low[0]
        self.near = net.swap(low[1].astype(BF16), 4)

    def result(self, near):
        return add(self.own, near)


def shards_16(
    activations,
    segment_ids,
    cotangent,
    querymat,
    keymat,
    valuemat,
    outmat,
    upmatrix,
    downmatrix,
    querybias,
    keybias,
    valuebias,
    outbias,
    upbias,
    downbias,
    firstgain,
    secondgain,
    thirdgain,
    fourthgain,
):
    net = Net(16)
    t, width = activations.shape
    rows = querymat.shape[0]
    hidden = upmatrix.shape[1]
    block = upbias.shape[0]
    half = width // 2
    me, core = net.me, net.core
    device = me * 2 + core
    where = jnp.stack([me, core]).astype(I32)

    dst = jnp.arange(width)
    place = (dst // rows) % 16
    chip = me ^ (place // 4 + 4 * (place % 4))
    src = chip * (2 * rows) + (core ^ (dst // half)) * rows + dst % rows
    order = (jnp.arange(width)[:, None] == src[None, :]).astype(BF16)
    slots = jnp.arange(t)
    segment = jnp.where(segment_ids >= 0, segment_ids, -1 - slots)
    col, row = segment[:, None], segment[None, :]
    valid = (segment_ids >= 0).astype(F32)[:, None]
    spots = positions_of(segment_ids).astype(F32)
    inverse = 10000.0 ** (-jnp.arange(HEAD // 2).astype(F32) * 2.0 / HEAD)
    angles = spots[:, None] * inverse[None, :]
    cosine = jnp.tile(jnp.cos(angles), (1, 4))
    sine = jnp.sin(angles)
    sine = jnp.tile(jnp.concatenate([-sine, sine], axis=1), (1, 2))

    ffn_shard = jnp.concatenate(
        [upmatrix.reshape(rows, 4, width).transpose(1, 0, 2), downmatrix.reshape(4, rows, width)]
    )
    ffn = lax.all_gather(ffn_shard, AXES, axis=0, tiled=False)
    qk = Gather(net, jnp.concatenate([querymat, keymat], axis=1))
    vo_shard = jnp.concatenate([valuemat, outmat], axis=1)
    nine = [querybias, keybias, valuebias, outbias, downbias, firstgain, secondgain, thirdgain, fourthgain]
    small = jnp.concatenate([jnp.pad(v[None], ((0, 0), (0, LANES - rows))) for v in nine] + [upbias[None]])
    buf = small[None]
    buf = jnp.concatenate([buf, net.sibling(buf)])
    for mask in (1, 2, 4, 8):
        buf = jnp.concatenate([buf, net.swap(buf, mask)])
    line, buf, vo_shard = after(qk.line, buf, vo_shard)
    qk.spread(line)
    vo = Gather(net, vo_shard)

    picks = (jnp.arange(32)[:, None] ^ device) == jnp.arange(32)[None, :]
    small_all = dot(picks.astype(BF16), buf.reshape(32, -1)).reshape(32, 10, LANES)
    b_q, b_k, b_v, b_o, b_d, g1, g2, g3, g4 = (
        small_all[:, i, :rows].reshape(1, width) for i in range(9)
    )
    b_up = small_all[:, 9].reshape(1, hidden)
    inputs = activations.astype(F32)
    normed = (inputs * inverse_rms(inputs) * g1).astype(BF16)
    turned = dot(normed, order).astype(BF16)
    x_own, x_sib = turned[:, :half], turned[:, half:]

    x, y, line = after(qk.x, qk.y, vo.line)
    qk.corner(x, y)
    vo.spread(line)
    d01, d23, x_own, x_sib = after(qk.d01, qk.d23, x_own, x_sib)
    qk.finish(d01, d23)
    x_oth = net.sibling(x_sib)
    x, y = after(vo.x, vo.y)
    vo.corner(x, y)
    qk_pieces = qk.pieces()
    qk_rot = project(x_own, x_sib, qk_pieces, 0, 2, jnp.concatenate([b_q, b_k], axis=1), (cosine, sine))
    d01, d23, qk_rot = after(vo.d01, vo.d23, qk_rot)
    vo.finish(d01, d23)
    vo_pieces = vo.pieces()
    v = project(x_own, x_sib, vo_pieces, 0, 1, b_v)
    mixed, lse = attend(qk_rot, v, col, row)
    m_own, m_sib, att, mid, normed_mid, n_own, n_sib = out_project(
        mixed, order, activations, b_o, g2, g3, vo_pieces
    )
    m_oth = net.sibling(m_sib)
    n_oth = net.sibling(n_sib)
    a_own, a_sib, s_own, s_sib = up_project(where, normed_mid, b_up, ffn)
    a_oth = net.sibling(a_sib)
    ffn_down = ffn.reshape(16, 2, 8, rows, width)
    layer_out, dc, down_sums, power = down_project(
        where, a_own, a_sib, b_d, mid, cotangent, valid, g4, ffn_down
    )

    dc_oth = net.sibling(dc)
    de, up_bias_sum = down_back(where, dc, s_own, s_sib, ffn_down)
    de, dc_oth, a_oth = after(de, dc_oth, a_oth)
    de_oth = net.sibling(de)
    slopes = block_slopes(where, a_own, a_oth, dc, dc_oth)
    slopes, de = after(slopes, de)
    down_sum = Scatter(net, slopes)
    dmid, datt, dmix, mid_sums = up_back(
        de, order, mid, att, cotangent, valid, g2, g3, ffn, vo_pieces
    )
    from_x, from_y, datt, dmix, de_oth = after(down_sum.from_x, down_sum.from_y, datt, dmix, de_oth)
    down_sum.second(from_x, from_y)
    datt_oth = net.sibling(datt)
    slopes = row_slopes(n_own, n_oth, [de], [de_oth], 4)
    slopes, rx01, ry23, datt_oth, datt, dmix = after(
        slopes, down_sum.rx01, down_sum.ry23, datt_oth, datt, dmix
    )
    up_sum = Scatter(net, slopes)
    down_sum.third(rx01, ry23)
    steps = width // LANES // 2
    d_a = attend_back(qk_rot, v, dmix, lse, col, row, cosine, sine, 0, steps)
    d_a, dmix, from_x, from_y, far = after(d_a, dmix, up_sum.from_x, up_sum.from_y, down_sum.far)
    up_sum.second(from_x, from_y)
    down_sum.fourth(far)
    *d_a, sums_a = d_a
    oth_a = [net.sibling(d) for d in d_a]
    slopes = row_slopes(m_own, m_oth, [datt], [datt_oth], 1)
    slopes, dmix = after(slopes, dmix)
    d_b = attend_back(qk_rot, v, dmix, lse, col, row, cosine, sine, steps, steps)
    d_b, oth_a, near, rx01, ry23, slopes = after(
        d_b, oth_a, down_sum.near, up_sum.rx01, up_sum.ry23, slopes
    )
    *d_b, sums_b = d_b
    down_total = down_sum.result(near)
    out_sum = Scatter(net, slopes)
    up_sum.third(rx01, ry23)
    oth_b = [net.sibling(d) for d in d_b]
    slopes = row_slopes(x_own, x_oth, d_a, oth_a, 1)
    slopes, oth_b, from_x, from_y, d_a, d_b = after(
        slopes, oth_b, out_sum.from_x, out_sum.from_y, d_a, d_b
    )
    qkv_a = Scatter(net, slopes)
    out_sum.second(from_x, from_y)
    slopes = row_slopes(x_own, x_oth, d_b, oth_b, 1)
    slopes, far, d_a, d_b, rx01, ry23 = after(
        slopes, up_sum.far, d_a, d_b, out_sum.rx01, out_sum.ry23
    )
    up_sum.fourth(far)
    qkv_b = Scatter(net, slopes)
    out_sum.third(rx01, ry23)
    input_gradient, first_sum = in_back(
        d_a, d_b, order, activations, dmid, g1, qk_pieces, vo_pieces
    )
    first_sum, a_x, a_y, near, far = after(
        first_sum, qkv_a.from_x, qkv_a.from_y, up_sum.near, out_sum.far
    )
    up_total = up_sum.result(near)
    qkv_a.second(a_x, a_y)
    out_sum.fourth(far)
    b_x, b_y, first_sum = after(qkv_b.from_x, qkv_b.from_y, first_sum)
    qkv_b.second(b_x, b_y)
    out_total = out_sum.result(out_sum.near)
    qkv_a.third(qkv_a.rx01, qkv_a.ry23)
    qkv_a.fourth(qkv_a.far)
    qkv_b.third(qkv_b.rx01, qkv_b.ry23)
    qkv_b.fourth(qkv_b.far)
    total_a = qkv_a.result(qkv_a.near).reshape(rows, 3, half)
    total_b = qkv_b.result(qkv_b.near).reshape(rows, 3, half)
    qkv_total = [jnp.concatenate([total_a[:, i], total_b[:, i]], axis=1) for i in range(3)]
    qkv_sums = jnp.concatenate([sums_a, sums_b], axis=1)

    sums = jnp.concatenate(
        [
            qkv_sums[0],
            qkv_sums[1],
            qkv_sums[2],
            mid_sums[2],
            down_sums[1],
            first_sum[0],
            mid_sums[1],
            mid_sums[0],
            down_sums[0],
            up_bias_sum[0],
            power[0],
        ]
    )
    sums = net.total(sums.reshape(-1, LANES)).reshape(-1)
    output_power = sums[-1] / (t * 32)
    own = lax.dynamic_slice_in_dim(sums[: 9 * width].reshape(9, width), device * rows, rows, 1)
    own_up = lax.dynamic_slice_in_dim(sums[9 * width : 9 * width + hidden], device * block, block, 0)
    return (
        layer_out,
        input_gradient,
        *qkv_total,
        out_total,
        up_total,
        down_total,
        own[0],
        own[1],
        own[2],
        own[3],
        own_up,
        own[4],
        own[5],
        own[6],
        own[7],
        own[8],
        output_power,
    )


def shards(*args):
    rows, length = args[3].shape[0], args[0].shape[0]
    if lax.axis_size("wide") == 16 and rows == 32 and length == 512:
        return shards_16(*args)
    return shards_any(*args)


def solution(mesh):
    matrix = P(AXES, None)
    vector = P(AXES)
    return jax.shard_map(
        shards,
        mesh=mesh,
        in_specs=(matrix, vector, matrix) + (matrix,) * 6 + (vector,) * 10,
        out_specs=(matrix,) * 8 + (vector,) * 10 + (P(),),
        check_vma=False,
    )
```

```python
import jax
import jax.numpy as jnp
import functools

from jax import lax
from jax.experimental import pallas as pl
from jax.experimental.pallas import tpu as pltpu
from jax.sharding import PartitionSpec as P

HEAD = 64
AXES = ("wide", "narrow")


def rms_norm(values, gain):
    return values * lax.rsqrt(jnp.mean(values * values, axis=-1, keepdims=True) + 1e-06) * gain


def rotate(values, cosine, sine):
    midpoint = values.shape[-1] // 2
    first_half = values[..., :midpoint]
    second_half = values[..., midpoint:]
    return jnp.concatenate(
        [first_half * cosine - second_half * sine, first_half * sine + second_half * cosine],
        axis=-1,
    )


def positions_of(segment):
    places = jnp.arange(segment.shape[0])
    matching = segment[:, None] == segment[None, :]
    earlier = places[None, :] < places[:, None]
    return jnp.sum(jnp.logical_and(matching, earlier).astype(jnp.int32), axis=1)


def angle_tables(segment):
    places = positions_of(segment).astype(jnp.float32)
    midpoint = HEAD // 2
    inverse = 10000.0 ** (-jnp.arange(midpoint).astype(jnp.float32) * 2.0 / HEAD)
    angles = places[:, None] * inverse[None, :]
    return (jnp.cos(angles)[:, None, :], jnp.sin(angles)[:, None, :])


def key_mask(segment):
    places = jnp.arange(segment.shape[0])
    matching = segment[:, None] == segment[None, :]
    allowed = matching & (segment[None, :] >= 0) & (places[None, :] <= places[:, None])
    return allowed | (places[None, :] == places[:, None])


def contract_rows(left, right):
    return lax.dot_general(
        left, right, (((0,), (0,)), ((), ())), preferred_element_type=jnp.float32
    )


def times_transpose(left, right):
    return lax.dot_general(
        left, right, (((1,), (1,)), ((), ())), preferred_element_type=jnp.float32
    )


def product(left, right):
    return jnp.dot(left, right, preferred_element_type=jnp.float32)


def column_sums(values):
    return jnp.sum(values.astype(jnp.float32), axis=0)


def masked_scores(query_rot, key_rot, allowed):
    scores = (
        jnp.einsum("qhd,khd->hqk", query_rot, key_rot, preferred_element_type=jnp.float32) * 0.125
    )
    return jnp.where(allowed[None], scores, -1e30)


class Net:
    def __init__(self, wide):
        self.wide = wide
        self.me = lax.axis_index("wide")
        self.core = lax.axis_index("narrow")
        outer = []
        mask = wide // 2
        while mask > 2:
            outer.append(mask)
            mask //= 2
        self.outer = outer

    def swap(self, value, mask):
        pairs = [(d, d ^ mask) for d in range(self.wide)]
        return lax.ppermute(value, "wide", pairs)

    def sibling(self, value):
        return lax.ppermute(value, "narrow", [(0, 1), (1, 0)])

    def bit(self, mask):
        return (self.me & mask) != 0

    def grow(self, value, mask, axis):
        other = self.swap(value, mask)
        bit = self.bit(mask)
        low = jnp.where(bit, other, value)
        high = jnp.where(bit, value, other)
        return jnp.stack([low, high], axis=axis)

    def shrink(self, value, mask, axis):
        bit = self.bit(mask).astype(jnp.int32)
        mine = lax.dynamic_index_in_dim(value, bit, axis, keepdims=False)
        theirs = lax.dynamic_index_in_dim(value, 1 - bit, axis, keepdims=False)
        other = self.swap(theirs, mask)
        return (mine.astype(jnp.float32) + other.astype(jnp.float32)).astype(jnp.bfloat16)

    def gather(self, first, second):
        r, c = first.shape
        both = jnp.stack([first, second])[None]
        for mask in self.outer:
            both = self.grow(both, mask, 1).reshape(-1, 2, r, c)
        outer = both.shape[0]
        a = self.grow(both[:, 0], 1, 1)
        a = self.grow(a, 2, 1)
        b = self.grow(both[:, 1], 2, 1)
        b = self.grow(b, 1, 2)
        return jnp.stack([a, b], axis=3).reshape(outer * 4 * 2 * r, c)

    def scatter(self, full):
        rows, c = full.shape
        r = rows // (self.wide * 2)
        outer = self.wide // 4
        parts = full.reshape(outer, 2, 2, 2, r, c)
        a, b = parts[:, :, :, 0], parts[:, :, :, 1]
        a = self.shrink(self.shrink(a, 2, 1), 1, 1)
        b = self.shrink(self.shrink(b, 1, 2), 2, 1)
        both = jnp.stack([a, b], axis=1)
        for mask in reversed(self.outer):
            count = both.shape[0] // 2
            both = self.shrink(both.reshape(count, 2, 2, r, c), mask, 1)
        return both[0, 0], both[0, 1]

    def gather_small(self, value):
        other = self.sibling(value)
        core = self.core == 1
        buf = jnp.stack([jnp.where(core, other, value), jnp.where(core, value, other)])[None]
        for mask in [1, 2] + self.outer[::-1]:
            buf = self.grow(buf, mask, 0).reshape(1, -1, *value.shape)
        return buf[0]

    def total(self, value):
        value = value + self.sibling(value)
        for mask in [1, 2] + self.outer[::-1]:
            value = value + self.swap(value, mask)
        return value

    def pick(self, value, axis):
        mine = lax.dynamic_index_in_dim(value, self.core, axis, keepdims=False)
        theirs = lax.dynamic_index_in_dim(value, 1 - self.core, axis, keepdims=False)
        return mine, theirs

    def halves(self, mine, theirs):
        core = self.core == 1
        return jnp.where(core, theirs, mine), jnp.where(core, mine, theirs)

    def columns_in(self, shard):
        mine, theirs = self.pick(shard, 1)
        return self.halves(mine, self.sibling(theirs))

    def columns_out(self, first, second):
        mine, theirs = self.pick(jnp.stack([first, second]), 0)
        other = self.sibling(theirs)
        left, right = self.halves(mine, other)
        return jnp.stack([left, right], axis=1)


def shards_any(
    activations,
    segment_ids,
    cotangent,
    querymat,
    keymat,
    valuemat,
    outmat,
    upmatrix,
    downmatrix,
    querybias,
    keybias,
    valuebias,
    outbias,
    upbias,
    downbias,
    firstgain,
    secondgain,
    thirdgain,
    fourthgain,
):
    wide = lax.axis_size("wide")
    net = Net(wide)
    core = net.core
    length, width = activations.shape
    rows = querymat.shape[0]
    hidden = upmatrix.shape[1]
    block = hidden // (2 * wide)
    half = width // 2
    heads = width // HEAD
    f32 = jnp.float32
    bf16 = jnp.bfloat16

    nine = [querybias, keybias, valuebias, outbias, downbias, firstgain, secondgain, thirdgain, fourthgain]
    small = jnp.concatenate([jnp.concatenate(nine), upbias])
    qkv_shard = jnp.concatenate(
        [m.reshape(rows, 2, half) for m in (querymat, keymat, valuemat)], axis=2
    )
    up_shard = upmatrix.reshape(rows, wide, 2, block).transpose(0, 2, 1, 3).reshape(rows, 2, hidden // 2)
    out_shard = outmat.reshape(rows, 2, half)
    small_all = net.gather_small(small)
    qkv_mine = net.gather(*net.columns_in(qkv_shard))
    out_mine = net.gather(*net.columns_in(out_shard))
    up_mine = net.gather(*net.columns_in(up_shard))
    down_rows = downmatrix.shape[0]
    down_mine = net.gather(downmatrix[: down_rows // 2], downmatrix[down_rows // 2 :])
    qkv_theirs, out_theirs, up_theirs, down_theirs = map(
        net.sibling, (qkv_mine, out_mine, up_mine, down_mine)
    )

    vectors = small_all[:, : 9 * rows].reshape(-1, 9, rows).transpose(1, 0, 2).reshape(9, width)
    vectors = vectors.astype(f32)
    bias_query, bias_key, bias_value, bias_output, bias_down = (vectors[i] for i in range(5))
    gain_first, gain_second, gain_third, gain_fourth = (vectors[i] for i in range(5, 9))
    bias_up_pair = small_all[:, 9 * rows :].reshape(wide, 2, block).astype(f32)
    bias_up_mine, bias_up_theirs = (v.reshape(-1) for v in net.pick(bias_up_pair, 1))

    def natural(mine, theirs):
        return jnp.where(
            core == 1,
            jnp.concatenate([theirs, mine], axis=-1),
            jnp.concatenate([mine, theirs], axis=-1),
        )

    inputs = activations.astype(f32)
    cosine, sine = angle_tables(segment_ids)
    allowed = key_mask(segment_ids)
    valid_row = (segment_ids >= 0).astype(f32)
    normed_in, pull_first = jax.vjp(rms_norm, inputs, gain_first)
    normed_low = normed_in.astype(bf16)
    normed_low_theirs = net.sibling(normed_low)
    qkv_m = product(normed_low, qkv_mine)
    qkv_t = product(normed_low, qkv_theirs)
    queries, keys_pre, values_pre = (
        natural(qkv_m[:, i * half : (i + 1) * half], qkv_t[:, i * half : (i + 1) * half]) + b
        for i, b in enumerate((bias_query, bias_key, bias_value))
    )
    query_rot = rotate(queries.reshape(length, heads, HEAD), cosine, sine).astype(bf16)
    key_rot = rotate(keys_pre.reshape(length, heads, HEAD), cosine, sine).astype(bf16)
    value_low = values_pre.reshape(length, heads, HEAD).astype(bf16)
    scores = masked_scores(query_rot, key_rot, allowed)
    peak = jnp.max(scores, axis=-1, keepdims=True)
    exponent = jnp.exp(scores - peak)
    totals = jnp.sum(exponent, axis=-1, keepdims=True)
    logsum = peak + jnp.log(totals)
    probs = exponent / totals
    mixed = jnp.einsum(
        "hqk,khd->qhd", probs.astype(bf16), value_low, preferred_element_type=f32
    )
    mixed_low = mixed.reshape(length, width).astype(bf16)
    mixed_low_theirs = net.sibling(mixed_low)
    attended = natural(product(mixed_low, out_mine), product(mixed_low, out_theirs)) + bias_output
    normed_att, pull_second = jax.vjp(rms_norm, attended, gain_second)
    middle = inputs + normed_att
    normed_mid, pull_third = jax.vjp(rms_norm, middle, gain_third)
    normed_mid_low = normed_mid.astype(bf16)
    normed_mid_low_theirs = net.sibling(normed_mid_low)
    act_m_f, pull_gelu_m = jax.vjp(jax.nn.gelu, product(normed_mid_low, up_mine) + bias_up_mine)
    act_t_f, pull_gelu_t = jax.vjp(jax.nn.gelu, product(normed_mid_low, up_theirs) + bias_up_theirs)
    act_m = act_m_f.astype(bf16)
    act_t = act_t_f.astype(bf16)
    act_other = net.sibling(act_t)
    contracted = product(act_m, down_mine) + product(act_t, down_theirs) + bias_down
    local_power = jnp.sum(valid_row * jnp.mean(contracted * contracted, axis=-1))
    normed_out, pull_fourth = jax.vjp(rms_norm, contracted, gain_fourth)
    layer_out = (middle + normed_out).astype(bf16)

    seed = cotangent.astype(f32) * valid_row[:, None]
    d_contracted_f, fourth_slope = pull_fourth(seed)
    d_contracted = d_contracted_f.astype(bf16)
    d_contracted_theirs = net.sibling(d_contracted)
    down_bias_slope = column_sums(d_contracted)
    d_exp_m = pull_gelu_m(times_transpose(d_contracted, down_mine))[0].astype(bf16)
    d_exp_t = pull_gelu_t(times_transpose(d_contracted, down_theirs))[0].astype(bf16)
    d_exp_other = net.sibling(d_exp_t)

    def both_rows(a, b):
        return jnp.concatenate([a, b], axis=0)

    down_slope = contract_rows(
        both_rows(act_m, act_other), both_rows(d_contracted, d_contracted_theirs)
    ).astype(bf16)
    down_sum = net.scatter(down_slope)
    up_slope = contract_rows(
        both_rows(normed_mid_low, normed_mid_low_theirs), both_rows(d_exp_m, d_exp_other)
    ).astype(bf16)
    up_sum = net.scatter(up_slope)
    up_bias_m, up_bias_t = column_sums(d_exp_m), column_sums(d_exp_t)
    d_normed_mid = times_transpose(d_exp_m, up_mine) + times_transpose(d_exp_t, up_theirs)
    d_middle_part, third_slope = pull_third(d_normed_mid)
    d_middle = seed + d_middle_part
    d_attended_f, second_slope = pull_second(d_middle)
    d_attended = d_attended_f.astype(bf16)
    output_bias_slope = column_sums(d_attended)
    d_att_m, d_att_t = net.pick(d_attended.reshape(length, 2, half), 1)
    d_att_other = net.sibling(d_att_t)
    out_slope = contract_rows(
        both_rows(mixed_low, mixed_low_theirs), both_rows(d_att_m, d_att_other)
    ).astype(bf16)
    out_sum = net.scatter(out_slope)
    d_mixed = (
        (times_transpose(d_att_m, out_mine) + times_transpose(d_att_t, out_theirs))
        .astype(bf16)
        .reshape(length, heads, HEAD)
    )
    probs_again = jnp.exp(masked_scores(query_rot, key_rot, allowed) - logsum)
    d_values = jnp.einsum(
        "hqk,qhd->khd", probs_again.astype(bf16), d_mixed, preferred_element_type=f32
    )
    d_probs = jnp.einsum("qhd,khd->hqk", d_mixed, value_low, preferred_element_type=f32)
    row_terms = jnp.sum(probs_again * d_probs, axis=-1, keepdims=True)
    d_scores = (probs_again * (d_probs - row_terms)).astype(bf16)
    d_query_rot = (
        jnp.einsum("hqk,khd->qhd", d_scores, key_rot, preferred_element_type=f32) * 0.125
    )
    d_key_rot = (
        jnp.einsum("hqk,qhd->khd", d_scores, query_rot, preferred_element_type=f32) * 0.125
    )
    d_queries = rotate(d_query_rot, cosine, -sine).reshape(length, width).astype(bf16)
    d_keys = rotate(d_key_rot, cosine, -sine).reshape(length, width).astype(bf16)
    d_values_low = d_values.reshape(length, width).astype(bf16)
    pairs = [net.pick(v.reshape(length, 2, half), 1) for v in (d_queries, d_keys, d_values_low)]
    d_qkv_m = jnp.concatenate([p[0] for p in pairs], axis=1)
    d_qkv_t = jnp.concatenate([p[1] for p in pairs], axis=1)
    d_qkv_other = net.sibling(d_qkv_t)
    qkv_slope = contract_rows(
        both_rows(normed_low, normed_low_theirs), both_rows(d_qkv_m, d_qkv_other)
    ).astype(bf16)
    qkv_sum = net.scatter(qkv_slope)
    d_normed = times_transpose(d_qkv_m, qkv_mine) + times_transpose(d_qkv_t, qkv_theirs)
    d_inputs_part, first_slope = pull_first(d_normed)
    input_gradient = d_middle + d_inputs_part

    up_bias_low = jnp.where(core == 1, up_bias_t, up_bias_m).reshape(wide, 1, block)
    up_bias_high = jnp.where(core == 1, up_bias_m, up_bias_t).reshape(wide, 1, block)
    up_bias_slope = jnp.concatenate([up_bias_low, up_bias_high], axis=1).reshape(-1)
    small_slopes = jnp.concatenate(
        [
            column_sums(d_queries),
            column_sums(d_keys),
            column_sums(d_values_low),
            output_bias_slope,
            down_bias_slope,
            first_slope,
            second_slope,
            third_slope,
            fourth_slope,
            up_bias_slope,
            jnp.full((128,), local_power, f32),
        ]
    )
    sums = net.total(small_slopes)
    output_power = sums[-1] / (length * wide * 2)
    device = net.me * 2 + core
    own = lax.dynamic_slice_in_dim(sums[: 9 * width].reshape(9, width), device * rows, rows, 1)
    own_up = lax.dynamic_slice_in_dim(sums[9 * width : 9 * width + hidden], device * 2 * block // 2, block, 0)

    qkv_grad = net.columns_out(*qkv_sum).astype(f32)
    out_grad = net.columns_out(*out_sum).astype(f32).reshape(rows, width)
    up_grad = net.columns_out(*up_sum).astype(f32)
    up_grad = up_grad.reshape(rows, 2, wide, block).transpose(0, 2, 1, 3).reshape(rows, hidden)
    down_grad = jnp.concatenate(down_sum, axis=0).astype(f32)
    q_grad, k_grad, v_grad = (
        qkv_grad[:, :, i * half : (i + 1) * half].reshape(rows, width) for i in range(3)
    )
    return (
        layer_out,
        input_gradient,
        q_grad,
        k_grad,
        v_grad,
        out_grad,
        up_grad,
        down_grad,
        own[0],
        own[1],
        own[2],
        own[3],
        own_up,
        own[4],
        own[5],
        own[6],
        own[7],
        own[8],
        output_power,
    )


F32 = jnp.float32
BF16 = jnp.bfloat16
I32 = jnp.int32
EPS = 1e-06
VMEM_LIMIT = 60 * 1024 * 1024
LANES = 128
GELU_A = 0.7978845608028654
GELU_B = 0.044715
TILE = 128
UP_TILE = 1024
DOWN_CHIPS = 4


def whole_spec():
    return pl.BlockSpec(memory_space=pltpu.VMEM)


def hbm_spec():
    return pl.BlockSpec(memory_space=pl.ANY)


def smem_spec():
    return pl.BlockSpec(memory_space=pltpu.SMEM)


def params():
    return pltpu.CompilerParams(vmem_limit_bytes=VMEM_LIMIT)


def shape(dims, dtype):
    return jax.ShapeDtypeStruct(dims, dtype)


def cost(flops, bytes_accessed):
    return pl.CostEstimate(flops=flops, bytes_accessed=bytes_accessed, transcendentals=0)


def dot(a, b):
    return lax.dot_general(a, b, (((1,), (0,)), ((), ())), preferred_element_type=F32)


def dot_t(a, b):
    return lax.dot_general(a, b, (((1,), (1,)), ((), ())), preferred_element_type=F32)


def t_dot(a, b):
    return lax.dot_general(a, b, (((0,), (0,)), ((), ())), preferred_element_type=F32)


def pair_mask(place):
    return place // 4 + 4 * (place % 4)


def assemble(where, pieces, target, sems, cols):
    copies = []
    for e in range(2):
        place = 0
        for piece in pieces[e * 5 : e * 5 + 5]:
            for j in range(piece.shape[0]):
                chip = where[0] ^ pair_mask(place)
                source = piece.at[j, :, pl.ds(*cols)]
                dest = target.at[chip, where[1] ^ e]
                copies.append(pltpu.make_async_copy(source, dest, sems.at[len(copies)]))
                place += 1
    for copy in copies:
        copy.start()
    return copies


def wait_all(copies):
    for copy in copies:
        copy.wait()


def fetch(sources, targets, sems, base=0):
    copies = [
        pltpu.make_async_copy(a, b, sems.at[base + i]) for i, (a, b) in enumerate(zip(sources, targets))
    ]
    for copy in copies:
        copy.start()
    return copies


def matrix(buf):
    return buf[...].reshape(-1, buf.shape[-1])


def inverse_rms(v):
    return lax.rsqrt(jnp.mean(v * v, axis=-1, keepdims=True) + EPS)


def rms_back(v, r, gain, e):
    ge = gain * e
    return r * ge - v * (r * r * r) * jnp.mean(v * ge, axis=-1, keepdims=True)


def row_sum(v):
    return jnp.sum(v, axis=0, keepdims=True)


def turn(v, cosine, sine):
    lane = lax.broadcasted_iota(I32, v.shape, 1)
    swapped = jnp.where((lane & 63) < 32, pltpu.roll(v, 96, 1), pltpu.roll(v, 32, 1))
    return v * cosine + swapped * sine


def project_kernel(parts, where, x, bias, *refs):
    pieces = refs[:10]
    tables = refs[10:-3]
    out, wbuf, sems = refs[-3:]
    width = x.shape[1]
    copies = [
        assemble(where, pieces, wbuf.at[i], sems.at[i], (i * width, width)) for i in range(parts)
    ]
    for i in range(parts):
        wait_all(copies[i])
        for c in range(0, width, 512):
            y = dot(x[...], wbuf[i, :, :, :, c : c + 512].reshape(width, 512))
            y = y + bias[:, i * width + c : i * width + c + 512]
            at = i * width + c
            if tables:
                cosine, sine = tables[0][...], tables[1][...]
                for b in range(0, 512, LANES):
                    z = turn(y[:, b : b + LANES], cosine, sine)
                    z = z * 0.125 if i == 0 else z
                    out[:, at + b : at + b + LANES] = z.astype(BF16)
            else:
                out[:, at : at + 512] = y.astype(BF16)


def project(where, x, pieces, parts, bias, tables=()):
    t, width = x.shape
    r = pieces[0].shape[1]
    return pl.pallas_call(
        functools.partial(project_kernel, parts),
        in_specs=[smem_spec(), whole_spec(), whole_spec()]
        + [hbm_spec()] * 10
        + [whole_spec()] * len(tables),
        out_specs=whole_spec(),
        out_shape=shape((t, parts * width), BF16),
        scratch_shapes=[
            pltpu.VMEM((parts, 16, 2, r, width), BF16),
            pltpu.SemaphoreType.DMA((parts, 32)),
        ],
        compiler_params=params(),
        cost_estimate=cost(2 * t * width * parts * width, 2 * parts * width * width),
        name="project",
    )(where, x, bias, *pieces, *tables)


def open_mask(col_ref, row_ref, open_ref):
    t = open_ref.shape[0]

    @pl.when(pl.program_id(0) == 0)
    def _():
        rows = lax.broadcasted_iota(I32, (t, t), 0)
        cols = lax.broadcasted_iota(I32, (t, t), 1)
        ok = (col_ref[...] == row_ref[...]) & (cols <= rows)
        open_ref[...] = jnp.where(ok, 0.0, -1e30)


def one_head(v, h):
    lane = lax.broadcasted_iota(I32, v.shape, 1)
    return jnp.where((lane < HEAD) == (h == 0), v, jnp.zeros_like(v))


def attend_kernel(q_ref, k_ref, v_ref, col_ref, row_ref, out_ref, lse_ref, open_ref):
    t = q_ref.shape[0]
    tile = TILE
    open_mask(col_ref, row_ref, open_ref)
    left = lax.broadcasted_iota(I32, (tile, LANES), 1) < HEAD
    spans = [(slice(i * tile, (i + 1) * tile), (i + 1) * tile) for i in range(t // tile)]
    pairs = [(rows, seen, h) for rows, seen in spans for h in range(2)]
    scores = [
        dot_t(one_head(q_ref[rows, :], h), k_ref[:seen, :]) + open_ref[rows, :seen]
        for rows, seen, h in pairs
    ]
    peaks = [jnp.max(s, axis=-1, keepdims=True) for s in scores]
    powers = [jnp.exp(s - peak) for s, peak in zip(scores, peaks)]
    totals = [jnp.sum(e, axis=-1, keepdims=True) for e in powers]
    outs = [
        dot(e.astype(BF16), v_ref[:seen, :]) / total
        for e, total, (rows, seen, h) in zip(powers, totals, pairs)
    ]
    sums = [peak + jnp.log(total) for peak, total in zip(peaks, totals)]
    for i, (rows, seen) in enumerate(spans):
        out_ref[rows, :] = jnp.where(left, outs[2 * i], outs[2 * i + 1]).astype(BF16)
        lse_ref[rows, :] = jnp.where(left, sums[2 * i], sums[2 * i + 1])


def attend(qk, v, col, row):
    t, width = v.shape
    steps = width // LANES
    block = lambda f: pl.BlockSpec((t, LANES), f)
    return pl.pallas_call(
        attend_kernel,
        grid=(steps,),
        in_specs=[
            block(lambda i: (0, i)),
            block(lambda i: (0, i + steps)),
            block(lambda i: (0, i)),
            pl.BlockSpec((t, 1), lambda i: (0, 0)),
            pl.BlockSpec((1, t), lambda i: (0, 0)),
        ],
        out_specs=[block(lambda i: (0, i))] * 2,
        out_shape=[shape((t, width), BF16), shape((t, width), F32)],
        scratch_shapes=[pltpu.VMEM((t, t), F32)],
        compiler_params=params(),
        cost_estimate=cost(4 * t * t * width, 10 * t * width),
        name="attend",
    )(qk, qk, v, col, row)


def attend_back_kernel(
    q_ref, k_ref, v_ref, dm_ref, lse_ref, col_ref, row_ref, cos_ref, sin_ref,
    d_ref, sum_ref, open_ref,
):
    t = q_ref.shape[0]
    tile = TILE
    open_mask(col_ref, row_ref, open_ref)
    left = lax.broadcasted_iota(I32, (tile, LANES), 1) < HEAD
    spans = [(slice(i * tile, (i + 1) * tile), (i + 1) * tile) for i in range(t // tile)]
    pairs = [(rows, seen, h) for rows, seen in spans for h in range(2)]
    scores = [
        dot_t(one_head(q_ref[rows, :], h), k_ref[:seen, :]) + open_ref[rows, :seen]
        for rows, seen, h in pairs
    ]
    d_probs = [dot_t(one_head(dm_ref[rows, :], h), v_ref[:seen, :]) for rows, seen, h in pairs]
    probs = [
        jnp.exp(s - lse_ref[rows, h * HEAD : h * HEAD + 1])
        for s, (rows, seen, h) in zip(scores, pairs)
    ]
    deltas = [jnp.sum(p * dp, axis=-1, keepdims=True) for p, dp in zip(probs, d_probs)]
    d_scores = [(p * (dp - d)).astype(BF16) for p, dp, d in zip(probs, d_probs, deltas)]
    probs = [p.astype(BF16) for p in probs]
    dq = [dot(ds, k_ref[:seen, :]) for ds, (rows, seen, h) in zip(d_scores, pairs)]
    total_q = jnp.zeros((1, LANES), F32)
    for i, (rows, seen) in enumerate(spans):
        v = jnp.where(left, dq[2 * i], dq[2 * i + 1]) * 0.125
        v = turn(v, cos_ref[rows, :], -sin_ref[rows, :]).astype(BF16)
        d_ref[0, rows, :] = v
        total_q += row_sum(v.astype(F32))
    sum_ref[0:1, :] = total_q
    for at, lhs, rhs in ((1, d_scores, q_ref), (2, probs, dm_ref)):
        total = jnp.zeros((1, LANES), F32)
        parts = [t_dot(a, rhs[rows, :]) for a, (rows, seen, h) in zip(lhs, pairs)]
        for i, (keys, _) in enumerate(spans):
            heads = [
                sum(parts[2 * j + h][keys] for j in range(i, len(spans))) for h in range(2)
            ]
            v = jnp.where(left, heads[0], heads[1])
            if at == 1:
                v = turn(v, cos_ref[keys, :], -sin_ref[keys, :])
            v = v.astype(BF16)
            d_ref[at, keys, :] = v
            total += row_sum(v.astype(F32))
        sum_ref[at : at + 1, :] = total


def attend_back(qk, v, dm, lse, col, row, cosine, sine, first, steps):
    t, width = v.shape
    key = width // LANES
    part = steps * LANES
    block = lambda f: pl.BlockSpec((t, LANES), f)
    fixed = lambda a: pl.BlockSpec(a.shape, lambda i: (0, 0))
    here = block(lambda i: (0, i))
    read = block(lambda i: (0, i + first))
    return pl.pallas_call(
        attend_back_kernel,
        grid=(steps,),
        in_specs=[read, block(lambda i: (0, i + first + key)), read, read, read]
        + [fixed(a) for a in (col, row, cosine, sine)],
        out_specs=[
            pl.BlockSpec((3, t, LANES), lambda i: (0, 0, i)),
            pl.BlockSpec((8, LANES), lambda i: (0, i)),
        ],
        out_shape=[shape((3, t, part), BF16), shape((8, part), F32)],
        scratch_shapes=[pltpu.VMEM((t, t), F32)],
        compiler_params=params(),
        cost_estimate=cost(10 * t * t * part, 18 * t * part),
        name="attend_back",
    )(qk, qk, v, dm, lse, col, row, cosine, sine)


def out_kernel(where, mixed, order, x, bias, g2, g3, *refs):
    pieces = refs[:10]
    m_own, m_sib, att_ref, mid_ref, n_ref, n_own, n_sib, wbuf, sems = refs[10:]
    t, width = mixed.shape
    half = width // 2
    copies = assemble(where, pieces, wbuf, sems, (width, width))
    turned = dot_t(order[...], mixed[...]).astype(BF16)
    m_own[...] = turned[:half]
    m_sib[...] = turned[half:]
    wait_all(copies)
    w = matrix(wbuf)
    tile = 256
    for i in range(t // tile):
        rows = slice(i * tile, (i + 1) * tile)
        att = dot(mixed[rows, :], w) + bias[...]
        att_ref[rows, :] = att
        mid = x[rows, :].astype(F32) + att * inverse_rms(att) * g2[...]
        mid_ref[rows, :] = mid
        n_ref[rows, :] = (mid * inverse_rms(mid) * g3[...]).astype(BF16)
    turned = dot_t(order[...], n_ref[...]).astype(BF16)
    n_own[...] = turned[:half]
    n_sib[...] = turned[half:]


def out_project(where, mixed, order, x, bias, g2, g3, pieces):
    t, width = mixed.shape
    half = width // 2
    r = pieces[0].shape[1]
    halves = [shape((half, t), BF16)] * 2
    return pl.pallas_call(
        out_kernel,
        in_specs=[smem_spec()] + [whole_spec()] * 6 + [hbm_spec()] * 10,
        out_specs=[whole_spec()] * 7,
        out_shape=halves + [shape((t, width), F32)] * 2 + [shape((t, width), BF16)] + halves,
        scratch_shapes=[pltpu.VMEM((16, 2, r, width), BF16), pltpu.SemaphoreType.DMA((32,))],
        compiler_params=params(),
        cost_estimate=cost(6 * t * width * width, 16 * t * width),
        name="out_project",
    )(where, mixed, order, x, bias, g2, g3, *pieces)


def up_kernel(where, x, bias, w_ref, a_own, a_sib, slope_ref):
    first = where[1] == 0
    width = x.shape[1]
    for j in range(w_ref.shape[3] // 256):
        cols = slice(j * 256, (j + 1) * 256)
        y = dot(x[...], w_ref[:, 0, :, cols].reshape(width, 256)) + bias[:, cols]
        yy = y * y
        h = 0.5 * jnp.tanh(y * (GELU_A + (GELU_A * GELU_B) * yy)) + 0.5
        act = y * h
        slope = h + act * (1.0 - h) * (2 * GELU_A + (6 * GELU_A * GELU_B) * yy)
        act = act.astype(BF16)
        slope_ref[:, cols] = slope.astype(BF16)
        dst = slice(j * 128, (j + 1) * 128)
        a0, a1 = act[:, :128], act[:, 128:]
        a_own[:, dst] = jnp.where(first, a0, a1)
        a_sib[:, dst] = jnp.where(first, a1, a0)


def up_project(where, x, bias, ffn):
    t, width = x.shape
    hidden = bias.shape[1]
    tn = UP_TILE
    per = ffn.shape[3] // tn
    return pl.pallas_call(
        up_kernel,
        grid=(hidden // tn,),
        in_specs=[
            smem_spec(),
            pl.BlockSpec((t, width), lambda i: (0, 0)),
            pl.BlockSpec((1, tn), lambda i: (0, i)),
            pl.BlockSpec((ffn.shape[0], 1, ffn.shape[2], tn), lambda i: (0, i // per, 0, i % per)),
        ],
        out_specs=[pl.BlockSpec((t, tn // 2), lambda i: (0, i))] * 2
        + [pl.BlockSpec((t, tn), lambda i: (0, i))],
        out_shape=[shape((t, hidden // 2), BF16)] * 2 + [shape((t, hidden), BF16)],
        compiler_params=params(),
        cost_estimate=cost(2 * t * width * hidden, 2 * width * hidden + 4 * t * hidden),
        name="up_project",
    )(where, x, bias, ffn)


def block_at(ref, where, place):
    chip = where[0] ^ pair_mask(place)
    return ref.at[:, pl.ds(pl.multiple_of(chip * LANES, LANES), LANES)]


def down_kernel(
    where, a_own, a_sib, w_own, w_sib, bias, valid, g4, mid_hbm, cot_hbm,
    out_ref, dc_ref, sums_ref, power_ref, acc, mid, cot, sems,
):
    step = pl.program_id(0)
    t, width = acc.shape
    copies = [
        pltpu.make_async_copy(mid_hbm, mid, sems.at[0]),
        pltpu.make_async_copy(cot_hbm, cot, sems.at[1]),
    ]
    w = jnp.concatenate([w_own[...].reshape(-1, width), w_sib[...].reshape(-1, width)], axis=0)
    y = dot(jnp.concatenate([a_own[...], a_sib[...]], axis=1), w)

    @pl.when(step == 0)
    def _():
        for copy in copies:
            copy.start()
        acc[...] = y + bias[...]

    @pl.when(step > 0)
    def _():
        acc[...] += y

    @pl.when(step == pl.num_programs(0) - 1)
    def _():
        wait_all(copies)
        tile = 128
        power = jnp.zeros((1, 1), F32)
        gain_sum = jnp.zeros((1, width), F32)
        bias_sum = jnp.zeros((1, width), F32)
        gain = g4[...]
        for i in range(t // tile):
            rows = slice(i * tile, (i + 1) * tile)
            v = acc[rows, :]
            ok = valid[rows, :]
            mean = jnp.mean(v * v, axis=-1, keepdims=True)
            power += row_sum(mean * ok)
            r = lax.rsqrt(mean + EPS)
            vr = v * r
            out_ref[rows, :] = (mid[rows, :] + vr * gain).astype(BF16)
            seed = cot[rows, :].astype(F32) * ok
            gain_sum += row_sum(vr * seed)
            dc = rms_back(v, r, gain, seed).astype(BF16)
            dc_ref[rows, :] = dc
            bias_sum += row_sum(dc.astype(F32))
        sums_ref[0:1, :] = gain_sum
        sums_ref[1:2, :] = bias_sum
        power_ref[...] = jnp.broadcast_to(power, power_ref.shape)


def down_project(where, a_own, a_sib, bias, mid, cot, valid, g4, ffn):
    t, width = mid.shape
    hidden = 2 * a_own.shape[1]
    r = ffn.shape[3]
    fixed = lambda a: pl.BlockSpec(a.shape, lambda i, w: (0, 0))
    weights = [
        pl.BlockSpec((4, 1, 4, r, width), lambda i, w, e=e: (i, w[1] ^ e, 1, 0, 0)) for e in range(2)
    ]
    out = pl.BlockSpec((t, width), lambda i, w: (0, 0))
    return pl.pallas_call(
        down_kernel,
        grid_spec=pltpu.PrefetchScalarGridSpec(
            num_scalar_prefetch=1,
            grid=(4,),
            in_specs=[pl.BlockSpec((t, 512), lambda i, w: (0, i))] * 2
            + weights
            + [fixed(bias), fixed(valid), fixed(g4), hbm_spec(), hbm_spec()],
            out_specs=[out, out]
            + [pl.BlockSpec((8, width), lambda i, w: (0, 0)), pl.BlockSpec((1, LANES), lambda i, w: (0, 0))],
            scratch_shapes=[
                pltpu.VMEM((t, width), F32),
                pltpu.VMEM((t, width), F32),
                pltpu.VMEM((t, width), BF16),
                pltpu.SemaphoreType.DMA((2,)),
            ],
        ),
        out_shape=[shape((t, width), BF16)] * 2 + [shape((8, width), F32), shape((1, LANES), F32)],
        compiler_params=params(),
        cost_estimate=cost(2 * t * hidden * width, 2 * hidden * width + 10 * t * width),
        name="down_project",
    )(where, a_own, a_sib, ffn, ffn, bias, valid, g4, mid, cot)


def down_back_kernel(dc, slope, w_ref, de_ref, sums_ref):
    width = dc.shape[1]
    for j in range(w_ref.shape[0]):
        cols = slice(j * 256, (j + 1) * 256)
        y = dot_t(dc[...], w_ref[j].reshape(256, width))
        d = (y * slope[:, cols].astype(F32)).astype(BF16)
        de_ref[:, cols] = d
        sums_ref[:, cols] = row_sum(d.astype(F32))


def down_back(dc, slope, ffn):
    t, width = dc.shape
    hidden = slope.shape[1]
    r = ffn.shape[3]
    chips = DOWN_CHIPS
    tn = chips * 256
    return pl.pallas_call(
        down_back_kernel,
        grid=(hidden // tn,),
        in_specs=[
            pl.BlockSpec((t, width), lambda i: (0, 0)),
            pl.BlockSpec((t, tn), lambda i: (0, i)),
            pl.BlockSpec((chips, 2, 4, r, width), lambda i: (i, 0, 1, 0, 0)),
        ],
        out_specs=[pl.BlockSpec((t, tn), lambda i: (0, i)), pl.BlockSpec((1, tn), lambda i: (0, i))],
        out_shape=[shape((t, hidden), BF16), shape((1, hidden), F32)],
        compiler_params=params(),
        cost_estimate=cost(2 * t * hidden * width, 2 * hidden * width),
        name="down_back",
    )(dc, slope, ffn)


GRAD_PLACES = {
    "d23": (14, 15),
    "d01": (12, 13),
    "x01": (4, 5),
    "y23": (10, 11),
    "x23": (6, 7),
    "y01": (8, 9),
    "f": (0, 1, 2, 3),
}


def runs_of(places):
    return [(at, places[at : at + 2]) for at in range(0, len(places), 2)]


def slope_kernel(parts, x_own, x_oth, *refs):
    dy_own, dy_oth = refs[:parts], refs[parts : 2 * parts]
    outs = refs[2 * parts :]
    for i in range(parts):
        n = dy_own[i].shape[1]
        y = dot(x_own[...], dy_own[i][...]) + dot(x_oth[...], dy_oth[i][...])
        y = y.astype(BF16)
        for places, out in zip(GRAD_PLACES.values(), outs):
            r = out.shape[1]
            for at, run in runs_of(places):
                part = y[run[0] * r : (run[-1] + 1) * r]
                out[at : at + 2, :, i * n : (i + 1) * n] = part.reshape(2, r, n)


def row_slopes(x_own, x_oth, dy_own, dy_oth, tiles):
    half, t = x_own.shape
    r = half // 16
    parts = len(dy_own)
    n = dy_own[0].shape[1] // tiles
    total = n * tiles * parts
    fixed = pl.BlockSpec((half, t), lambda i: (0, 0))
    return pl.pallas_call(
        functools.partial(slope_kernel, parts),
        grid=(tiles,),
        in_specs=[fixed] * 2 + [pl.BlockSpec((t, n), lambda i: (0, i))] * (2 * parts),
        out_specs=[
            pl.BlockSpec((len(p), r, n * parts), lambda i: (0, 0, i)) for p in GRAD_PLACES.values()
        ],
        out_shape=[shape((len(p), r, total), BF16) for p in GRAD_PLACES.values()],
        compiler_params=params(),
        cost_estimate=cost(4 * t * half * total, 8 * t * total + 2 * half * total),
        name="row_slopes",
    )(x_own, x_oth, *dy_own, *dy_oth)


def qkv_slope_kernel(x_own, x_oth, a_own, b_own, a_oth, b_oth, *outs):
    n = a_own.shape[2]
    for i, (own, oth) in enumerate(((a_own, a_oth), (b_own, b_oth))):
        y = dot(x_own[...], own[0]) + dot(x_oth[...], oth[0])
        y = y.astype(BF16)
        for places, out in zip(GRAD_PLACES.values(), outs):
            r = out.shape[1]
            for at, run in runs_of(places):
                part = y[run[0] * r : (run[-1] + 1) * r]
                out[at : at + 2, :, i * n : (i + 1) * n] = part.reshape(2, r, n)


def qkv_slopes(x_own, x_oth, a_own, b_own, a_oth, b_oth):
    half, t = x_own.shape
    r = half // 16
    n = a_own.shape[2]
    fixed = pl.BlockSpec((half, t), lambda i: (0, 0))
    return pl.pallas_call(
        qkv_slope_kernel,
        grid=(3,),
        in_specs=[fixed] * 2 + [pl.BlockSpec((1, t, n), lambda i: (i, 0, 0))] * 4,
        out_specs=[pl.BlockSpec((len(p), r, 2 * n), lambda i: (0, 0, i)) for p in GRAD_PLACES.values()],
        out_shape=[shape((len(p), r, 6 * n), BF16) for p in GRAD_PLACES.values()],
        compiler_params=params(),
        cost_estimate=cost(24 * t * half * n, 24 * t * n + 12 * half * n),
        name="qkv_slopes",
    )(x_own, x_oth, a_own, b_own, a_oth, b_oth)


def block_slope_kernel(where, a_own, a_oth, dy_own, dy_oth, *refs):
    outs = refs[:7]
    stage, sems = refs[7:]
    sent = []
    for places, out in zip(GRAD_PLACES.values(), outs):
        for at, run in runs_of(places):
            i = len(sent)
            mine, other = (
                jnp.concatenate([block_at(act, where, p)[...] for p in run], axis=1)
                for act in (a_own, a_oth)
            )
            y = t_dot(mine, dy_own[...]) + t_dot(other, dy_oth[...])
            stage[i] = y.astype(BF16).reshape(2, LANES, y.shape[1])
            copy = pltpu.make_async_copy(stage.at[i], out.at[pl.ds(at, 2)], sems.at[i])
            copy.start()
            sent.append(copy)
    wait_all(sent)


def block_slopes(where, a_own, a_oth, dy_own, dy_oth):
    t, half = a_own.shape
    width = dy_own.shape[1]
    return pl.pallas_call(
        block_slope_kernel,
        in_specs=[smem_spec()] + [whole_spec()] * 4,
        out_specs=[hbm_spec()] * 7,
        out_shape=[shape((len(p), LANES, width), BF16) for p in GRAD_PLACES.values()],
        scratch_shapes=[pltpu.VMEM((8, 2, LANES, width), BF16), pltpu.SemaphoreType.DMA((8,))],
        compiler_params=params(),
        cost_estimate=cost(4 * t * half * width, 4 * t * (half + width) + 2 * half * width),
        name="block_slopes",
    )(where, a_own, a_oth, dy_own, dy_oth)


def up_back_kernel(where, de, valid, g2_ref, g3_ref, w_ref, mid_hbm, att_hbm, cot_hbm, *refs):
    pieces = refs[:10]
    dmid_ref, datt_ref, dmix_ref, sums_ref, acc, wbuf, mid_buf, att_buf, cot_buf, sems = refs[10:]
    step = pl.program_id(0)
    t, width = acc.shape

    @pl.when(step == 0)
    def _():
        assemble(where, pieces, wbuf, sems, (width, width))
        fetch((mid_hbm, att_hbm, cot_hbm), (mid_buf, att_buf, cot_buf), sems, 32)

    y = dot_t(de[...], w_ref[:, 0].reshape(width, -1))

    @pl.when(step == 0)
    def _():
        acc[...] = y

    @pl.when(step > 0)
    def _():
        acc[...] += y

    @pl.when(step == pl.num_programs(0) - 1)
    def _():
        for i in range(32):
            pltpu.make_async_copy(pieces[0].at[0, :, pl.ds(width, width)], wbuf.at[0, 0], sems.at[i]).wait()
        for i, (a, b) in enumerate(((mid_hbm, mid_buf), (att_hbm, att_buf), (cot_hbm, cot_buf))):
            pltpu.make_async_copy(a, b, sems.at[32 + i]).wait()
        tile = 128
        g2, g3 = g2_ref[...], g3_ref[...]
        w = matrix(wbuf)
        sums = [jnp.zeros((1, width), F32)] * 3
        for i in range(t // tile):
            rows = slice(i * tile, (i + 1) * tile)
            e = acc[rows, :]
            mid = mid_buf[rows, :]
            r3 = inverse_rms(mid)
            dmid = cot_buf[rows, :].astype(F32) * valid[rows, :] + rms_back(mid, r3, g3, e)
            dmid_ref[rows, :] = dmid
            att = att_buf[rows, :]
            r2 = inverse_rms(att)
            datt = rms_back(att, r2, g2, dmid).astype(BF16)
            datt_ref[rows, :] = datt
            sums[0] += row_sum(mid * r3 * e)
            sums[1] += row_sum(att * r2 * dmid)
            sums[2] += row_sum(datt.astype(F32))
        dmix_ref[...] = dot_t(datt_ref[...], w).astype(BF16)
        for i in range(3):
            sums_ref[i : i + 1, :] = sums[i]


def up_back(where, de, mid, att, cot, valid, g2, g3, ffn, pieces):
    t, width = mid.shape
    hidden = de.shape[1]
    tk = ffn.shape[3]
    r = pieces[0].shape[1]
    fixed = lambda a: pl.BlockSpec(a.shape, lambda i: (0, 0))
    return pl.pallas_call(
        up_back_kernel,
        grid=(hidden // tk,),
        in_specs=[smem_spec(), pl.BlockSpec((t, tk), lambda i: (0, i))]
        + [fixed(a) for a in (valid, g2, g3)]
        + [pl.BlockSpec((ffn.shape[0], 1, ffn.shape[2], tk), lambda i: (0, i, 0, 0))]
        + [hbm_spec()] * 13,
        out_specs=[pl.BlockSpec((t, width), lambda i: (0, 0))] * 3
        + [pl.BlockSpec((8, width), lambda i: (0, 0))],
        out_shape=[shape((t, width), F32), shape((t, width), BF16), shape((t, width), BF16), shape((8, width), F32)],
        scratch_shapes=[
            pltpu.VMEM((t, width), F32),
            pltpu.VMEM((16, 2, r, width), BF16),
            pltpu.VMEM((t, width), F32),
            pltpu.VMEM((t, width), F32),
            pltpu.VMEM((t, width), BF16),
            pltpu.SemaphoreType.DMA((35,)),
        ],
        compiler_params=params(),
        cost_estimate=cost(2 * t * width * hidden, 2 * width * hidden + 2 * t * hidden),
        name="up_back",
    )(where, de, valid, g2, g3, ffn, mid, att, cot, *pieces)


def in_back_kernel(where, *refs):
    d_a, d_b, x_hbm, dmid_hbm, g1_ref = refs[:5]
    qk, vo = refs[5:15], refs[15:25]
    out_ref, sums_ref, wbuf, x_buf, dmid_buf, sems = refs[25:]
    t, width = out_ref.shape
    half = width // 2
    copies = [
        assemble(where, pieces, wbuf.at[i], sems.at[i], (start, width))
        for i, (pieces, start) in enumerate(((qk, 0), (qk, width), (vo, 0)))
    ]
    late = fetch((x_hbm, dmid_hbm), (x_buf, dmid_buf), sems.at[3])
    e = None
    for i in range(3):
        wait_all(copies[i])
        d = jnp.concatenate([d_a[i], d_b[i]], axis=1)
        y = dot_t(d, wbuf[i].reshape(width, width))
        e = y if e is None else e + y
    wait_all(late)
    gain = g1_ref[...]
    tile = 128
    total = jnp.zeros((1, width), F32)
    for i in range(t // tile):
        rows = slice(i * tile, (i + 1) * tile)
        x = x_buf[rows, :].astype(F32)
        r = inverse_rms(x)
        out_ref[rows, :] = dmid_buf[rows, :] + rms_back(x, r, gain, e[rows, :])
        total += row_sum(x * r * e[rows, :])
    sums_ref[...] = total


def in_back(where, d_a, d_b, x, dmid, g1, qk_pieces, vo_pieces):
    t, width = x.shape
    r = qk_pieces[0].shape[1]
    return pl.pallas_call(
        in_back_kernel,
        in_specs=[smem_spec()] + [whole_spec()] * 2 + [hbm_spec()] * 2 + [whole_spec()] + [hbm_spec()] * 20,
        out_specs=[whole_spec()] * 2,
        out_shape=[shape((t, width), F32), shape((1, width), F32)],
        scratch_shapes=[
            pltpu.VMEM((3, 16, 2, r, width), BF16),
            pltpu.VMEM((t, width), BF16),
            pltpu.VMEM((t, width), F32),
            pltpu.SemaphoreType.DMA((4, 32)),
        ],
        compiler_params=params(),
        cost_estimate=cost(6 * t * width * width, 6 * width * width),
        name="in_back",
    )(where, d_a, d_b, x, dmid, g1, *qk_pieces, *vo_pieces)


def after(*values):
    return lax.optimization_barrier(values)


def add(*values):
    total = values[0].astype(F32)
    for v in values[1:]:
        total = total + v.astype(F32)
    return total


class Gather:
    def __init__(self, net, shard):
        self.net = net
        self.line = [shard] + [net.swap(shard, 4 * m) for m in (1, 2, 3)]

    def spread(self, line):
        net = self.net
        self.lines = jnp.stack(line)
        self.x = net.swap(self.lines, 1)
        self.y = net.swap(self.lines, 2)
        self.sib = [net.sibling(self.lines)]

    def corner(self, x, y):
        net = self.net
        self.x, self.y = x, y
        self.d01 = net.swap(x[:2], 2)
        self.d23 = net.swap(y[2:], 1)
        self.sib += [net.sibling(x), net.sibling(y)]

    def finish(self, d01, d23):
        net = self.net
        self.d01, self.d23 = d01, d23
        self.sib += [net.sibling(d01), net.sibling(d23)]

    def pieces(self):
        return [self.lines, self.x, self.y, self.d01, self.d23] + self.sib


class Scatter:
    def __init__(self, net, pieces):
        self.net = net
        self.pieces = pieces

    def a(self):
        d23, d01, *self.rest = self.pieces
        self.got = [self.net.swap(d23, 1), self.net.swap(d01, 2)]

    def b(self, got):
        r23, r01 = got
        x01, y23, *self.rest = self.rest
        self.got = [
            self.net.swap(add(x01, r01).astype(BF16), 1),
            self.net.swap(add(y23, r23).astype(BF16), 2),
        ]

    def c(self, got):
        self.low, self.high = got
        x23, y01, self.f = self.rest
        self.got = [self.net.swap(x23, 1), self.net.swap(y01, 2)]

    def near(self, got):
        rx23, ry01 = got
        low = add(self.f[:2], self.low, ry01)
        high = add(self.f[2:], self.high, rx23)
        self.keep = low[0], high[0]
        self.got = [self.net.swap(jnp.stack([low[1], high[1]]).astype(BF16), 4)]

    def far(self, got):
        low, high = self.keep
        self.own = add(low, got[0][0])
        self.got = [self.net.swap(add(high, got[0][1]).astype(BF16), 8)]

    def result(self, got):
        return add(self.own, got[0])


def shards_16(
    activations,
    segment_ids,
    cotangent,
    querymat,
    keymat,
    valuemat,
    outmat,
    upmatrix,
    downmatrix,
    querybias,
    keybias,
    valuebias,
    outbias,
    upbias,
    downbias,
    firstgain,
    secondgain,
    thirdgain,
    fourthgain,
):
    net = Net(16)
    t, width = activations.shape
    rows = querymat.shape[0]
    hidden = upmatrix.shape[1]
    block = upbias.shape[0]
    half = width // 2
    me, core = net.me, net.core
    device = me * 2 + core
    where = jnp.stack([me, core]).astype(I32)

    dst = jnp.arange(width)
    place = (dst // rows) % 16
    chip = me ^ (place // 4 + 4 * (place % 4))
    src = chip * (2 * rows) + (core ^ (dst // half)) * rows + dst % rows
    order = (src[:, None] == jnp.arange(width)[None, :]).astype(BF16)
    slots = jnp.arange(t)
    segment = jnp.where(segment_ids >= 0, segment_ids, -1 - slots)
    col, row = segment[:, None], segment[None, :]
    valid = (segment_ids >= 0).astype(F32)[:, None]
    spots = positions_of(segment_ids).astype(F32)
    inverse = 10000.0 ** (-jnp.arange(HEAD // 2).astype(F32) * 2.0 / HEAD)
    angles = spots[:, None] * inverse[None, :]
    cosine = jnp.tile(jnp.cos(angles), (1, 4))
    sine = jnp.sin(angles)
    sine = jnp.tile(jnp.concatenate([-sine, sine], axis=1), (1, 2))

    ffn_shard = jnp.concatenate(
        [upmatrix.reshape(rows, 4, width).transpose(1, 0, 2), downmatrix.reshape(4, rows, width)]
    )
    ffn = lax.all_gather(ffn_shard, AXES, axis=0, tiled=False)
    qk = Gather(net, jnp.concatenate([querymat, keymat], axis=1))
    vo_shard = jnp.concatenate([valuemat, outmat], axis=1)
    nine = [querybias, keybias, valuebias, outbias, downbias, firstgain, secondgain, thirdgain, fourthgain]
    small = jnp.concatenate([jnp.pad(v[None], ((0, 0), (0, LANES - rows))) for v in nine] + [upbias[None]])
    buf = small[None]
    buf = jnp.concatenate([buf, net.sibling(buf)])
    for mask in (1, 2, 4, 8):
        buf = jnp.concatenate([buf, net.swap(buf, mask)])
    line, buf, vo_shard = after(qk.line, buf, vo_shard)
    qk.spread(line)
    vo = Gather(net, vo_shard)

    picks = (jnp.arange(32)[:, None] ^ device) == jnp.arange(32)[None, :]
    small_all = dot(picks.astype(BF16), buf.reshape(32, -1)).reshape(32, 10, LANES)
    b_q, b_k, b_v, b_o, b_d, g1, g2, g3, g4 = (
        small_all[:, i, :rows].reshape(1, width) for i in range(9)
    )
    b_up = small_all[:, 9].reshape(1, hidden)
    inputs = activations.astype(F32)
    normed = (inputs * inverse_rms(inputs) * g1).astype(BF16)
    turned = dot_t(order, normed).astype(BF16)
    x_own, x_sib = turned[:half], turned[half:]

    x, y, line = after(qk.x, qk.y, vo.line)
    qk.corner(x, y)
    vo.spread(line)
    d01, d23, x_sib, normed = after(qk.d01, qk.d23, x_sib, normed)
    qk.finish(d01, d23)
    x_oth = net.sibling(x_sib)
    x, y = after(vo.x, vo.y)
    vo.corner(x, y)
    qk_pieces = qk.pieces()
    qk_rot = project(where, normed, qk_pieces, 2, jnp.concatenate([b_q, b_k], axis=1), (cosine, sine))
    d01, d23, qk_rot = after(vo.d01, vo.d23, qk_rot)
    vo.finish(d01, d23)
    vo_pieces = vo.pieces()
    v = project(where, normed, vo_pieces, 1, b_v)
    mixed, lse = attend(qk_rot, v, col, row)
    m_own, m_sib, att, mid, normed_mid, n_own, n_sib = out_project(
        where, mixed, order, activations, b_o, g2, g3, vo_pieces
    )
    m_oth = net.sibling(m_sib)
    n_oth = net.sibling(n_sib)
    a_own, a_sib, slope = up_project(where, normed_mid, b_up, ffn)
    a_oth = net.sibling(a_sib)
    ffn_down = ffn.reshape(16, 2, 8, rows, width)
    layer_out, dc, down_sums, power = down_project(
        where, a_own, a_sib, b_d, mid, cotangent, valid, g4, ffn_down
    )

    dc_oth = net.sibling(dc)
    dc, dc_oth, a_oth = after(dc, dc_oth, a_oth)
    slopes, dc = after(block_slopes(where, a_own, a_oth, dc, dc_oth), dc)
    down_sum = Scatter(net, slopes)

    down_sum.a()
    de, up_bias_sum = down_back(dc, slope, ffn_down)
    de, got = after(de, down_sum.got)

    down_sum.b(got)
    de_oth = net.sibling(de)
    back = up_back(where, de, mid, att, cotangent, valid, g2, g3, ffn, vo_pieces)
    back, de_oth, de, got, n_own = after(back, de_oth, de, down_sum.got, n_own)
    dmid, datt, dmix, mid_sums = back

    down_sum.c(got)
    datt_oth = net.sibling(datt)
    slopes = row_slopes(n_own, n_oth, [de], [de_oth], 4)
    slopes, got, datt_oth, datt, dmix = after(slopes, down_sum.got, datt_oth, datt, dmix)
    up_sum = Scatter(net, slopes)

    down_sum.near(got)
    up_sum.a()
    steps = width // LANES // 2
    part_a = attend_back(qk_rot, v, dmix, lse, col, row, cosine, sine, 0, steps)
    part_a, dmix, got, up_got = after(part_a, dmix, down_sum.got, up_sum.got)
    d_a, sums_a = part_a

    down_sum.far(got)
    up_sum.b(up_got)
    a_other = net.sibling(d_a)
    part_b = attend_back(qk_rot, v, dmix, lse, col, row, cosine, sine, steps, steps)
    part_b, datt, got, up_got, a_other, m_own = after(
        part_b, datt, down_sum.got, up_sum.got, a_other, m_own
    )
    d_b, sums_b = part_b
    down_total = down_sum.result(got)

    up_sum.c(up_got)
    b_other = net.sibling(d_b)
    slopes = row_slopes(m_own, m_oth, [datt], [datt_oth], 1)
    out_sum = Scatter(net, slopes)
    slopes, b_other, d_a, d_b, a_other = after(slopes, b_other, d_a, d_b, a_other)
    slopes = qkv_slopes(x_own, x_oth, d_a, d_b, a_other, b_other)
    slopes, up_got, d_a, d_b = after(slopes, up_sum.got, d_a, d_b)
    qkv_sum = Scatter(net, slopes)

    up_sum.near(up_got)
    qkv_sum.a()
    input_gradient, first_sum = in_back(where, d_a, d_b, activations, dmid, g1, qk_pieces, vo_pieces)
    qkv_sums = jnp.concatenate([sums_a, sums_b], axis=1)
    first_sum, qkv_sums, got, up_got = after(first_sum, qkv_sums, qkv_sum.got, up_sum.got)

    up_sum.far(up_got)
    qkv_sum.b(got)
    sums = jnp.concatenate(
        [
            qkv_sums[0],
            qkv_sums[1],
            qkv_sums[2],
            mid_sums[2],
            down_sums[1],
            first_sum[0],
            mid_sums[1],
            mid_sums[0],
            down_sums[0],
            up_bias_sum[0],
            power[0],
        ]
    ).reshape(-1, LANES)
    sums = sums + net.sibling(sums)
    got, sums, out_sum.pieces = after(qkv_sum.got, sums, out_sum.pieces)

    qkv_sum.c(got)
    sums = sums + net.swap(sums, 1)
    got, up_got, sums, out_sum.pieces = after(qkv_sum.got, up_sum.got, sums, out_sum.pieces)
    up_total = up_sum.result(up_got)

    qkv_sum.near(got)
    out_sum.a()
    sums = sums + net.swap(sums, 2)
    out_got, sums = after(out_sum.got, sums)

    out_sum.b(out_got)
    out_got, got = after(out_sum.got, qkv_sum.got)

    qkv_sum.far(got)
    out_sum.c(out_got)
    sums = sums + net.swap(sums, 4)
    out_got, sums = after(out_sum.got, sums)

    out_sum.near(out_got)
    sums = sums + net.swap(sums, 8)
    out_got, got = after(out_sum.got, qkv_sum.got)

    out_sum.far(out_got)
    qkv_total = qkv_sum.result(got)
    out_total = out_sum.result(out_sum.got)
    qkv_total = [qkv_total[:, i * width : (i + 1) * width] for i in range(3)]

    sums = sums.reshape(-1)
    output_power = sums[-1] / (t * 32)
    own = lax.dynamic_slice_in_dim(sums[: 9 * width].reshape(9, width), device * rows, rows, 1)
    own_up = lax.dynamic_slice_in_dim(sums[9 * width : 9 * width + hidden], device * block, block, 0)
    return (
        layer_out,
        input_gradient,
        *qkv_total,
        out_total,
        up_total,
        down_total,
        own[0],
        own[1],
        own[2],
        own[3],
        own_up,
        own[4],
        own[5],
        own[6],
        own[7],
        own[8],
        output_power,
    )


def shards(*args):
    rows, length = args[3].shape[0], args[0].shape[0]
    if lax.axis_size("wide") == 16 and rows == 32 and length == 512:
        return shards_16(*args)
    return shards_any(*args)


def solution(mesh):
    matrix = P(AXES, None)
    vector = P(AXES)
    return jax.shard_map(
        shards,
        mesh=mesh,
        in_specs=(matrix, vector, matrix) + (matrix,) * 6 + (vector,) * 10,
        out_specs=(matrix,) * 8 + (vector,) * 10 + (P(),),
        check_vma=False,
    )
```

```python
import jax
import jax.numpy as jnp
import functools

from jax import lax
from jax.experimental import pallas as pl
from jax.experimental.pallas import tpu as pltpu
from jax.sharding import PartitionSpec as P

HEAD = 64
AXES = ("wide", "narrow")


def rms_norm(values, gain):
    return values * lax.rsqrt(jnp.mean(values * values, axis=-1, keepdims=True) + 1e-06) * gain


def rotate(values, cosine, sine):
    midpoint = values.shape[-1] // 2
    first_half = values[..., :midpoint]
    second_half = values[..., midpoint:]
    return jnp.concatenate(
        [first_half * cosine - second_half * sine, first_half * sine + second_half * cosine],
        axis=-1,
    )


def positions_of(segment):
    places = jnp.arange(segment.shape[0])
    matching = segment[:, None] == segment[None, :]
    earlier = places[None, :] < places[:, None]
    return jnp.sum(jnp.logical_and(matching, earlier).astype(jnp.int32), axis=1)


def angle_tables(segment):
    places = positions_of(segment).astype(jnp.float32)
    midpoint = HEAD // 2
    inverse = 10000.0 ** (-jnp.arange(midpoint).astype(jnp.float32) * 2.0 / HEAD)
    angles = places[:, None] * inverse[None, :]
    return (jnp.cos(angles)[:, None, :], jnp.sin(angles)[:, None, :])


def key_mask(segment):
    places = jnp.arange(segment.shape[0])
    matching = segment[:, None] == segment[None, :]
    allowed = matching & (segment[None, :] >= 0) & (places[None, :] <= places[:, None])
    return allowed | (places[None, :] == places[:, None])


def contract_rows(left, right):
    return lax.dot_general(
        left, right, (((0,), (0,)), ((), ())), preferred_element_type=jnp.float32
    )


def times_transpose(left, right):
    return lax.dot_general(
        left, right, (((1,), (1,)), ((), ())), preferred_element_type=jnp.float32
    )


def product(left, right):
    return jnp.dot(left, right, preferred_element_type=jnp.float32)


def column_sums(values):
    return jnp.sum(values.astype(jnp.float32), axis=0)


def masked_scores(query_rot, key_rot, allowed):
    scores = (
        jnp.einsum("qhd,khd->hqk", query_rot, key_rot, preferred_element_type=jnp.float32) * 0.125
    )
    return jnp.where(allowed[None], scores, -1e30)


class Net:
    def __init__(self, wide):
        self.wide = wide
        self.me = lax.axis_index("wide")
        self.core = lax.axis_index("narrow")
        outer = []
        mask = wide // 2
        while mask > 2:
            outer.append(mask)
            mask //= 2
        self.outer = outer

    def swap(self, value, mask):
        pairs = [(d, d ^ mask) for d in range(self.wide)]
        return lax.ppermute(value, "wide", pairs)

    def sibling(self, value):
        return lax.ppermute(value, "narrow", [(0, 1), (1, 0)])

    def bit(self, mask):
        return (self.me & mask) != 0

    def grow(self, value, mask, axis):
        other = self.swap(value, mask)
        bit = self.bit(mask)
        low = jnp.where(bit, other, value)
        high = jnp.where(bit, value, other)
        return jnp.stack([low, high], axis=axis)

    def shrink(self, value, mask, axis):
        bit = self.bit(mask).astype(jnp.int32)
        mine = lax.dynamic_index_in_dim(value, bit, axis, keepdims=False)
        theirs = lax.dynamic_index_in_dim(value, 1 - bit, axis, keepdims=False)
        other = self.swap(theirs, mask)
        return (mine.astype(jnp.float32) + other.astype(jnp.float32)).astype(jnp.bfloat16)

    def gather(self, first, second):
        r, c = first.shape
        both = jnp.stack([first, second])[None]
        for mask in self.outer:
            both = self.grow(both, mask, 1).reshape(-1, 2, r, c)
        outer = both.shape[0]
        a = self.grow(both[:, 0], 1, 1)
        a = self.grow(a, 2, 1)
        b = self.grow(both[:, 1], 2, 1)
        b = self.grow(b, 1, 2)
        return jnp.stack([a, b], axis=3).reshape(outer * 4 * 2 * r, c)

    def scatter(self, full):
        rows, c = full.shape
        r = rows // (self.wide * 2)
        outer = self.wide // 4
        parts = full.reshape(outer, 2, 2, 2, r, c)
        a, b = parts[:, :, :, 0], parts[:, :, :, 1]
        a = self.shrink(self.shrink(a, 2, 1), 1, 1)
        b = self.shrink(self.shrink(b, 1, 2), 2, 1)
        both = jnp.stack([a, b], axis=1)
        for mask in reversed(self.outer):
            count = both.shape[0] // 2
            both = self.shrink(both.reshape(count, 2, 2, r, c), mask, 1)
        return both[0, 0], both[0, 1]

    def gather_small(self, value):
        other = self.sibling(value)
        core = self.core == 1
        buf = jnp.stack([jnp.where(core, other, value), jnp.where(core, value, other)])[None]
        for mask in [1, 2] + self.outer[::-1]:
            buf = self.grow(buf, mask, 0).reshape(1, -1, *value.shape)
        return buf[0]

    def total(self, value):
        value = value + self.sibling(value)
        for mask in [1, 2] + self.outer[::-1]:
            value = value + self.swap(value, mask)
        return value

    def pick(self, value, axis):
        mine = lax.dynamic_index_in_dim(value, self.core, axis, keepdims=False)
        theirs = lax.dynamic_index_in_dim(value, 1 - self.core, axis, keepdims=False)
        return mine, theirs

    def halves(self, mine, theirs):
        core = self.core == 1
        return jnp.where(core, theirs, mine), jnp.where(core, mine, theirs)

    def columns_in(self, shard):
        mine, theirs = self.pick(shard, 1)
        return self.halves(mine, self.sibling(theirs))

    def columns_out(self, first, second):
        mine, theirs = self.pick(jnp.stack([first, second]), 0)
        other = self.sibling(theirs)
        left, right = self.halves(mine, other)
        return jnp.stack([left, right], axis=1)


def shards_any(
    activations,
    segment_ids,
    cotangent,
    querymat,
    keymat,
    valuemat,
    outmat,
    upmatrix,
    downmatrix,
    querybias,
    keybias,
    valuebias,
    outbias,
    upbias,
    downbias,
    firstgain,
    secondgain,
    thirdgain,
    fourthgain,
):
    wide = lax.axis_size("wide")
    net = Net(wide)
    core = net.core
    length, width = activations.shape
    rows = querymat.shape[0]
    hidden = upmatrix.shape[1]
    block = hidden // (2 * wide)
    half = width // 2
    heads = width // HEAD
    f32 = jnp.float32
    bf16 = jnp.bfloat16

    nine = [querybias, keybias, valuebias, outbias, downbias, firstgain, secondgain, thirdgain, fourthgain]
    small = jnp.concatenate([jnp.concatenate(nine), upbias])
    qkv_shard = jnp.concatenate(
        [m.reshape(rows, 2, half) for m in (querymat, keymat, valuemat)], axis=2
    )
    up_shard = upmatrix.reshape(rows, wide, 2, block).transpose(0, 2, 1, 3).reshape(rows, 2, hidden // 2)
    out_shard = outmat.reshape(rows, 2, half)
    small_all = net.gather_small(small)
    qkv_mine = net.gather(*net.columns_in(qkv_shard))
    out_mine = net.gather(*net.columns_in(out_shard))
    up_mine = net.gather(*net.columns_in(up_shard))
    down_rows = downmatrix.shape[0]
    down_mine = net.gather(downmatrix[: down_rows // 2], downmatrix[down_rows // 2 :])
    qkv_theirs, out_theirs, up_theirs, down_theirs = map(
        net.sibling, (qkv_mine, out_mine, up_mine, down_mine)
    )

    vectors = small_all[:, : 9 * rows].reshape(-1, 9, rows).transpose(1, 0, 2).reshape(9, width)
    vectors = vectors.astype(f32)
    bias_query, bias_key, bias_value, bias_output, bias_down = (vectors[i] for i in range(5))
    gain_first, gain_second, gain_third, gain_fourth = (vectors[i] for i in range(5, 9))
    bias_up_pair = small_all[:, 9 * rows :].reshape(wide, 2, block).astype(f32)
    bias_up_mine, bias_up_theirs = (v.reshape(-1) for v in net.pick(bias_up_pair, 1))

    def natural(mine, theirs):
        return jnp.where(
            core == 1,
            jnp.concatenate([theirs, mine], axis=-1),
            jnp.concatenate([mine, theirs], axis=-1),
        )

    inputs = activations.astype(f32)
    cosine, sine = angle_tables(segment_ids)
    allowed = key_mask(segment_ids)
    valid_row = (segment_ids >= 0).astype(f32)
    normed_in, pull_first = jax.vjp(rms_norm, inputs, gain_first)
    normed_low = normed_in.astype(bf16)
    normed_low_theirs = net.sibling(normed_low)
    qkv_m = product(normed_low, qkv_mine)
    qkv_t = product(normed_low, qkv_theirs)
    queries, keys_pre, values_pre = (
        natural(qkv_m[:, i * half : (i + 1) * half], qkv_t[:, i * half : (i + 1) * half]) + b
        for i, b in enumerate((bias_query, bias_key, bias_value))
    )
    query_rot = rotate(queries.reshape(length, heads, HEAD), cosine, sine).astype(bf16)
    key_rot = rotate(keys_pre.reshape(length, heads, HEAD), cosine, sine).astype(bf16)
    value_low = values_pre.reshape(length, heads, HEAD).astype(bf16)
    scores = masked_scores(query_rot, key_rot, allowed)
    peak = jnp.max(scores, axis=-1, keepdims=True)
    exponent = jnp.exp(scores - peak)
    totals = jnp.sum(exponent, axis=-1, keepdims=True)
    logsum = peak + jnp.log(totals)
    probs = exponent / totals
    mixed = jnp.einsum(
        "hqk,khd->qhd", probs.astype(bf16), value_low, preferred_element_type=f32
    )
    mixed_low = mixed.reshape(length, width).astype(bf16)
    mixed_low_theirs = net.sibling(mixed_low)
    attended = natural(product(mixed_low, out_mine), product(mixed_low, out_theirs)) + bias_output
    normed_att, pull_second = jax.vjp(rms_norm, attended, gain_second)
    middle = inputs + normed_att
    normed_mid, pull_third = jax.vjp(rms_norm, middle, gain_third)
    normed_mid_low = normed_mid.astype(bf16)
    normed_mid_low_theirs = net.sibling(normed_mid_low)
    act_m_f, pull_gelu_m = jax.vjp(jax.nn.gelu, product(normed_mid_low, up_mine) + bias_up_mine)
    act_t_f, pull_gelu_t = jax.vjp(jax.nn.gelu, product(normed_mid_low, up_theirs) + bias_up_theirs)
    act_m = act_m_f.astype(bf16)
    act_t = act_t_f.astype(bf16)
    act_other = net.sibling(act_t)
    contracted = product(act_m, down_mine) + product(act_t, down_theirs) + bias_down
    local_power = jnp.sum(valid_row * jnp.mean(contracted * contracted, axis=-1))
    normed_out, pull_fourth = jax.vjp(rms_norm, contracted, gain_fourth)
    layer_out = (middle + normed_out).astype(bf16)

    seed = cotangent.astype(f32) * valid_row[:, None]
    d_contracted_f, fourth_slope = pull_fourth(seed)
    d_contracted = d_contracted_f.astype(bf16)
    d_contracted_theirs = net.sibling(d_contracted)
    down_bias_slope = column_sums(d_contracted)
    d_exp_m = pull_gelu_m(times_transpose(d_contracted, down_mine))[0].astype(bf16)
    d_exp_t = pull_gelu_t(times_transpose(d_contracted, down_theirs))[0].astype(bf16)
    d_exp_other = net.sibling(d_exp_t)

    def both_rows(a, b):
        return jnp.concatenate([a, b], axis=0)

    down_slope = contract_rows(
        both_rows(act_m, act_other), both_rows(d_contracted, d_contracted_theirs)
    ).astype(bf16)
    down_sum = net.scatter(down_slope)
    up_slope = contract_rows(
        both_rows(normed_mid_low, normed_mid_low_theirs), both_rows(d_exp_m, d_exp_other)
    ).astype(bf16)
    up_sum = net.scatter(up_slope)
    up_bias_m, up_bias_t = column_sums(d_exp_m), column_sums(d_exp_t)
    d_normed_mid = times_transpose(d_exp_m, up_mine) + times_transpose(d_exp_t, up_theirs)
    d_middle_part, third_slope = pull_third(d_normed_mid)
    d_middle = seed + d_middle_part
    d_attended_f, second_slope = pull_second(d_middle)
    d_attended = d_attended_f.astype(bf16)
    output_bias_slope = column_sums(d_attended)
    d_att_m, d_att_t = net.pick(d_attended.reshape(length, 2, half), 1)
    d_att_other = net.sibling(d_att_t)
    out_slope = contract_rows(
        both_rows(mixed_low, mixed_low_theirs), both_rows(d_att_m, d_att_other)
    ).astype(bf16)
    out_sum = net.scatter(out_slope)
    d_mixed = (
        (times_transpose(d_att_m, out_mine) + times_transpose(d_att_t, out_theirs))
        .astype(bf16)
        .reshape(length, heads, HEAD)
    )
    probs_again = jnp.exp(masked_scores(query_rot, key_rot, allowed) - logsum)
    d_values = jnp.einsum(
        "hqk,qhd->khd", probs_again.astype(bf16), d_mixed, preferred_element_type=f32
    )
    d_probs = jnp.einsum("qhd,khd->hqk", d_mixed, value_low, preferred_element_type=f32)
    row_terms = jnp.sum(probs_again * d_probs, axis=-1, keepdims=True)
    d_scores = (probs_again * (d_probs - row_terms)).astype(bf16)
    d_query_rot = (
        jnp.einsum("hqk,khd->qhd", d_scores, key_rot, preferred_element_type=f32) * 0.125
    )
    d_key_rot = (
        jnp.einsum("hqk,qhd->khd", d_scores, query_rot, preferred_element_type=f32) * 0.125
    )
    d_queries = rotate(d_query_rot, cosine, -sine).reshape(length, width).astype(bf16)
    d_keys = rotate(d_key_rot, cosine, -sine).reshape(length, width).astype(bf16)
    d_values_low = d_values.reshape(length, width).astype(bf16)
    pairs = [net.pick(v.reshape(length, 2, half), 1) for v in (d_queries, d_keys, d_values_low)]
    d_qkv_m = jnp.concatenate([p[0] for p in pairs], axis=1)
    d_qkv_t = jnp.concatenate([p[1] for p in pairs], axis=1)
    d_qkv_other = net.sibling(d_qkv_t)
    qkv_slope = contract_rows(
        both_rows(normed_low, normed_low_theirs), both_rows(d_qkv_m, d_qkv_other)
    ).astype(bf16)
    qkv_sum = net.scatter(qkv_slope)
    d_normed = times_transpose(d_qkv_m, qkv_mine) + times_transpose(d_qkv_t, qkv_theirs)
    d_inputs_part, first_slope = pull_first(d_normed)
    input_gradient = d_middle + d_inputs_part

    up_bias_low = jnp.where(core == 1, up_bias_t, up_bias_m).reshape(wide, 1, block)
    up_bias_high = jnp.where(core == 1, up_bias_m, up_bias_t).reshape(wide, 1, block)
    up_bias_slope = jnp.concatenate([up_bias_low, up_bias_high], axis=1).reshape(-1)
    small_slopes = jnp.concatenate(
        [
            column_sums(d_queries),
            column_sums(d_keys),
            column_sums(d_values_low),
            output_bias_slope,
            down_bias_slope,
            first_slope,
            second_slope,
            third_slope,
            fourth_slope,
            up_bias_slope,
            jnp.full((128,), local_power, f32),
        ]
    )
    sums = net.total(small_slopes)
    output_power = sums[-1] / (length * wide * 2)
    device = net.me * 2 + core
    own = lax.dynamic_slice_in_dim(sums[: 9 * width].reshape(9, width), device * rows, rows, 1)
    own_up = lax.dynamic_slice_in_dim(sums[9 * width : 9 * width + hidden], device * 2 * block // 2, block, 0)

    qkv_grad = net.columns_out(*qkv_sum).astype(f32)
    out_grad = net.columns_out(*out_sum).astype(f32).reshape(rows, width)
    up_grad = net.columns_out(*up_sum).astype(f32)
    up_grad = up_grad.reshape(rows, 2, wide, block).transpose(0, 2, 1, 3).reshape(rows, hidden)
    down_grad = jnp.concatenate(down_sum, axis=0).astype(f32)
    q_grad, k_grad, v_grad = (
        qkv_grad[:, :, i * half : (i + 1) * half].reshape(rows, width) for i in range(3)
    )
    return (
        layer_out,
        input_gradient,
        q_grad,
        k_grad,
        v_grad,
        out_grad,
        up_grad,
        down_grad,
        own[0],
        own[1],
        own[2],
        own[3],
        own_up,
        own[4],
        own[5],
        own[6],
        own[7],
        own[8],
        output_power,
    )


F32 = jnp.float32
BF16 = jnp.bfloat16
I32 = jnp.int32
EPS = 1e-06
VMEM_LIMIT = 60 * 1024 * 1024
LANES = 128
GELU_A = 0.7978845608028654
GELU_B = 0.044715
TILE = 128
UP_TILE = 1024
DOWN_CHIPS = 4


def whole_spec():
    return pl.BlockSpec(memory_space=pltpu.VMEM)


def hbm_spec():
    return pl.BlockSpec(memory_space=pl.ANY)


def smem_spec():
    return pl.BlockSpec(memory_space=pltpu.SMEM)


def params():
    return pltpu.CompilerParams(vmem_limit_bytes=VMEM_LIMIT)


def shape(dims, dtype):
    return jax.ShapeDtypeStruct(dims, dtype)


def cost(flops, bytes_accessed):
    return pl.CostEstimate(flops=flops, bytes_accessed=bytes_accessed, transcendentals=0)


def dot(a, b):
    return lax.dot_general(a, b, (((1,), (0,)), ((), ())), preferred_element_type=F32)


def dot_t(a, b):
    return lax.dot_general(a, b, (((1,), (1,)), ((), ())), preferred_element_type=F32)


def t_dot(a, b):
    return lax.dot_general(a, b, (((0,), (0,)), ((), ())), preferred_element_type=F32)


def pair_mask(place):
    return place // 4 + 4 * (place % 4)


def assemble(where, pieces, target, sems, cols):
    copies = []
    for e in range(2):
        place = 0
        for piece in pieces[e * 5 : e * 5 + 5]:
            for j in range(piece.shape[0]):
                chip = where[0] ^ pair_mask(place)
                source = piece.at[j, :, pl.ds(*cols)]
                dest = target.at[chip, where[1] ^ e]
                copies.append(pltpu.make_async_copy(source, dest, sems.at[len(copies)]))
                place += 1
    for copy in copies:
        copy.start()
    return copies


def wait_all(copies):
    for copy in copies:
        copy.wait()


def fetch(sources, targets, sems, base=0):
    copies = [
        pltpu.make_async_copy(a, b, sems.at[base + i]) for i, (a, b) in enumerate(zip(sources, targets))
    ]
    for copy in copies:
        copy.start()
    return copies


def matrix(buf):
    return buf[...].reshape(-1, buf.shape[-1])


def inverse_rms(v):
    return lax.rsqrt(jnp.mean(v * v, axis=-1, keepdims=True) + EPS)


def place_rows(first, rows):
    n = rows[0].shape[1]
    at = lax.broadcasted_iota(I32, (8, n), 0)
    out = jnp.zeros((8, n), F32)
    for i, row in enumerate(rows):
        out = jnp.where(at == first + i, jnp.broadcast_to(row, (8, n)), out)
    return out


def rms_back(v, r, gain, e):
    ge = gain * e
    return r * ge - v * (r * r * r) * jnp.mean(v * ge, axis=-1, keepdims=True)


def row_sum(v):
    return jnp.sum(v, axis=0, keepdims=True)


def turn(v, cosine, sine):
    lane = lax.broadcasted_iota(I32, v.shape, 1)
    swapped = jnp.where((lane & 63) < 32, pltpu.roll(v, 96, 1), pltpu.roll(v, 32, 1))
    return v * cosine + swapped * sine


def project_kernel(parts, where, x, bias, *refs):
    pieces = refs[:10]
    tables = refs[10:-3]
    out, wbuf, sems = refs[-3:]
    width = x.shape[1]
    copies = [
        assemble(where, pieces, wbuf.at[i], sems.at[i], (i * width, width)) for i in range(parts)
    ]
    for i in range(parts):
        wait_all(copies[i])
        for c in range(0, width, 512):
            y = dot(x[...], wbuf[i, :, :, :, c : c + 512].reshape(width, 512))
            y = y + bias[:, i * width + c : i * width + c + 512]
            at = i * width + c
            if tables:
                cosine, sine = tables[0][...], tables[1][...]
                for b in range(0, 512, LANES):
                    z = turn(y[:, b : b + LANES], cosine, sine)
                    z = z * 0.125 if i == 0 else z
                    out[:, at + b : at + b + LANES] = z.astype(BF16)
            else:
                out[:, at : at + 512] = y.astype(BF16)


def project(where, x, pieces, parts, bias, tables=()):
    t, width = x.shape
    r = pieces[0].shape[1]
    return pl.pallas_call(
        functools.partial(project_kernel, parts),
        in_specs=[smem_spec(), whole_spec(), whole_spec()]
        + [hbm_spec()] * 10
        + [whole_spec()] * len(tables),
        out_specs=whole_spec(),
        out_shape=shape((t, parts * width), BF16),
        scratch_shapes=[
            pltpu.VMEM((parts, 16, 2, r, width), BF16),
            pltpu.SemaphoreType.DMA((parts, 32)),
        ],
        compiler_params=params(),
        cost_estimate=cost(2 * t * width * parts * width, 2 * parts * width * width),
        name="project",
    )(where, x, bias, *pieces, *tables)


def open_mask(col_ref, row_ref, open_ref):
    t = open_ref.shape[0]

    @pl.when(pl.program_id(0) == 0)
    def _():
        rows = lax.broadcasted_iota(I32, (t, t), 0)
        cols = lax.broadcasted_iota(I32, (t, t), 1)
        ok = (col_ref[...] == row_ref[...]) & (cols <= rows)
        open_ref[...] = jnp.where(ok, 0.0, -1e30)


def one_head(v, h):
    lane = lax.broadcasted_iota(I32, v.shape, 1)
    return jnp.where((lane < HEAD) == (h == 0), v, jnp.zeros_like(v))


def attend_kernel(q_ref, k_ref, v_ref, col_ref, row_ref, out_ref, lse_ref, open_ref):
    t = q_ref.shape[0]
    tile = TILE
    open_mask(col_ref, row_ref, open_ref)
    left = lax.broadcasted_iota(I32, (tile, LANES), 1) < HEAD
    spans = [(slice(i * tile, (i + 1) * tile), (i + 1) * tile) for i in range(t // tile)]
    pairs = [(rows, seen, h) for rows, seen in spans for h in range(2)]
    scores = [
        dot_t(one_head(q_ref[rows, :], h), k_ref[:seen, :]) + open_ref[rows, :seen]
        for rows, seen, h in pairs
    ]
    peaks = [jnp.max(s, axis=-1, keepdims=True) for s in scores]
    powers = [jnp.exp(s - peak) for s, peak in zip(scores, peaks)]
    totals = [jnp.sum(e, axis=-1, keepdims=True) for e in powers]
    outs = [
        dot(e.astype(BF16), v_ref[:seen, :]) / total
        for e, total, (rows, seen, h) in zip(powers, totals, pairs)
    ]
    sums = [peak + jnp.log(total) for peak, total in zip(peaks, totals)]
    for i, (rows, seen) in enumerate(spans):
        out_ref[rows, :] = jnp.where(left, outs[2 * i], outs[2 * i + 1]).astype(BF16)
        lse_ref[rows, :] = jnp.where(left, sums[2 * i], sums[2 * i + 1])


def attend(qk, v, col, row):
    t, width = v.shape
    steps = width // LANES
    block = lambda f: pl.BlockSpec((t, LANES), f)
    return pl.pallas_call(
        attend_kernel,
        grid=(steps,),
        in_specs=[
            block(lambda i: (0, i)),
            block(lambda i: (0, i + steps)),
            block(lambda i: (0, i)),
            pl.BlockSpec((t, 1), lambda i: (0, 0)),
            pl.BlockSpec((1, t), lambda i: (0, 0)),
        ],
        out_specs=[block(lambda i: (0, i))] * 2,
        out_shape=[shape((t, width), BF16), shape((t, width), F32)],
        scratch_shapes=[pltpu.VMEM((t, t), F32)],
        compiler_params=params(),
        cost_estimate=cost(4 * t * t * width, 10 * t * width),
        name="attend",
    )(qk, qk, v, col, row)


def attend_back_kernel(
    q_ref, k_ref, v_ref, dm_ref, lse_ref, col_ref, row_ref, cos_ref, sin_ref,
    d_ref, sum_ref, open_ref,
):
    t = q_ref.shape[0]
    tile = TILE
    open_mask(col_ref, row_ref, open_ref)
    left = lax.broadcasted_iota(I32, (tile, LANES), 1) < HEAD
    spans = [(slice(i * tile, (i + 1) * tile), (i + 1) * tile) for i in range(t // tile)]
    pairs = [(rows, seen, h) for rows, seen in spans for h in range(2)]
    scores = [
        dot_t(one_head(q_ref[rows, :], h), k_ref[:seen, :]) + open_ref[rows, :seen]
        for rows, seen, h in pairs
    ]
    d_probs = [dot_t(one_head(dm_ref[rows, :], h), v_ref[:seen, :]) for rows, seen, h in pairs]
    probs = [
        jnp.exp(s - lse_ref[rows, h * HEAD : h * HEAD + 1])
        for s, (rows, seen, h) in zip(scores, pairs)
    ]
    deltas = [jnp.sum(p * dp, axis=-1, keepdims=True) for p, dp in zip(probs, d_probs)]
    d_scores = [(p * (dp - d)).astype(BF16) for p, dp, d in zip(probs, d_probs, deltas)]
    probs = [p.astype(BF16) for p in probs]
    dq = [dot(ds, k_ref[:seen, :]) for ds, (rows, seen, h) in zip(d_scores, pairs)]
    total_q = jnp.zeros((1, LANES), F32)
    for i, (rows, seen) in enumerate(spans):
        v = jnp.where(left, dq[2 * i], dq[2 * i + 1]) * 0.125
        v = turn(v, cos_ref[rows, :], -sin_ref[rows, :]).astype(BF16)
        d_ref[0, rows, :] = v
        total_q += row_sum(v.astype(F32))
    totals = [total_q]
    for at, lhs, rhs in ((1, d_scores, q_ref), (2, probs, dm_ref)):
        total = jnp.zeros((1, LANES), F32)
        parts = [t_dot(a, rhs[rows, :]) for a, (rows, seen, h) in zip(lhs, pairs)]
        for i, (keys, _) in enumerate(spans):
            heads = [
                sum(parts[2 * j + h][keys] for j in range(i, len(spans))) for h in range(2)
            ]
            v = jnp.where(left, heads[0], heads[1])
            if at == 1:
                v = turn(v, cos_ref[keys, :], -sin_ref[keys, :])
            v = v.astype(BF16)
            d_ref[at, keys, :] = v
            total += row_sum(v.astype(F32))
        totals.append(total)
    sum_ref[...] = place_rows(0, totals)


def attend_back(qk, v, dm, lse, col, row, cosine, sine, first, steps):
    t, width = v.shape
    key = width // LANES
    part = steps * LANES
    block = lambda f: pl.BlockSpec((t, LANES), f)
    fixed = lambda a: pl.BlockSpec(a.shape, lambda i: (0, 0))
    here = block(lambda i: (0, i))
    read = block(lambda i: (0, i + first))
    return pl.pallas_call(
        attend_back_kernel,
        grid=(steps,),
        in_specs=[read, block(lambda i: (0, i + first + key)), read, read, read]
        + [fixed(a) for a in (col, row, cosine, sine)],
        out_specs=[
            pl.BlockSpec((3, t, LANES), lambda i: (0, 0, i)),
            pl.BlockSpec((8, LANES), lambda i: (0, i)),
        ],
        out_shape=[shape((3, t, part), BF16), shape((8, part), F32)],
        scratch_shapes=[pltpu.VMEM((t, t), F32)],
        compiler_params=params(),
        cost_estimate=cost(10 * t * t * part, 18 * t * part),
        name="attend_back",
    )(qk, qk, v, dm, lse, col, row, cosine, sine)


def out_kernel(where, mixed, order, x, bias, g2, g3, *refs):
    pieces = refs[:10]
    m_own, m_sib, att_ref, mid_ref, n_ref, n_own, n_sib, wbuf, sems = refs[10:]
    t, width = mixed.shape
    half = width // 2
    copies = assemble(where, pieces, wbuf, sems, (width, width))
    turned = dot_t(order[...], mixed[...]).astype(BF16)
    m_own[...] = turned[:half]
    m_sib[...] = turned[half:]
    wait_all(copies)
    w = matrix(wbuf)
    tile = 256
    for i in range(t // tile):
        rows = slice(i * tile, (i + 1) * tile)
        att = dot(mixed[rows, :], w) + bias[...]
        att_ref[rows, :] = att
        mid = x[rows, :].astype(F32) + att * inverse_rms(att) * g2[...]
        mid_ref[rows, :] = mid
        n_ref[rows, :] = (mid * inverse_rms(mid) * g3[...]).astype(BF16)
    turned = dot_t(order[...], n_ref[...]).astype(BF16)
    n_own[...] = turned[:half]
    n_sib[...] = turned[half:]


def out_project(where, mixed, order, x, bias, g2, g3, pieces):
    t, width = mixed.shape
    half = width // 2
    r = pieces[0].shape[1]
    halves = [shape((half, t), BF16)] * 2
    return pl.pallas_call(
        out_kernel,
        in_specs=[smem_spec()] + [whole_spec()] * 6 + [hbm_spec()] * 10,
        out_specs=[whole_spec()] * 7,
        out_shape=halves + [shape((t, width), F32)] * 2 + [shape((t, width), BF16)] + halves,
        scratch_shapes=[pltpu.VMEM((16, 2, r, width), BF16), pltpu.SemaphoreType.DMA((32,))],
        compiler_params=params(),
        cost_estimate=cost(6 * t * width * width, 16 * t * width),
        name="out_project",
    )(where, mixed, order, x, bias, g2, g3, *pieces)


def up_kernel(where, x, bias, w_ref, a_own, a_sib, slope_ref):
    first = where[1] == 0
    width = x.shape[1]
    for j in range(w_ref.shape[3] // 256):
        cols = slice(j * 256, (j + 1) * 256)
        y = dot(x[...], w_ref[:, 0, :, cols].reshape(width, 256)) + bias[:, cols]
        yy = y * y
        h = 0.5 * jnp.tanh(y * (GELU_A + (GELU_A * GELU_B) * yy)) + 0.5
        act = y * h
        slope = h + act * (1.0 - h) * (2 * GELU_A + (6 * GELU_A * GELU_B) * yy)
        act = act.astype(BF16)
        slope_ref[:, cols] = slope.astype(BF16)
        dst = slice(j * 128, (j + 1) * 128)
        a0, a1 = act[:, :128], act[:, 128:]
        a_own[:, dst] = jnp.where(first, a0, a1)
        a_sib[:, dst] = jnp.where(first, a1, a0)


def up_project(where, x, bias, ffn):
    t, width = x.shape
    hidden = bias.shape[1]
    tn = UP_TILE
    per = ffn.shape[3] // tn
    return pl.pallas_call(
        up_kernel,
        grid=(hidden // tn,),
        in_specs=[
            smem_spec(),
            pl.BlockSpec((t, width), lambda i: (0, 0)),
            pl.BlockSpec((1, tn), lambda i: (0, i)),
            pl.BlockSpec((ffn.shape[0], 1, ffn.shape[2], tn), lambda i: (0, i // per, 0, i % per)),
        ],
        out_specs=[pl.BlockSpec((t, tn // 2), lambda i: (0, i))] * 2
        + [pl.BlockSpec((t, tn), lambda i: (0, i))],
        out_shape=[shape((t, hidden // 2), BF16)] * 2 + [shape((t, hidden), BF16)],
        compiler_params=params(),
        cost_estimate=cost(2 * t * width * hidden, 2 * width * hidden + 4 * t * hidden),
        name="up_project",
    )(where, x, bias, ffn)


def block_at(ref, where, place):
    chip = where[0] ^ pair_mask(place)
    return ref.at[:, pl.ds(pl.multiple_of(chip * LANES, LANES), LANES)]


def down_kernel(
    where, a_own, a_sib, w_own, w_sib, bias, valid, g4, mid_hbm, cot_hbm,
    out_ref, dc_ref, sums_ref, power_ref, acc, mid, cot, sems,
):
    step = pl.program_id(0)
    t, width = acc.shape
    copies = [
        pltpu.make_async_copy(mid_hbm, mid, sems.at[0]),
        pltpu.make_async_copy(cot_hbm, cot, sems.at[1]),
    ]
    w = jnp.concatenate([w_own[...].reshape(-1, width), w_sib[...].reshape(-1, width)], axis=0)
    y = dot(jnp.concatenate([a_own[...], a_sib[...]], axis=1), w)

    @pl.when(step == 0)
    def _():
        for copy in copies:
            copy.start()
        acc[...] = y + bias[...]

    @pl.when(step > 0)
    def _():
        acc[...] += y

    @pl.when(step == pl.num_programs(0) - 1)
    def _():
        wait_all(copies)
        tile = 128
        power = jnp.zeros((1, 1), F32)
        gain_sum = jnp.zeros((1, width), F32)
        bias_sum = jnp.zeros((1, width), F32)
        gain = g4[...]
        for i in range(t // tile):
            rows = slice(i * tile, (i + 1) * tile)
            v = acc[rows, :]
            ok = valid[rows, :]
            mean = jnp.mean(v * v, axis=-1, keepdims=True)
            power += row_sum(mean * ok)
            r = lax.rsqrt(mean + EPS)
            vr = v * r
            out_ref[rows, :] = (mid[rows, :] + vr * gain).astype(BF16)
            seed = cot[rows, :].astype(F32) * ok
            gain_sum += row_sum(vr * seed)
            dc = rms_back(v, r, gain, seed).astype(BF16)
            dc_ref[rows, :] = dc
            bias_sum += row_sum(dc.astype(F32))
        sums_ref[...] = place_rows(6, [gain_sum, bias_sum])
        power_ref[...] = jnp.broadcast_to(power, power_ref.shape)


def down_project(where, a_own, a_sib, bias, mid, cot, valid, g4, ffn):
    t, width = mid.shape
    hidden = 2 * a_own.shape[1]
    r = ffn.shape[3]
    fixed = lambda a: pl.BlockSpec(a.shape, lambda i, w: (0, 0))
    weights = [
        pl.BlockSpec((4, 1, 4, r, width), lambda i, w, e=e: (i, w[1] ^ e, 1, 0, 0)) for e in range(2)
    ]
    out = pl.BlockSpec((t, width), lambda i, w: (0, 0))
    return pl.pallas_call(
        down_kernel,
        grid_spec=pltpu.PrefetchScalarGridSpec(
            num_scalar_prefetch=1,
            grid=(4,),
            in_specs=[pl.BlockSpec((t, 512), lambda i, w: (0, i))] * 2
            + weights
            + [fixed(bias), fixed(valid), fixed(g4), hbm_spec(), hbm_spec()],
            out_specs=[out, out]
            + [pl.BlockSpec((8, width), lambda i, w: (0, 0)), pl.BlockSpec((1, LANES), lambda i, w: (0, 0))],
            scratch_shapes=[
                pltpu.VMEM((t, width), F32),
                pltpu.VMEM((t, width), F32),
                pltpu.VMEM((t, width), BF16),
                pltpu.SemaphoreType.DMA((2,)),
            ],
        ),
        out_shape=[shape((t, width), BF16)] * 2 + [shape((8, width), F32), shape((1, LANES), F32)],
        compiler_params=params(),
        cost_estimate=cost(2 * t * hidden * width, 2 * hidden * width + 10 * t * width),
        name="down_project",
    )(where, a_own, a_sib, ffn, ffn, bias, valid, g4, mid, cot)


def down_back_kernel(dc, slope, w_ref, de_ref, sums_ref):
    width = dc.shape[1]
    for j in range(w_ref.shape[0]):
        cols = slice(j * 256, (j + 1) * 256)
        y = dot_t(dc[...], w_ref[j].reshape(256, width))
        d = (y * slope[:, cols].astype(F32)).astype(BF16)
        de_ref[:, cols] = d
        sums_ref[:, cols] = row_sum(d.astype(F32))


def down_back(dc, slope, ffn):
    t, width = dc.shape
    hidden = slope.shape[1]
    r = ffn.shape[3]
    chips = DOWN_CHIPS
    tn = chips * 256
    return pl.pallas_call(
        down_back_kernel,
        grid=(hidden // tn,),
        in_specs=[
            pl.BlockSpec((t, width), lambda i: (0, 0)),
            pl.BlockSpec((t, tn), lambda i: (0, i)),
            pl.BlockSpec((chips, 2, 4, r, width), lambda i: (i, 0, 1, 0, 0)),
        ],
        out_specs=[pl.BlockSpec((t, tn), lambda i: (0, i)), pl.BlockSpec((1, tn), lambda i: (0, i))],
        out_shape=[shape((t, hidden), BF16), shape((1, hidden), F32)],
        compiler_params=params(),
        cost_estimate=cost(2 * t * hidden * width, 2 * hidden * width),
        name="down_back",
    )(dc, slope, ffn)


GRAD_PLACES = {
    "d23": (14, 15),
    "d01": (12, 13),
    "x01": (4, 5),
    "y23": (10, 11),
    "x23": (6, 7),
    "y01": (8, 9),
    "f": (0, 1, 2, 3),
}


def runs_of(places):
    return [(at, places[at : at + 2]) for at in range(0, len(places), 2)]


def slope_kernel(parts, x_own, x_oth, *refs):
    dy_own, dy_oth = refs[:parts], refs[parts : 2 * parts]
    outs = refs[2 * parts :]
    for i in range(parts):
        n = dy_own[i].shape[1]
        y = dot(x_own[...], dy_own[i][...]) + dot(x_oth[...], dy_oth[i][...])
        y = y.astype(BF16)
        for places, out in zip(GRAD_PLACES.values(), outs):
            r = out.shape[1]
            for at, run in runs_of(places):
                part = y[run[0] * r : (run[-1] + 1) * r]
                out[at : at + 2, :, i * n : (i + 1) * n] = part.reshape(2, r, n)


def row_slopes(x_own, x_oth, dy_own, dy_oth, tiles, first=0):
    half, t = x_own.shape
    r = half // 16
    n = dy_own.shape[1] // tiles
    total = n * (first + tiles)
    fixed = pl.BlockSpec((half, t), lambda i: (0, 0))
    return pl.pallas_call(
        functools.partial(slope_kernel, 1),
        grid=(tiles,),
        in_specs=[fixed] * 2 + [pl.BlockSpec((t, n), lambda i: (0, i))] * 2,
        out_specs=[pl.BlockSpec((len(p), r, n), lambda i: (0, 0, i + first)) for p in GRAD_PLACES.values()],
        out_shape=[shape((len(p), r, total), BF16) for p in GRAD_PLACES.values()],
        compiler_params=params(),
        cost_estimate=cost(4 * t * half * n * tiles, 8 * t * n * tiles + 2 * half * n * tiles),
        name="row_slopes",
    )(x_own, x_oth, dy_own, dy_oth)


def qkv_slope_kernel(x_own, x_oth, a_own, b_own, a_oth, b_oth, *refs):
    outs = refs[len(GRAD_PLACES) :]
    n = a_own.shape[2]
    for i, (own, oth) in enumerate(((a_own, a_oth), (b_own, b_oth))):
        y = dot(x_own[...], own[0]) + dot(x_oth[...], oth[0])
        y = y.astype(BF16)
        for places, out in zip(GRAD_PLACES.values(), outs):
            r = out.shape[1]
            for at, run in runs_of(places):
                part = y[run[0] * r : (run[-1] + 1) * r]
                out[at : at + 2, :, i * n : (i + 1) * n] = part.reshape(2, r, n)


def qkv_slopes(x_own, x_oth, a_own, b_own, a_oth, b_oth, pieces):
    half, t = x_own.shape
    r = half // 16
    n = a_own.shape[2]
    fixed = pl.BlockSpec((half, t), lambda i: (0, 0))
    return pl.pallas_call(
        qkv_slope_kernel,
        grid=(3,),
        in_specs=[fixed] * 2
        + [pl.BlockSpec((1, t, n), lambda i: (i, 0, 0))] * 4
        + [hbm_spec()] * len(pieces),
        out_specs=[pl.BlockSpec((len(p), r, 2 * n), lambda i: (0, 0, i)) for p in GRAD_PLACES.values()],
        out_shape=[shape(p.shape, BF16) for p in pieces],
        input_output_aliases={6 + i: i for i in range(len(pieces))},
        compiler_params=params(),
        cost_estimate=cost(24 * t * half * n, 24 * t * n + 12 * half * n),
        name="qkv_slopes",
    )(x_own, x_oth, a_own, b_own, a_oth, b_oth, *pieces)


def block_slope_kernel(where, a_own, a_oth, dy_own, dy_oth, *refs):
    outs = refs[:7]
    stage, sems = refs[7:]
    sent = []
    for places, out in zip(GRAD_PLACES.values(), outs):
        for at, run in runs_of(places):
            i = len(sent)
            mine, other = (
                jnp.concatenate([block_at(act, where, p)[...] for p in run], axis=1)
                for act in (a_own, a_oth)
            )
            y = t_dot(mine, dy_own[...]) + t_dot(other, dy_oth[...])
            stage[i] = y.astype(BF16).reshape(2, LANES, y.shape[1])
            copy = pltpu.make_async_copy(stage.at[i], out.at[pl.ds(at, 2)], sems.at[i])
            copy.start()
            sent.append(copy)
    wait_all(sent)


def block_slopes(where, a_own, a_oth, dy_own, dy_oth):
    t, half = a_own.shape
    width = dy_own.shape[1]
    return pl.pallas_call(
        block_slope_kernel,
        in_specs=[smem_spec()] + [whole_spec()] * 4,
        out_specs=[hbm_spec()] * 7,
        out_shape=[shape((len(p), LANES, width), BF16) for p in GRAD_PLACES.values()],
        scratch_shapes=[pltpu.VMEM((8, 2, LANES, width), BF16), pltpu.SemaphoreType.DMA((8,))],
        compiler_params=params(),
        cost_estimate=cost(4 * t * half * width, 4 * t * (half + width) + 2 * half * width),
        name="block_slopes",
    )(where, a_own, a_oth, dy_own, dy_oth)


def up_back_kernel(where, de, valid, g2_ref, g3_ref, w_ref, mid_hbm, att_hbm, cot_hbm, *refs):
    pieces = refs[:10]
    dmid_ref, datt_ref, dmix_ref, sums_ref, acc, wbuf, mid_buf, att_buf, cot_buf, sems = refs[10:]
    step = pl.program_id(0)
    t, width = acc.shape

    @pl.when(step == 0)
    def _():
        assemble(where, pieces, wbuf, sems, (width, width))
        fetch((mid_hbm, att_hbm, cot_hbm), (mid_buf, att_buf, cot_buf), sems, 32)

    y = dot_t(de[...], w_ref[:, 0].reshape(width, -1))

    @pl.when(step == 0)
    def _():
        acc[...] = y

    @pl.when(step > 0)
    def _():
        acc[...] += y

    @pl.when(step == pl.num_programs(0) - 1)
    def _():
        for i in range(32):
            pltpu.make_async_copy(pieces[0].at[0, :, pl.ds(width, width)], wbuf.at[0, 0], sems.at[i]).wait()
        for i, (a, b) in enumerate(((mid_hbm, mid_buf), (att_hbm, att_buf), (cot_hbm, cot_buf))):
            pltpu.make_async_copy(a, b, sems.at[32 + i]).wait()
        tile = 128
        g2, g3 = g2_ref[...], g3_ref[...]
        w = matrix(wbuf)
        sums = [jnp.zeros((1, width), F32)] * 3
        for i in range(t // tile):
            rows = slice(i * tile, (i + 1) * tile)
            e = acc[rows, :]
            mid = mid_buf[rows, :]
            r3 = inverse_rms(mid)
            dmid = cot_buf[rows, :].astype(F32) * valid[rows, :] + rms_back(mid, r3, g3, e)
            dmid_ref[rows, :] = dmid
            att = att_buf[rows, :]
            r2 = inverse_rms(att)
            datt = rms_back(att, r2, g2, dmid).astype(BF16)
            datt_ref[rows, :] = datt
            sums[0] += row_sum(mid * r3 * e)
            sums[1] += row_sum(att * r2 * dmid)
            sums[2] += row_sum(datt.astype(F32))
        dmix_ref[...] = dot_t(datt_ref[...], w).astype(BF16)
        sums_ref[...] = place_rows(3, sums)


def up_back(where, de, mid, att, cot, valid, g2, g3, ffn, pieces):
    t, width = mid.shape
    hidden = de.shape[1]
    tk = ffn.shape[3]
    r = pieces[0].shape[1]
    fixed = lambda a: pl.BlockSpec(a.shape, lambda i: (0, 0))
    return pl.pallas_call(
        up_back_kernel,
        grid=(hidden // tk,),
        in_specs=[smem_spec(), pl.BlockSpec((t, tk), lambda i: (0, i))]
        + [fixed(a) for a in (valid, g2, g3)]
        + [pl.BlockSpec((ffn.shape[0], 1, ffn.shape[2], tk), lambda i: (0, i, 0, 0))]
        + [hbm_spec()] * 13,
        out_specs=[pl.BlockSpec((t, width), lambda i: (0, 0))] * 3
        + [pl.BlockSpec((8, width), lambda i: (0, 0))],
        out_shape=[shape((t, width), F32), shape((t, width), BF16), shape((t, width), BF16), shape((8, width), F32)],
        scratch_shapes=[
            pltpu.VMEM((t, width), F32),
            pltpu.VMEM((16, 2, r, width), BF16),
            pltpu.VMEM((t, width), F32),
            pltpu.VMEM((t, width), F32),
            pltpu.VMEM((t, width), BF16),
            pltpu.SemaphoreType.DMA((35,)),
        ],
        compiler_params=params(),
        cost_estimate=cost(2 * t * width * hidden, 2 * width * hidden + 2 * t * hidden),
        name="up_back",
    )(where, de, valid, g2, g3, ffn, mid, att, cot, *pieces)


def in_back_kernel(where, *refs):
    d_a, d_b, x_hbm, dmid_hbm, g1_ref = refs[:5]
    qk, vo = refs[5:15], refs[15:25]
    out_ref, sums_ref, wbuf, x_buf, dmid_buf, sems = refs[25:]
    t, width = out_ref.shape
    half = width // 2
    copies = [
        assemble(where, pieces, wbuf.at[i], sems.at[i], (start, width))
        for i, (pieces, start) in enumerate(((qk, 0), (qk, width), (vo, 0)))
    ]
    late = fetch((x_hbm, dmid_hbm), (x_buf, dmid_buf), sems.at[3])
    e = None
    for i in range(3):
        wait_all(copies[i])
        d = jnp.concatenate([d_a[i], d_b[i]], axis=1)
        y = dot_t(d, wbuf[i].reshape(width, width))
        e = y if e is None else e + y
    wait_all(late)
    gain = g1_ref[...]
    tile = 128
    total = jnp.zeros((1, width), F32)
    for i in range(t // tile):
        rows = slice(i * tile, (i + 1) * tile)
        x = x_buf[rows, :].astype(F32)
        r = inverse_rms(x)
        out_ref[rows, :] = dmid_buf[rows, :] + rms_back(x, r, gain, e[rows, :])
        total += row_sum(x * r * e[rows, :])
    sums_ref[...] = total


def in_back(where, d_a, d_b, x, dmid, g1, qk_pieces, vo_pieces):
    t, width = x.shape
    r = qk_pieces[0].shape[1]
    return pl.pallas_call(
        in_back_kernel,
        in_specs=[smem_spec()] + [whole_spec()] * 2 + [hbm_spec()] * 2 + [whole_spec()] + [hbm_spec()] * 20,
        out_specs=[whole_spec()] * 2,
        out_shape=[shape((t, width), F32), shape((1, width), F32)],
        scratch_shapes=[
            pltpu.VMEM((3, 16, 2, r, width), BF16),
            pltpu.VMEM((t, width), BF16),
            pltpu.VMEM((t, width), F32),
            pltpu.SemaphoreType.DMA((4, 32)),
        ],
        compiler_params=params(),
        cost_estimate=cost(6 * t * width * width, 6 * width * width),
        name="in_back",
    )(where, d_a, d_b, x, dmid, g1, *qk_pieces, *vo_pieces)


def after(*values):
    return lax.optimization_barrier(values)


def add(*values):
    total = values[0].astype(F32)
    for v in values[1:]:
        total = total + v.astype(F32)
    return total


class Gather:
    def __init__(self, net, shard):
        self.net = net
        self.line = [shard] + [net.swap(shard, 4 * m) for m in (1, 2, 3)]

    def spread(self, line):
        net = self.net
        self.lines = jnp.stack(line)
        self.x = net.swap(self.lines, 1)
        self.y = net.swap(self.lines, 2)
        self.sib = [net.sibling(self.lines)]

    def corner(self, x, y):
        net = self.net
        self.x, self.y = x, y
        self.d01 = net.swap(x[:2], 2)
        self.d23 = net.swap(y[2:], 1)
        self.sib += [net.sibling(x), net.sibling(y)]

    def finish(self, d01, d23):
        net = self.net
        self.d01, self.d23 = d01, d23
        self.sib += [net.sibling(d01), net.sibling(d23)]

    def pieces(self):
        return [self.lines, self.x, self.y, self.d01, self.d23] + self.sib


class Scatter:
    def __init__(self, net, pieces):
        self.net = net
        self.d23, self.d01, self.x01, self.y23, self.x23, self.y01, self.f = pieces

    def a(self):
        self.got = [self.net.swap(self.d23, 1), self.net.swap(self.d01, 2)]

    def c(self, x23, y01):
        self.last = [self.net.swap(x23, 1), self.net.swap(y01, 2)]

    def fold_b(self, got):
        return [add(self.x01, got[1]).astype(BF16), add(self.y23, got[0]).astype(BF16)]

    def b(self, fold):
        self.got = [self.net.swap(fold[0], 1), self.net.swap(fold[1], 2)]

    def fold_last(self, last):
        return [add(self.f[:2], last[1]), add(self.f[2:], last[0])]

    def fold_near(self, got, part):
        low, high = add(part[0], got[0]), add(part[1], got[1])
        return [low[0], high[0], jnp.stack([low[1], high[1]]).astype(BF16)]

    def near(self, fold):
        self.low, self.high, send = fold
        self.got = [self.net.swap(send, 4)]

    def fold_far(self, got):
        return [add(self.low, got[0][0]), add(self.high, got[0][1]).astype(BF16)]

    def far(self, fold):
        self.own, send = fold
        self.got = [self.net.swap(send, 8)]

    def result(self, got):
        return add(self.own, got[0])


def shards_16(
    activations,
    segment_ids,
    cotangent,
    querymat,
    keymat,
    valuemat,
    outmat,
    upmatrix,
    downmatrix,
    querybias,
    keybias,
    valuebias,
    outbias,
    upbias,
    downbias,
    firstgain,
    secondgain,
    thirdgain,
    fourthgain,
):
    net = Net(16)
    t, width = activations.shape
    rows = querymat.shape[0]
    hidden = upmatrix.shape[1]
    block = upbias.shape[0]
    half = width // 2
    me, core = net.me, net.core
    device = me * 2 + core
    where = jnp.stack([me, core]).astype(I32)

    dst = jnp.arange(width)
    place = (dst // rows) % 16
    chip = me ^ (place // 4 + 4 * (place % 4))
    src = chip * (2 * rows) + (core ^ (dst // half)) * rows + dst % rows
    order = (src[:, None] == jnp.arange(width)[None, :]).astype(BF16)
    slots = jnp.arange(t)
    segment = jnp.where(segment_ids >= 0, segment_ids, -1 - slots)
    col, row = segment[:, None], segment[None, :]
    valid = (segment_ids >= 0).astype(F32)[:, None]
    spots = positions_of(segment_ids).astype(F32)
    inverse = 10000.0 ** (-jnp.arange(HEAD // 2).astype(F32) * 2.0 / HEAD)
    angles = spots[:, None] * inverse[None, :]
    cosine = jnp.tile(jnp.cos(angles), (1, 4))
    sine = jnp.sin(angles)
    sine = jnp.tile(jnp.concatenate([-sine, sine], axis=1), (1, 2))

    ffn_shard = jnp.concatenate(
        [upmatrix.reshape(rows, 4, width).transpose(1, 0, 2), downmatrix.reshape(4, rows, width)]
    )
    ffn = lax.all_gather(ffn_shard, AXES, axis=0, tiled=False)
    qk = Gather(net, jnp.concatenate([querymat, keymat], axis=1))
    vo_shard = jnp.concatenate([valuemat, outmat], axis=1)
    nine = [querybias, keybias, valuebias, outbias, downbias, firstgain, secondgain, thirdgain, fourthgain]
    small = jnp.concatenate([jnp.pad(v[None], ((0, 0), (0, LANES - rows))) for v in nine] + [upbias[None]])
    buf = small[None]
    buf = jnp.concatenate([buf, net.sibling(buf)])
    for mask in (1, 2, 4, 8):
        buf = jnp.concatenate([buf, net.swap(buf, mask)])
    line, buf, vo_shard = after(qk.line, buf, vo_shard)
    qk.spread(line)
    vo = Gather(net, vo_shard)

    picks = (jnp.arange(32)[:, None] ^ device) == jnp.arange(32)[None, :]
    small_all = dot(picks.astype(BF16), buf.reshape(32, -1)).reshape(32, 10, LANES)
    b_q, b_k, b_v, b_o, b_d, g1, g2, g3, g4 = (
        small_all[:, i, :rows].reshape(1, width) for i in range(9)
    )
    b_up = small_all[:, 9].reshape(1, hidden)
    inputs = activations.astype(F32)
    normed = (inputs * inverse_rms(inputs) * g1).astype(BF16)
    turned = dot_t(order, normed).astype(BF16)
    x_own, x_sib = turned[:half], turned[half:]

    x, y, line = after(qk.x, qk.y, vo.line)
    qk.corner(x, y)
    vo.spread(line)
    d01, d23, x_sib, normed, tables, vectors = after(
        qk.d01,
        qk.d23,
        x_sib,
        normed,
        (cosine, sine, col, row, valid, order),
        (b_q, b_k, b_v, b_o, b_d, g2, g3, g4, b_up),
    )
    cosine, sine, col, row, valid, order = tables
    b_q, b_k, b_v, b_o, b_d, g2, g3, g4, b_up = vectors
    qk.finish(d01, d23)
    x_oth = net.sibling(x_sib)
    x, y = after(vo.x, vo.y)
    vo.corner(x, y)
    qk_pieces = qk.pieces()
    qk_rot = project(where, normed, qk_pieces, 2, jnp.concatenate([b_q, b_k], axis=1), (cosine, sine))
    d01, d23, qk_rot = after(vo.d01, vo.d23, qk_rot)
    vo.finish(d01, d23)
    vo_pieces = vo.pieces()
    v = project(where, normed, vo_pieces, 1, b_v)
    mixed, lse = attend(qk_rot, v, col, row)
    m_own, m_sib, att, mid, normed_mid, n_own, n_sib = out_project(
        where, mixed, order, activations, b_o, g2, g3, vo_pieces
    )
    m_oth = net.sibling(m_sib)
    n_oth = net.sibling(n_sib)
    a_own, a_sib, slope = up_project(where, normed_mid, b_up, ffn)
    a_oth = net.sibling(a_sib)
    ffn_down = ffn.reshape(16, 2, 8, rows, width)
    layer_out, dc, down_sums, power = down_project(
        where, a_own, a_sib, b_d, mid, cotangent, valid, g4, ffn_down
    )

    dc_oth = net.sibling(dc)
    dc, dc_oth, a_oth = after(dc, dc_oth, a_oth)
    slopes, dc = after(block_slopes(where, a_own, a_oth, dc, dc_oth), dc)

    down_sum = Scatter(net, slopes)
    down_sum.a()
    de, up_bias_sum = down_back(dc, slope, ffn_down)
    de, got, x23, y01 = after(de, down_sum.got, down_sum.x23, down_sum.y01)

    down_sum.c(x23, y01)
    fold = down_sum.fold_b(got)
    de_oth = net.sibling(de)
    back = up_back(where, de, mid, att, cotangent, valid, g2, g3, ffn, vo_pieces)
    back, de_oth, de, fold, last, n_own = after(back, de_oth, de, fold, down_sum.last, n_own)
    dmid, datt, dmix, mid_sums = back

    down_sum.b(fold)
    datt_oth = net.sibling(datt)
    slopes = row_slopes(n_own, n_oth, de, de_oth, 4)
    slopes, got, datt_oth, datt, dmix, last = after(slopes, down_sum.got, datt_oth, datt, dmix, last)

    up_sum = Scatter(net, slopes)
    up_sum.a()
    fold = down_sum.fold_near(got, down_sum.fold_last(last))
    steps = width // LANES // 2
    part_a = attend_back(qk_rot, v, dmix, lse, col, row, cosine, sine, 0, steps)
    part_a, dmix, up_got, fold, x23, y01 = after(
        part_a, dmix, up_sum.got, fold, up_sum.x23, up_sum.y01
    )
    d_a, sums_a = part_a

    up_sum.c(x23, y01)
    down_sum.near(fold)
    a_other = net.sibling(d_a)
    up_fold = up_sum.fold_b(up_got)
    part_b = attend_back(qk_rot, v, dmix, lse, col, row, cosine, sine, steps, steps)
    part_b, datt, up_fold, up_last, got, a_other, m_own = after(
        part_b, datt, up_fold, up_sum.last, down_sum.got, a_other, m_own
    )
    d_b, sums_b = part_b

    up_sum.b(up_fold)
    b_other = net.sibling(d_b)
    fold = down_sum.fold_far(got)
    slopes = row_slopes(m_own, m_oth, datt, datt_oth, 1, 3)
    slopes, b_other, d_a, d_b, a_other, fold = after(slopes, b_other, d_a, d_b, a_other, fold)

    down_sum.far(fold)
    part = up_sum.fold_last(up_last)
    slopes = qkv_slopes(x_own, x_oth, d_a, d_b, a_other, b_other, slopes)
    slopes, up_got, d_a, d_b, part = after(slopes, up_sum.got, d_a, d_b, part)

    att_sum = Scatter(net, slopes)
    att_sum.a()
    up_fold = up_sum.fold_near(up_got, part)
    input_gradient, first_sum = in_back(where, d_a, d_b, activations, dmid, g1, qk_pieces, vo_pieces)
    sums = jnp.concatenate([sums_a, sums_b], axis=1) + mid_sums + down_sums
    sums = jnp.concatenate(
        [
            sums,
            first_sum,
            up_bias_sum.reshape(4, width),
            jnp.pad(power, ((0, 2), (0, width - LANES))),
        ]
    )
    sums, got, up_fold, x23, y01, down_got = after(
        sums, att_sum.got, up_fold, att_sum.x23, att_sum.y01, down_sum.got
    )

    att_sum.c(x23, y01)
    up_sum.near(up_fold)
    down_total = down_sum.result(down_got)
    fold = att_sum.fold_b(got)
    sums = sums + net.sibling(sums)
    sums = sums + net.swap(sums, 1)
    fold, up_got, sums, last = after(fold, up_sum.got, sums, att_sum.last)

    att_sum.b(fold)
    up_sum.far(up_sum.fold_far(up_got))
    part = att_sum.fold_last(last)
    sums = sums + net.swap(sums, 2)
    sums = sums + net.swap(sums, 4)
    got, sums, up_got, part = after(att_sum.got, sums, up_sum.got, part)

    att_sum.near(att_sum.fold_near(got, part))
    up_total = up_sum.result(up_got)
    sums = sums + net.swap(sums, 8)
    own = lax.dynamic_slice_in_dim(sums[:9], device * rows, rows, 1)
    own_up = lax.dynamic_slice_in_dim(sums[9:13].reshape(-1), device * block, block, 0)
    got, own, own_up, power_sum = after(att_sum.got, own, own_up, sums[13, 0])

    att_sum.far(att_sum.fold_far(got))
    att_total = att_sum.result(att_sum.got)
    qkv_total = [att_total[:, i * width : (i + 1) * width] for i in range(3)]
    out_total = att_total[:, 3 * width :]

    output_power = power_sum / (t * 32)
    own = [own[i] for i in (0, 1, 2, 5, 7, 8, 4, 3, 6)]
    return (
        layer_out,
        input_gradient,
        *qkv_total,
        out_total,
        up_total,
        down_total,
        own[0],
        own[1],
        own[2],
        own[3],
        own_up,
        own[4],
        own[5],
        own[6],
        own[7],
        own[8],
        output_power,
    )


def shards(*args):
    rows, length = args[3].shape[0], args[0].shape[0]
    if lax.axis_size("wide") == 16 and rows == 32 and length == 512:
        return shards_16(*args)
    return shards_any(*args)


def solution(mesh):
    matrix = P(AXES, None)
    vector = P(AXES)
    return jax.shard_map(
        shards,
        mesh=mesh,
        in_specs=(matrix, vector, matrix) + (matrix,) * 6 + (vector,) * 10,
        out_specs=(matrix,) * 8 + (vector,) * 10 + (P(),),
        check_vma=False,
    )
```

```python
import jax
import jax.numpy as jnp
import functools

from jax import lax
from jax.experimental import pallas as pl
from jax.experimental.pallas import tpu as pltpu
from jax.sharding import PartitionSpec as P

HEAD = 64
AXES = ("wide", "narrow")


def rms_norm(values, gain):
    return values * lax.rsqrt(jnp.mean(values * values, axis=-1, keepdims=True) + 1e-06) * gain


def rotate(values, cosine, sine):
    midpoint = values.shape[-1] // 2
    first_half = values[..., :midpoint]
    second_half = values[..., midpoint:]
    return jnp.concatenate(
        [first_half * cosine - second_half * sine, first_half * sine + second_half * cosine],
        axis=-1,
    )


def positions_of(segment):
    places = jnp.arange(segment.shape[0])
    matching = segment[:, None] == segment[None, :]
    earlier = places[None, :] < places[:, None]
    return jnp.sum(jnp.logical_and(matching, earlier).astype(jnp.int32), axis=1)


def angle_tables(segment):
    places = positions_of(segment).astype(jnp.float32)
    midpoint = HEAD // 2
    inverse = 10000.0 ** (-jnp.arange(midpoint).astype(jnp.float32) * 2.0 / HEAD)
    angles = places[:, None] * inverse[None, :]
    return (jnp.cos(angles)[:, None, :], jnp.sin(angles)[:, None, :])


def key_mask(segment):
    places = jnp.arange(segment.shape[0])
    matching = segment[:, None] == segment[None, :]
    allowed = matching & (segment[None, :] >= 0) & (places[None, :] <= places[:, None])
    return allowed | (places[None, :] == places[:, None])


def contract_rows(left, right):
    return lax.dot_general(
        left, right, (((0,), (0,)), ((), ())), preferred_element_type=jnp.float32
    )


def times_transpose(left, right):
    return lax.dot_general(
        left, right, (((1,), (1,)), ((), ())), preferred_element_type=jnp.float32
    )


def product(left, right):
    return jnp.dot(left, right, preferred_element_type=jnp.float32)


def column_sums(values):
    return jnp.sum(values.astype(jnp.float32), axis=0)


def masked_scores(query_rot, key_rot, allowed):
    scores = (
        jnp.einsum("qhd,khd->hqk", query_rot, key_rot, preferred_element_type=jnp.float32) * 0.125
    )
    return jnp.where(allowed[None], scores, -1e30)


class Net:
    def __init__(self, wide):
        self.wide = wide
        self.me = lax.axis_index("wide")
        self.core = lax.axis_index("narrow")
        outer = []
        mask = wide // 2
        while mask > 2:
            outer.append(mask)
            mask //= 2
        self.outer = outer

    def swap(self, value, mask):
        pairs = [(d, d ^ mask) for d in range(self.wide)]
        return lax.ppermute(value, "wide", pairs)

    def sibling(self, value):
        return lax.ppermute(value, "narrow", [(0, 1), (1, 0)])

    def bit(self, mask):
        return (self.me & mask) != 0

    def grow(self, value, mask, axis):
        other = self.swap(value, mask)
        bit = self.bit(mask)
        low = jnp.where(bit, other, value)
        high = jnp.where(bit, value, other)
        return jnp.stack([low, high], axis=axis)

    def shrink(self, value, mask, axis):
        bit = self.bit(mask).astype(jnp.int32)
        mine = lax.dynamic_index_in_dim(value, bit, axis, keepdims=False)
        theirs = lax.dynamic_index_in_dim(value, 1 - bit, axis, keepdims=False)
        other = self.swap(theirs, mask)
        return (mine.astype(jnp.float32) + other.astype(jnp.float32)).astype(jnp.bfloat16)

    def gather(self, first, second):
        r, c = first.shape
        both = jnp.stack([first, second])[None]
        for mask in self.outer:
            both = self.grow(both, mask, 1).reshape(-1, 2, r, c)
        outer = both.shape[0]
        a = self.grow(both[:, 0], 1, 1)
        a = self.grow(a, 2, 1)
        b = self.grow(both[:, 1], 2, 1)
        b = self.grow(b, 1, 2)
        return jnp.stack([a, b], axis=3).reshape(outer * 4 * 2 * r, c)

    def scatter(self, full):
        rows, c = full.shape
        r = rows // (self.wide * 2)
        outer = self.wide // 4
        parts = full.reshape(outer, 2, 2, 2, r, c)
        a, b = parts[:, :, :, 0], parts[:, :, :, 1]
        a = self.shrink(self.shrink(a, 2, 1), 1, 1)
        b = self.shrink(self.shrink(b, 1, 2), 2, 1)
        both = jnp.stack([a, b], axis=1)
        for mask in reversed(self.outer):
            count = both.shape[0] // 2
            both = self.shrink(both.reshape(count, 2, 2, r, c), mask, 1)
        return both[0, 0], both[0, 1]

    def gather_small(self, value):
        other = self.sibling(value)
        core = self.core == 1
        buf = jnp.stack([jnp.where(core, other, value), jnp.where(core, value, other)])[None]
        for mask in [1, 2] + self.outer[::-1]:
            buf = self.grow(buf, mask, 0).reshape(1, -1, *value.shape)
        return buf[0]

    def total(self, value):
        value = value + self.sibling(value)
        for mask in [1, 2] + self.outer[::-1]:
            value = value + self.swap(value, mask)
        return value

    def pick(self, value, axis):
        mine = lax.dynamic_index_in_dim(value, self.core, axis, keepdims=False)
        theirs = lax.dynamic_index_in_dim(value, 1 - self.core, axis, keepdims=False)
        return mine, theirs

    def halves(self, mine, theirs):
        core = self.core == 1
        return jnp.where(core, theirs, mine), jnp.where(core, mine, theirs)

    def columns_in(self, shard):
        mine, theirs = self.pick(shard, 1)
        return self.halves(mine, self.sibling(theirs))

    def columns_out(self, first, second):
        mine, theirs = self.pick(jnp.stack([first, second]), 0)
        other = self.sibling(theirs)
        left, right = self.halves(mine, other)
        return jnp.stack([left, right], axis=1)


def shards_any(
    activations,
    segment_ids,
    cotangent,
    querymat,
    keymat,
    valuemat,
    outmat,
    upmatrix,
    downmatrix,
    querybias,
    keybias,
    valuebias,
    outbias,
    upbias,
    downbias,
    firstgain,
    secondgain,
    thirdgain,
    fourthgain,
):
    wide = lax.axis_size("wide")
    net = Net(wide)
    core = net.core
    length, width = activations.shape
    rows = querymat.shape[0]
    hidden = upmatrix.shape[1]
    block = hidden // (2 * wide)
    half = width // 2
    heads = width // HEAD
    f32 = jnp.float32
    bf16 = jnp.bfloat16

    nine = [querybias, keybias, valuebias, outbias, downbias, firstgain, secondgain, thirdgain, fourthgain]
    small = jnp.concatenate([jnp.concatenate(nine), upbias])
    qkv_shard = jnp.concatenate(
        [m.reshape(rows, 2, half) for m in (querymat, keymat, valuemat)], axis=2
    )
    up_shard = upmatrix.reshape(rows, wide, 2, block).transpose(0, 2, 1, 3).reshape(rows, 2, hidden // 2)
    out_shard = outmat.reshape(rows, 2, half)
    small_all = net.gather_small(small)
    qkv_mine = net.gather(*net.columns_in(qkv_shard))
    out_mine = net.gather(*net.columns_in(out_shard))
    up_mine = net.gather(*net.columns_in(up_shard))
    down_rows = downmatrix.shape[0]
    down_mine = net.gather(downmatrix[: down_rows // 2], downmatrix[down_rows // 2 :])
    qkv_theirs, out_theirs, up_theirs, down_theirs = map(
        net.sibling, (qkv_mine, out_mine, up_mine, down_mine)
    )

    vectors = small_all[:, : 9 * rows].reshape(-1, 9, rows).transpose(1, 0, 2).reshape(9, width)
    vectors = vectors.astype(f32)
    bias_query, bias_key, bias_value, bias_output, bias_down = (vectors[i] for i in range(5))
    gain_first, gain_second, gain_third, gain_fourth = (vectors[i] for i in range(5, 9))
    bias_up_pair = small_all[:, 9 * rows :].reshape(wide, 2, block).astype(f32)
    bias_up_mine, bias_up_theirs = (v.reshape(-1) for v in net.pick(bias_up_pair, 1))

    def natural(mine, theirs):
        return jnp.where(
            core == 1,
            jnp.concatenate([theirs, mine], axis=-1),
            jnp.concatenate([mine, theirs], axis=-1),
        )

    inputs = activations.astype(f32)
    cosine, sine = angle_tables(segment_ids)
    allowed = key_mask(segment_ids)
    valid_row = (segment_ids >= 0).astype(f32)
    normed_in, pull_first = jax.vjp(rms_norm, inputs, gain_first)
    normed_low = normed_in.astype(bf16)
    normed_low_theirs = net.sibling(normed_low)
    qkv_m = product(normed_low, qkv_mine)
    qkv_t = product(normed_low, qkv_theirs)
    queries, keys_pre, values_pre = (
        natural(qkv_m[:, i * half : (i + 1) * half], qkv_t[:, i * half : (i + 1) * half]) + b
        for i, b in enumerate((bias_query, bias_key, bias_value))
    )
    query_rot = rotate(queries.reshape(length, heads, HEAD), cosine, sine).astype(bf16)
    key_rot = rotate(keys_pre.reshape(length, heads, HEAD), cosine, sine).astype(bf16)
    value_low = values_pre.reshape(length, heads, HEAD).astype(bf16)
    scores = masked_scores(query_rot, key_rot, allowed)
    peak = jnp.max(scores, axis=-1, keepdims=True)
    exponent = jnp.exp(scores - peak)
    totals = jnp.sum(exponent, axis=-1, keepdims=True)
    logsum = peak + jnp.log(totals)
    probs = exponent / totals
    mixed = jnp.einsum(
        "hqk,khd->qhd", probs.astype(bf16), value_low, preferred_element_type=f32
    )
    mixed_low = mixed.reshape(length, width).astype(bf16)
    mixed_low_theirs = net.sibling(mixed_low)
    attended = natural(product(mixed_low, out_mine), product(mixed_low, out_theirs)) + bias_output
    normed_att, pull_second = jax.vjp(rms_norm, attended, gain_second)
    middle = inputs + normed_att
    normed_mid, pull_third = jax.vjp(rms_norm, middle, gain_third)
    normed_mid_low = normed_mid.astype(bf16)
    normed_mid_low_theirs = net.sibling(normed_mid_low)
    act_m_f, pull_gelu_m = jax.vjp(jax.nn.gelu, product(normed_mid_low, up_mine) + bias_up_mine)
    act_t_f, pull_gelu_t = jax.vjp(jax.nn.gelu, product(normed_mid_low, up_theirs) + bias_up_theirs)
    act_m = act_m_f.astype(bf16)
    act_t = act_t_f.astype(bf16)
    act_other = net.sibling(act_t)
    contracted = product(act_m, down_mine) + product(act_t, down_theirs) + bias_down
    local_power = jnp.sum(valid_row * jnp.mean(contracted * contracted, axis=-1))
    normed_out, pull_fourth = jax.vjp(rms_norm, contracted, gain_fourth)
    layer_out = (middle + normed_out).astype(bf16)

    seed = cotangent.astype(f32) * valid_row[:, None]
    d_contracted_f, fourth_slope = pull_fourth(seed)
    d_contracted = d_contracted_f.astype(bf16)
    d_contracted_theirs = net.sibling(d_contracted)
    down_bias_slope = column_sums(d_contracted)
    d_exp_m = pull_gelu_m(times_transpose(d_contracted, down_mine))[0].astype(bf16)
    d_exp_t = pull_gelu_t(times_transpose(d_contracted, down_theirs))[0].astype(bf16)
    d_exp_other = net.sibling(d_exp_t)

    def both_rows(a, b):
        return jnp.concatenate([a, b], axis=0)

    down_slope = contract_rows(
        both_rows(act_m, act_other), both_rows(d_contracted, d_contracted_theirs)
    ).astype(bf16)
    down_sum = net.scatter(down_slope)
    up_slope = contract_rows(
        both_rows(normed_mid_low, normed_mid_low_theirs), both_rows(d_exp_m, d_exp_other)
    ).astype(bf16)
    up_sum = net.scatter(up_slope)
    up_bias_m, up_bias_t = column_sums(d_exp_m), column_sums(d_exp_t)
    d_normed_mid = times_transpose(d_exp_m, up_mine) + times_transpose(d_exp_t, up_theirs)
    d_middle_part, third_slope = pull_third(d_normed_mid)
    d_middle = seed + d_middle_part
    d_attended_f, second_slope = pull_second(d_middle)
    d_attended = d_attended_f.astype(bf16)
    output_bias_slope = column_sums(d_attended)
    d_att_m, d_att_t = net.pick(d_attended.reshape(length, 2, half), 1)
    d_att_other = net.sibling(d_att_t)
    out_slope = contract_rows(
        both_rows(mixed_low, mixed_low_theirs), both_rows(d_att_m, d_att_other)
    ).astype(bf16)
    out_sum = net.scatter(out_slope)
    d_mixed = (
        (times_transpose(d_att_m, out_mine) + times_transpose(d_att_t, out_theirs))
        .astype(bf16)
        .reshape(length, heads, HEAD)
    )
    probs_again = jnp.exp(masked_scores(query_rot, key_rot, allowed) - logsum)
    d_values = jnp.einsum(
        "hqk,qhd->khd", probs_again.astype(bf16), d_mixed, preferred_element_type=f32
    )
    d_probs = jnp.einsum("qhd,khd->hqk", d_mixed, value_low, preferred_element_type=f32)
    row_terms = jnp.sum(probs_again * d_probs, axis=-1, keepdims=True)
    d_scores = (probs_again * (d_probs - row_terms)).astype(bf16)
    d_query_rot = (
        jnp.einsum("hqk,khd->qhd", d_scores, key_rot, preferred_element_type=f32) * 0.125
    )
    d_key_rot = (
        jnp.einsum("hqk,qhd->khd", d_scores, query_rot, preferred_element_type=f32) * 0.125
    )
    d_queries = rotate(d_query_rot, cosine, -sine).reshape(length, width).astype(bf16)
    d_keys = rotate(d_key_rot, cosine, -sine).reshape(length, width).astype(bf16)
    d_values_low = d_values.reshape(length, width).astype(bf16)
    pairs = [net.pick(v.reshape(length, 2, half), 1) for v in (d_queries, d_keys, d_values_low)]
    d_qkv_m = jnp.concatenate([p[0] for p in pairs], axis=1)
    d_qkv_t = jnp.concatenate([p[1] for p in pairs], axis=1)
    d_qkv_other = net.sibling(d_qkv_t)
    qkv_slope = contract_rows(
        both_rows(normed_low, normed_low_theirs), both_rows(d_qkv_m, d_qkv_other)
    ).astype(bf16)
    qkv_sum = net.scatter(qkv_slope)
    d_normed = times_transpose(d_qkv_m, qkv_mine) + times_transpose(d_qkv_t, qkv_theirs)
    d_inputs_part, first_slope = pull_first(d_normed)
    input_gradient = d_middle + d_inputs_part

    up_bias_low = jnp.where(core == 1, up_bias_t, up_bias_m).reshape(wide, 1, block)
    up_bias_high = jnp.where(core == 1, up_bias_m, up_bias_t).reshape(wide, 1, block)
    up_bias_slope = jnp.concatenate([up_bias_low, up_bias_high], axis=1).reshape(-1)
    small_slopes = jnp.concatenate(
        [
            column_sums(d_queries),
            column_sums(d_keys),
            column_sums(d_values_low),
            output_bias_slope,
            down_bias_slope,
            first_slope,
            second_slope,
            third_slope,
            fourth_slope,
            up_bias_slope,
            jnp.full((128,), local_power, f32),
        ]
    )
    sums = net.total(small_slopes)
    output_power = sums[-1] / (length * wide * 2)
    device = net.me * 2 + core
    own = lax.dynamic_slice_in_dim(sums[: 9 * width].reshape(9, width), device * rows, rows, 1)
    own_up = lax.dynamic_slice_in_dim(sums[9 * width : 9 * width + hidden], device * 2 * block // 2, block, 0)

    qkv_grad = net.columns_out(*qkv_sum).astype(f32)
    out_grad = net.columns_out(*out_sum).astype(f32).reshape(rows, width)
    up_grad = net.columns_out(*up_sum).astype(f32)
    up_grad = up_grad.reshape(rows, 2, wide, block).transpose(0, 2, 1, 3).reshape(rows, hidden)
    down_grad = jnp.concatenate(down_sum, axis=0).astype(f32)
    q_grad, k_grad, v_grad = (
        qkv_grad[:, :, i * half : (i + 1) * half].reshape(rows, width) for i in range(3)
    )
    return (
        layer_out,
        input_gradient,
        q_grad,
        k_grad,
        v_grad,
        out_grad,
        up_grad,
        down_grad,
        own[0],
        own[1],
        own[2],
        own[3],
        own_up,
        own[4],
        own[5],
        own[6],
        own[7],
        own[8],
        output_power,
    )


F32 = jnp.float32
BF16 = jnp.bfloat16
I32 = jnp.int32
EPS = 1e-06
VMEM_LIMIT = 60 * 1024 * 1024
LANES = 128
GELU_A = 0.7978845608028654
GELU_B = 0.044715
TILE = 128
DOWN_CHIPS = 4


def whole_spec():
    return pl.BlockSpec(memory_space=pltpu.VMEM)


def hbm_spec():
    return pl.BlockSpec(memory_space=pl.ANY)


def smem_spec():
    return pl.BlockSpec(memory_space=pltpu.SMEM)


def params():
    return pltpu.CompilerParams(vmem_limit_bytes=VMEM_LIMIT)


def shape(dims, dtype):
    return jax.ShapeDtypeStruct(dims, dtype)


def cost(flops, bytes_accessed):
    return pl.CostEstimate(flops=flops, bytes_accessed=bytes_accessed, transcendentals=0)


def dot(a, b):
    return lax.dot_general(a, b, (((1,), (0,)), ((), ())), preferred_element_type=F32)


def dot_t(a, b):
    return lax.dot_general(a, b, (((1,), (1,)), ((), ())), preferred_element_type=F32)


def t_dot(a, b):
    return lax.dot_general(a, b, (((0,), (0,)), ((), ())), preferred_element_type=F32)


def pair_mask(place):
    return place // 4 + 4 * (place % 4)


def assemble(where, pieces, target, sems, cols):
    copies = []
    for e in range(2):
        place = 0
        for piece in pieces[e * 5 : e * 5 + 5]:
            for j in range(piece.shape[0]):
                chip = where[0] ^ pair_mask(place)
                source = piece.at[j, :, pl.ds(*cols)]
                dest = target.at[chip, where[1] ^ e]
                copies.append(pltpu.make_async_copy(source, dest, sems.at[len(copies)]))
                place += 1
    for copy in copies:
        copy.start()
    return copies


def wait_all(copies):
    for copy in copies:
        copy.wait()


def fetch(sources, targets, sems, base=0):
    copies = [
        pltpu.make_async_copy(a, b, sems.at[base + i]) for i, (a, b) in enumerate(zip(sources, targets))
    ]
    for copy in copies:
        copy.start()
    return copies


def matrix(buf):
    return buf[...].reshape(-1, buf.shape[-1])


def inverse_rms(v):
    return lax.rsqrt(jnp.mean(v * v, axis=-1, keepdims=True) + EPS)


def place_rows(first, rows):
    n = rows[0].shape[1]
    at = lax.broadcasted_iota(I32, (8, n), 0)
    out = jnp.zeros((8, n), F32)
    for i, row in enumerate(rows):
        out = jnp.where(at == first + i, jnp.broadcast_to(row, (8, n)), out)
    return out


def rms_back(v, r, gain, e):
    ge = gain * e
    return r * ge - v * (r * r * r) * jnp.mean(v * ge, axis=-1, keepdims=True)


def row_sum(v):
    return jnp.sum(v, axis=0, keepdims=True)


def turn(v, cosine, sine):
    lane = lax.broadcasted_iota(I32, v.shape, 1)
    swapped = jnp.where((lane & 63) < 32, pltpu.roll(v, 96, 1), pltpu.roll(v, 32, 1))
    return v * cosine + swapped * sine


def project_kernel(parts, where, x, bias, *refs):
    pieces = refs[:10]
    tables = refs[10:-3]
    out, wbuf, sems = refs[-3:]
    width = x.shape[1]
    copies = [
        assemble(where, pieces, wbuf.at[i], sems.at[i], (i * width, width)) for i in range(parts)
    ]
    for i in range(parts):
        wait_all(copies[i])
        for c in range(0, width, 512):
            y = dot(x[...], wbuf[i, :, :, :, c : c + 512].reshape(width, 512))
            y = y + bias[:, i * width + c : i * width + c + 512]
            at = i * width + c
            if tables:
                cosine, sine = tables[0][...], tables[1][...]
                for b in range(0, 512, LANES):
                    z = turn(y[:, b : b + LANES], cosine, sine)
                    z = z * 0.125 if i == 0 else z
                    out[:, at + b : at + b + LANES] = z.astype(BF16)
            else:
                out[:, at : at + 512] = y.astype(BF16)


def project(where, x, pieces, parts, bias, tables=()):
    t, width = x.shape
    r = pieces[0].shape[1]
    return pl.pallas_call(
        functools.partial(project_kernel, parts),
        in_specs=[smem_spec(), whole_spec(), whole_spec()]
        + [hbm_spec()] * 10
        + [whole_spec()] * len(tables),
        out_specs=whole_spec(),
        out_shape=shape((t, parts * width), BF16),
        scratch_shapes=[
            pltpu.VMEM((parts, 16, 2, r, width), BF16),
            pltpu.SemaphoreType.DMA((parts, 32)),
        ],
        compiler_params=params(),
        cost_estimate=cost(2 * t * width * parts * width, 2 * parts * width * width),
        name="project",
    )(where, x, bias, *pieces, *tables)


def open_mask(col_ref, row_ref, open_ref):
    t = open_ref.shape[0]

    @pl.when(pl.program_id(0) == 0)
    def _():
        rows = lax.broadcasted_iota(I32, (t, t), 0)
        cols = lax.broadcasted_iota(I32, (t, t), 1)
        ok = (col_ref[...] == row_ref[...]) & (cols <= rows)
        open_ref[...] = jnp.where(ok, 0.0, -1e30)


def one_head(v, h):
    lane = lax.broadcasted_iota(I32, v.shape, 1)
    return jnp.where((lane < HEAD) == (h == 0), v, jnp.zeros_like(v))


def attend_kernel(q_ref, k_ref, v_ref, col_ref, row_ref, out_ref, lse_ref, open_ref):
    t = q_ref.shape[0]
    tile = TILE
    open_mask(col_ref, row_ref, open_ref)
    left = lax.broadcasted_iota(I32, (tile, LANES), 1) < HEAD
    spans = [(slice(i * tile, (i + 1) * tile), (i + 1) * tile) for i in range(t // tile)]
    pairs = [(rows, seen, h) for rows, seen in spans for h in range(2)]
    scores = [
        dot_t(one_head(q_ref[rows, :], h), k_ref[:seen, :]) + open_ref[rows, :seen]
        for rows, seen, h in pairs
    ]
    peaks = [jnp.max(s, axis=-1, keepdims=True) for s in scores]
    powers = [jnp.exp(s - peak) for s, peak in zip(scores, peaks)]
    totals = [jnp.sum(e, axis=-1, keepdims=True) for e in powers]
    outs = [
        dot(e.astype(BF16), v_ref[:seen, :]) / total
        for e, total, (rows, seen, h) in zip(powers, totals, pairs)
    ]
    sums = [peak + jnp.log(total) for peak, total in zip(peaks, totals)]
    for i, (rows, seen) in enumerate(spans):
        out_ref[rows, :] = jnp.where(left, outs[2 * i], outs[2 * i + 1]).astype(BF16)
        lse_ref[rows, :] = jnp.where(left, sums[2 * i], sums[2 * i + 1])


def attend(qk, v, col, row):
    t, width = v.shape
    steps = width // LANES
    block = lambda f: pl.BlockSpec((t, LANES), f)
    return pl.pallas_call(
        attend_kernel,
        grid=(steps,),
        in_specs=[
            block(lambda i: (0, i)),
            block(lambda i: (0, i + steps)),
            block(lambda i: (0, i)),
            pl.BlockSpec((t, 1), lambda i: (0, 0)),
            pl.BlockSpec((1, t), lambda i: (0, 0)),
        ],
        out_specs=[block(lambda i: (0, i))] * 2,
        out_shape=[shape((t, width), BF16), shape((t, width), F32)],
        scratch_shapes=[pltpu.VMEM((t, t), F32)],
        compiler_params=params(),
        cost_estimate=cost(4 * t * t * width, 10 * t * width),
        name="attend",
    )(qk, qk, v, col, row)


def attend_back_kernel(
    q_ref, k_ref, v_ref, dm_ref, lse_ref, col_ref, row_ref, cos_ref, sin_ref,
    d_ref, sum_ref, open_ref,
):
    t = q_ref.shape[0]
    tile = TILE
    open_mask(col_ref, row_ref, open_ref)
    left = lax.broadcasted_iota(I32, (tile, LANES), 1) < HEAD
    spans = [(slice(i * tile, (i + 1) * tile), (i + 1) * tile) for i in range(t // tile)]
    pairs = [(rows, seen, h) for rows, seen in spans for h in range(2)]
    scores = [
        dot_t(one_head(q_ref[rows, :], h), k_ref[:seen, :]) + open_ref[rows, :seen]
        for rows, seen, h in pairs
    ]
    d_probs = [dot_t(one_head(dm_ref[rows, :], h), v_ref[:seen, :]) for rows, seen, h in pairs]
    probs = [
        jnp.exp(s - lse_ref[rows, h * HEAD : h * HEAD + 1])
        for s, (rows, seen, h) in zip(scores, pairs)
    ]
    deltas = [jnp.sum(p * dp, axis=-1, keepdims=True) for p, dp in zip(probs, d_probs)]
    d_scores = [(p * (dp - d)).astype(BF16) for p, dp, d in zip(probs, d_probs, deltas)]
    probs = [p.astype(BF16) for p in probs]
    dq = [dot(ds, k_ref[:seen, :]) for ds, (rows, seen, h) in zip(d_scores, pairs)]
    total_q = jnp.zeros((1, LANES), F32)
    for i, (rows, seen) in enumerate(spans):
        v = jnp.where(left, dq[2 * i], dq[2 * i + 1]) * 0.125
        v = turn(v, cos_ref[rows, :], -sin_ref[rows, :]).astype(BF16)
        d_ref[0, rows, :] = v
        total_q += row_sum(v.astype(F32))
    totals = [total_q]
    for at, lhs, rhs in ((1, d_scores, q_ref), (2, probs, dm_ref)):
        total = jnp.zeros((1, LANES), F32)
        parts = [t_dot(a, rhs[rows, :]) for a, (rows, seen, h) in zip(lhs, pairs)]
        for i, (keys, _) in enumerate(spans):
            heads = [
                sum(parts[2 * j + h][keys] for j in range(i, len(spans))) for h in range(2)
            ]
            v = jnp.where(left, heads[0], heads[1])
            if at == 1:
                v = turn(v, cos_ref[keys, :], -sin_ref[keys, :])
            v = v.astype(BF16)
            d_ref[at, keys, :] = v
            total += row_sum(v.astype(F32))
        totals.append(total)
    sum_ref[...] = place_rows(0, totals)


def attend_back(qk, v, dm, lse, col, row, cosine, sine, first, steps):
    t, width = v.shape
    key = width // LANES
    part = steps * LANES
    block = lambda f: pl.BlockSpec((t, LANES), f)
    fixed = lambda a: pl.BlockSpec(a.shape, lambda i: (0, 0))
    here = block(lambda i: (0, i))
    read = block(lambda i: (0, i + first))
    return pl.pallas_call(
        attend_back_kernel,
        grid=(steps,),
        in_specs=[read, block(lambda i: (0, i + first + key)), read, read, read]
        + [fixed(a) for a in (col, row, cosine, sine)],
        out_specs=[
            pl.BlockSpec((3, t, LANES), lambda i: (0, 0, i)),
            pl.BlockSpec((8, LANES), lambda i: (0, i)),
        ],
        out_shape=[shape((3, t, part), BF16), shape((8, part), F32)],
        scratch_shapes=[pltpu.VMEM((t, t), F32)],
        compiler_params=params(),
        cost_estimate=cost(10 * t * t * part, 18 * t * part),
        name="attend_back",
    )(qk, qk, v, dm, lse, col, row, cosine, sine)


def out_kernel(where, mixed, order, x, bias, g2, g3, *refs):
    pieces = refs[:10]
    m_own, m_sib, att_ref, mid_ref, n_ref, n_own, n_sib, wbuf, sems = refs[10:]
    t, width = mixed.shape
    half = width // 2
    copies = assemble(where, pieces, wbuf, sems, (width, width))
    turned = dot_t(order[...], mixed[...]).astype(BF16)
    m_own[...] = turned[:half]
    m_sib[...] = turned[half:]
    wait_all(copies)
    w = matrix(wbuf)
    tile = 256
    for i in range(t // tile):
        rows = slice(i * tile, (i + 1) * tile)
        att = dot(mixed[rows, :], w) + bias[...]
        att_ref[rows, :] = att
        mid = x[rows, :].astype(F32) + att * inverse_rms(att) * g2[...]
        mid_ref[rows, :] = mid
        n_ref[rows, :] = (mid * inverse_rms(mid) * g3[...]).astype(BF16)
    turned = dot_t(order[...], n_ref[...]).astype(BF16)
    n_own[...] = turned[:half]
    n_sib[...] = turned[half:]


def out_project(where, mixed, order, x, bias, g2, g3, pieces):
    t, width = mixed.shape
    half = width // 2
    r = pieces[0].shape[1]
    halves = [shape((half, t), BF16)] * 2
    return pl.pallas_call(
        out_kernel,
        in_specs=[smem_spec()] + [whole_spec()] * 6 + [hbm_spec()] * 10,
        out_specs=[whole_spec()] * 7,
        out_shape=halves + [shape((t, width), F32)] * 2 + [shape((t, width), BF16)] + halves,
        scratch_shapes=[pltpu.VMEM((16, 2, r, width), BF16), pltpu.SemaphoreType.DMA((32,))],
        compiler_params=params(),
        cost_estimate=cost(6 * t * width * width, 16 * t * width),
        name="out_project",
    )(where, mixed, order, x, bias, g2, g3, *pieces)


def feed_kernel(
    where, x, b_up, w_up, w_down, b_down, valid, g4, mid_hbm, cot_hbm,
    a_own, a_sib, slope_ref, out_ref, dc_ref, sums_ref, power_ref, act_buf, acc, mid, cot, sems,
):
    step = pl.program_id(0)
    t, width = acc.shape
    first = where[1] == 0
    copies = [
        pltpu.make_async_copy(mid_hbm, mid, sems.at[0]),
        pltpu.make_async_copy(cot_hbm, cot, sems.at[1]),
    ]

    @pl.when(step == 0)
    def _():
        for copy in copies:
            copy.start()

    for j in range(w_up.shape[3] // 256):
        cols = slice(j * 256, (j + 1) * 256)
        y = dot(x[...], w_up[:, 0, :, cols].reshape(width, 256)) + b_up[:, cols]
        yy = y * y
        h = 0.5 * jnp.tanh(y * (GELU_A + (GELU_A * GELU_B) * yy)) + 0.5
        act = y * h
        slope = h + act * (1.0 - h) * (2 * GELU_A + (6 * GELU_A * GELU_B) * yy)
        act = act.astype(BF16)
        act_buf[:, cols] = act
        slope_ref[:, cols] = slope.astype(BF16)
        dst = slice(j * 128, (j + 1) * 128)
        a0, a1 = act[:, :128], act[:, 128:]
        a_own[:, dst] = jnp.where(first, a0, a1)
        a_sib[:, dst] = jnp.where(first, a1, a0)
    y = dot(act_buf[...], w_down[...].reshape(-1, width))

    @pl.when(step == 0)
    def _():
        acc[...] = y + b_down[...]

    @pl.when(step > 0)
    def _():
        acc[...] += y

    @pl.when(step == pl.num_programs(0) - 1)
    def _():
        wait_all(copies)
        tile = 128
        power = jnp.zeros((1, 1), F32)
        gain_sum = jnp.zeros((1, width), F32)
        bias_sum = jnp.zeros((1, width), F32)
        gain = g4[...]
        for i in range(t // tile):
            rows = slice(i * tile, (i + 1) * tile)
            v = acc[rows, :]
            ok = valid[rows, :]
            mean = jnp.mean(v * v, axis=-1, keepdims=True)
            power += row_sum(mean * ok)
            r = lax.rsqrt(mean + EPS)
            vr = v * r
            out_ref[rows, :] = (mid[rows, :] + vr * gain).astype(BF16)
            seed = cot[rows, :].astype(F32) * ok
            gain_sum += row_sum(vr * seed)
            dc = rms_back(v, r, gain, seed).astype(BF16)
            dc_ref[rows, :] = dc
            bias_sum += row_sum(dc.astype(F32))
        sums_ref[...] = place_rows(6, [gain_sum, bias_sum])
        power_ref[...] = jnp.broadcast_to(power, power_ref.shape)


def feed_forward(where, x, b_up, b_down, mid, cot, valid, g4, ffn):
    t, width = x.shape
    hidden = b_up.shape[1]
    devices, _, r, tn = ffn.shape
    steps = hidden // tn
    fixed = lambda a: pl.BlockSpec(a.shape, lambda i: (0, 0))
    tile = lambda n: pl.BlockSpec((t, n), lambda i: (0, i))
    return pl.pallas_call(
        feed_kernel,
        grid=(steps,),
        in_specs=[
            smem_spec(),
            fixed(x),
            pl.BlockSpec((1, tn), lambda i: (0, i)),
            pl.BlockSpec((devices, 1, r, tn), lambda i: (0, i, 0, 0)),
            pl.BlockSpec((devices // steps, 4, r, width), lambda i: (i, 1, 0, 0)),
            fixed(b_down),
            fixed(valid),
            fixed(g4),
            hbm_spec(),
            hbm_spec(),
        ],
        out_specs=[tile(tn // 2), tile(tn // 2), tile(tn)]
        + [pl.BlockSpec((t, width), lambda i: (0, 0))] * 2
        + [pl.BlockSpec((8, width), lambda i: (0, 0)), pl.BlockSpec((1, LANES), lambda i: (0, 0))],
        out_shape=[shape((t, hidden // 2), BF16)] * 2
        + [shape((t, hidden), BF16)]
        + [shape((t, width), BF16)] * 2
        + [shape((8, width), F32), shape((1, LANES), F32)],
        scratch_shapes=[
            pltpu.VMEM((t, tn), BF16),
            pltpu.VMEM((t, width), F32),
            pltpu.VMEM((t, width), F32),
            pltpu.VMEM((t, width), BF16),
            pltpu.SemaphoreType.DMA((2,)),
        ],
        compiler_params=params(),
        cost_estimate=cost(4 * t * width * hidden, 4 * width * hidden + 8 * t * hidden),
        name="feed_forward",
    )(where, x, b_up, ffn, ffn, b_down, valid, g4, mid, cot)


def block_at(ref, where, place):
    chip = where[0] ^ pair_mask(place)
    return ref.at[:, pl.ds(pl.multiple_of(chip * LANES, LANES), LANES)]


def down_back_kernel(dc, slope, w_ref, de_ref, sums_ref):
    width = dc.shape[1]
    for j in range(w_ref.shape[0]):
        cols = slice(j * 256, (j + 1) * 256)
        y = dot_t(dc[...], w_ref[j].reshape(256, width))
        d = (y * slope[:, cols].astype(F32)).astype(BF16)
        de_ref[:, cols] = d
        sums_ref[:, cols] = row_sum(d.astype(F32))


def down_back(dc, slope, ffn):
    t, width = dc.shape
    hidden = slope.shape[1]
    r = ffn.shape[3]
    chips = DOWN_CHIPS
    tn = chips * 256
    return pl.pallas_call(
        down_back_kernel,
        grid=(hidden // tn,),
        in_specs=[
            pl.BlockSpec((t, width), lambda i: (0, 0)),
            pl.BlockSpec((t, tn), lambda i: (0, i)),
            pl.BlockSpec((chips, 2, 4, r, width), lambda i: (i, 0, 1, 0, 0)),
        ],
        out_specs=[pl.BlockSpec((t, tn), lambda i: (0, i)), pl.BlockSpec((1, tn), lambda i: (0, i))],
        out_shape=[shape((t, hidden), BF16), shape((1, hidden), F32)],
        compiler_params=params(),
        cost_estimate=cost(2 * t * hidden * width, 2 * hidden * width),
        name="down_back",
    )(dc, slope, ffn)


GRAD_PLACES = {
    "d23": (14, 15),
    "d01": (12, 13),
    "x01": (4, 5),
    "y23": (10, 11),
    "x23": (6, 7),
    "y01": (8, 9),
    "f": (0, 1, 2, 3),
}


def runs_of(places):
    return [(at, places[at : at + 2]) for at in range(0, len(places), 2)]


def slope_kernel(parts, x_own, x_oth, *refs):
    dy_own, dy_oth = refs[:parts], refs[parts : 2 * parts]
    outs = refs[2 * parts :]
    for i in range(parts):
        n = dy_own[i].shape[1]
        y = dot(x_own[...], dy_own[i][...]) + dot(x_oth[...], dy_oth[i][...])
        y = y.astype(BF16)
        for places, out in zip(GRAD_PLACES.values(), outs):
            r = out.shape[1]
            for at, run in runs_of(places):
                part = y[run[0] * r : (run[-1] + 1) * r]
                out[at : at + 2, :, i * n : (i + 1) * n] = part.reshape(2, r, n)


def row_slopes(x_own, x_oth, dy_own, dy_oth, tiles, first=0):
    half, t = x_own.shape
    r = half // 16
    n = dy_own.shape[1] // tiles
    total = n * (first + tiles)
    fixed = pl.BlockSpec((half, t), lambda i: (0, 0))
    return pl.pallas_call(
        functools.partial(slope_kernel, 1),
        grid=(tiles,),
        in_specs=[fixed] * 2 + [pl.BlockSpec((t, n), lambda i: (0, i))] * 2,
        out_specs=[pl.BlockSpec((len(p), r, n), lambda i: (0, 0, i + first)) for p in GRAD_PLACES.values()],
        out_shape=[shape((len(p), r, total), BF16) for p in GRAD_PLACES.values()],
        compiler_params=params(),
        cost_estimate=cost(4 * t * half * n * tiles, 8 * t * n * tiles + 2 * half * n * tiles),
        name="row_slopes",
    )(x_own, x_oth, dy_own, dy_oth)


def qkv_slope_kernel(x_own, x_oth, a_own, b_own, a_oth, b_oth, *refs):
    outs = refs[len(GRAD_PLACES) :]
    n = a_own.shape[2]
    for i, (own, oth) in enumerate(((a_own, a_oth), (b_own, b_oth))):
        y = dot(x_own[...], own[0]) + dot(x_oth[...], oth[0])
        y = y.astype(BF16)
        for places, out in zip(GRAD_PLACES.values(), outs):
            r = out.shape[1]
            for at, run in runs_of(places):
                part = y[run[0] * r : (run[-1] + 1) * r]
                out[at : at + 2, :, i * n : (i + 1) * n] = part.reshape(2, r, n)


def qkv_slopes(x_own, x_oth, a_own, b_own, a_oth, b_oth, pieces):
    half, t = x_own.shape
    r = half // 16
    n = a_own.shape[2]
    fixed = pl.BlockSpec((half, t), lambda i: (0, 0))
    return pl.pallas_call(
        qkv_slope_kernel,
        grid=(3,),
        in_specs=[fixed] * 2
        + [pl.BlockSpec((1, t, n), lambda i: (i, 0, 0))] * 4
        + [hbm_spec()] * len(pieces),
        out_specs=[pl.BlockSpec((len(p), r, 2 * n), lambda i: (0, 0, i)) for p in GRAD_PLACES.values()],
        out_shape=[shape(p.shape, BF16) for p in pieces],
        input_output_aliases={6 + i: i for i in range(len(pieces))},
        compiler_params=params(),
        cost_estimate=cost(24 * t * half * n, 24 * t * n + 12 * half * n),
        name="qkv_slopes",
    )(x_own, x_oth, a_own, b_own, a_oth, b_oth, *pieces)


def block_slope_kernel(where, a_own, a_oth, dy_own, dy_oth, *refs):
    outs = refs[:7]
    stage, sems = refs[7:]
    sent = []
    for places, out in zip(GRAD_PLACES.values(), outs):
        for at, run in runs_of(places):
            i = len(sent)
            mine, other = (
                jnp.concatenate([block_at(act, where, p)[...] for p in run], axis=1)
                for act in (a_own, a_oth)
            )
            y = t_dot(mine, dy_own[...]) + t_dot(other, dy_oth[...])
            stage[i] = y.astype(BF16).reshape(2, LANES, y.shape[1])
            copy = pltpu.make_async_copy(stage.at[i], out.at[pl.ds(at, 2)], sems.at[i])
            copy.start()
            sent.append(copy)
    wait_all(sent)


def block_slopes(where, a_own, a_oth, dy_own, dy_oth):
    t, half = a_own.shape
    width = dy_own.shape[1]
    return pl.pallas_call(
        block_slope_kernel,
        in_specs=[smem_spec()] + [whole_spec()] * 4,
        out_specs=[hbm_spec()] * 7,
        out_shape=[shape((len(p), LANES, width), BF16) for p in GRAD_PLACES.values()],
        scratch_shapes=[pltpu.VMEM((8, 2, LANES, width), BF16), pltpu.SemaphoreType.DMA((8,))],
        compiler_params=params(),
        cost_estimate=cost(4 * t * half * width, 4 * t * (half + width) + 2 * half * width),
        name="block_slopes",
    )(where, a_own, a_oth, dy_own, dy_oth)


def up_back_kernel(where, de, valid, g2_ref, g3_ref, w_ref, mid_hbm, att_hbm, cot_hbm, *refs):
    pieces = refs[:10]
    dmid_ref, datt_ref, dmix_ref, sums_ref, acc, wbuf, mid_buf, att_buf, cot_buf, sems = refs[10:]
    step = pl.program_id(0)
    t, width = acc.shape

    @pl.when(step == 0)
    def _():
        assemble(where, pieces, wbuf, sems, (width, width))
        fetch((mid_hbm, att_hbm, cot_hbm), (mid_buf, att_buf, cot_buf), sems, 32)

    y = dot_t(de[...], w_ref[:, 0].reshape(width, -1))

    @pl.when(step == 0)
    def _():
        acc[...] = y

    @pl.when(step > 0)
    def _():
        acc[...] += y

    @pl.when(step == pl.num_programs(0) - 1)
    def _():
        for i in range(32):
            pltpu.make_async_copy(pieces[0].at[0, :, pl.ds(width, width)], wbuf.at[0, 0], sems.at[i]).wait()
        for i, (a, b) in enumerate(((mid_hbm, mid_buf), (att_hbm, att_buf), (cot_hbm, cot_buf))):
            pltpu.make_async_copy(a, b, sems.at[32 + i]).wait()
        tile = 128
        g2, g3 = g2_ref[...], g3_ref[...]
        w = matrix(wbuf)
        sums = [jnp.zeros((1, width), F32)] * 3
        for i in range(t // tile):
            rows = slice(i * tile, (i + 1) * tile)
            e = acc[rows, :]
            mid = mid_buf[rows, :]
            r3 = inverse_rms(mid)
            dmid = cot_buf[rows, :].astype(F32) * valid[rows, :] + rms_back(mid, r3, g3, e)
            dmid_ref[rows, :] = dmid
            att = att_buf[rows, :]
            r2 = inverse_rms(att)
            datt = rms_back(att, r2, g2, dmid).astype(BF16)
            datt_ref[rows, :] = datt
            sums[0] += row_sum(mid * r3 * e)
            sums[1] += row_sum(att * r2 * dmid)
            sums[2] += row_sum(datt.astype(F32))
        dmix_ref[...] = dot_t(datt_ref[...], w).astype(BF16)
        sums_ref[...] = place_rows(3, sums)


def up_back(where, de, mid, att, cot, valid, g2, g3, ffn, pieces):
    t, width = mid.shape
    hidden = de.shape[1]
    tk = ffn.shape[3]
    r = pieces[0].shape[1]
    fixed = lambda a: pl.BlockSpec(a.shape, lambda i: (0, 0))
    return pl.pallas_call(
        up_back_kernel,
        grid=(hidden // tk,),
        in_specs=[smem_spec(), pl.BlockSpec((t, tk), lambda i: (0, i))]
        + [fixed(a) for a in (valid, g2, g3)]
        + [pl.BlockSpec((ffn.shape[0], 1, ffn.shape[2], tk), lambda i: (0, i, 0, 0))]
        + [hbm_spec()] * 13,
        out_specs=[pl.BlockSpec((t, width), lambda i: (0, 0))] * 3
        + [pl.BlockSpec((8, width), lambda i: (0, 0))],
        out_shape=[shape((t, width), F32), shape((t, width), BF16), shape((t, width), BF16), shape((8, width), F32)],
        scratch_shapes=[
            pltpu.VMEM((t, width), F32),
            pltpu.VMEM((16, 2, r, width), BF16),
            pltpu.VMEM((t, width), F32),
            pltpu.VMEM((t, width), F32),
            pltpu.VMEM((t, width), BF16),
            pltpu.SemaphoreType.DMA((35,)),
        ],
        compiler_params=params(),
        cost_estimate=cost(2 * t * width * hidden, 2 * width * hidden + 2 * t * hidden),
        name="up_back",
    )(where, de, valid, g2, g3, ffn, mid, att, cot, *pieces)


def in_back_kernel(where, *refs):
    d_a, d_b, x_hbm, dmid_hbm, g1_ref = refs[:5]
    qk, vo = refs[5:15], refs[15:25]
    out_ref, sums_ref, wbuf, x_buf, dmid_buf, sems = refs[25:]
    t, width = out_ref.shape
    half = width // 2
    copies = [
        assemble(where, pieces, wbuf.at[i], sems.at[i], (start, width))
        for i, (pieces, start) in enumerate(((qk, 0), (qk, width), (vo, 0)))
    ]
    late = fetch((x_hbm, dmid_hbm), (x_buf, dmid_buf), sems.at[3])
    e = None
    for i in range(3):
        wait_all(copies[i])
        d = jnp.concatenate([d_a[i], d_b[i]], axis=1)
        y = dot_t(d, wbuf[i].reshape(width, width))
        e = y if e is None else e + y
    wait_all(late)
    gain = g1_ref[...]
    tile = 128
    total = jnp.zeros((1, width), F32)
    for i in range(t // tile):
        rows = slice(i * tile, (i + 1) * tile)
        x = x_buf[rows, :].astype(F32)
        r = inverse_rms(x)
        out_ref[rows, :] = dmid_buf[rows, :] + rms_back(x, r, gain, e[rows, :])
        total += row_sum(x * r * e[rows, :])
    sums_ref[...] = total


def in_back(where, d_a, d_b, x, dmid, g1, qk_pieces, vo_pieces):
    t, width = x.shape
    r = qk_pieces[0].shape[1]
    return pl.pallas_call(
        in_back_kernel,
        in_specs=[smem_spec()] + [whole_spec()] * 2 + [hbm_spec()] * 2 + [whole_spec()] + [hbm_spec()] * 20,
        out_specs=[whole_spec()] * 2,
        out_shape=[shape((t, width), F32), shape((1, width), F32)],
        scratch_shapes=[
            pltpu.VMEM((3, 16, 2, r, width), BF16),
            pltpu.VMEM((t, width), BF16),
            pltpu.VMEM((t, width), F32),
            pltpu.SemaphoreType.DMA((4, 32)),
        ],
        compiler_params=params(),
        cost_estimate=cost(6 * t * width * width, 6 * width * width),
        name="in_back",
    )(where, d_a, d_b, x, dmid, g1, *qk_pieces, *vo_pieces)


def after(*values):
    return lax.optimization_barrier(values)


def add(*values):
    total = values[0].astype(F32)
    for v in values[1:]:
        total = total + v.astype(F32)
    return total


class Gather:
    def __init__(self, net, shard):
        self.net = net
        self.line = [shard] + [net.swap(shard, 4 * m) for m in (1, 2, 3)]

    def spread(self, line):
        net = self.net
        self.lines = jnp.stack(line)
        self.x = net.swap(self.lines, 1)
        self.y = net.swap(self.lines, 2)
        self.sib = [net.sibling(self.lines)]

    def corner(self, x, y):
        net = self.net
        self.x, self.y = x, y
        self.d01 = net.swap(x[:2], 2)
        self.d23 = net.swap(y[2:], 1)
        self.sib += [net.sibling(x), net.sibling(y)]

    def finish(self, d01, d23):
        net = self.net
        self.d01, self.d23 = d01, d23
        self.sib += [net.sibling(d01), net.sibling(d23)]

    def pieces(self):
        return [self.lines, self.x, self.y, self.d01, self.d23] + self.sib


class Scatter:
    def __init__(self, net, pieces):
        self.net = net
        self.d23, self.d01, self.x01, self.y23, self.x23, self.y01, self.f = pieces

    def a(self):
        self.got = [self.net.swap(self.d23, 1), self.net.swap(self.d01, 2)]

    def c(self, x23, y01):
        self.last = [self.net.swap(x23, 1), self.net.swap(y01, 2)]

    def fold_b(self, got):
        return [add(self.x01, got[1]).astype(BF16), add(self.y23, got[0]).astype(BF16)]

    def b(self, fold):
        self.got = [self.net.swap(fold[0], 1), self.net.swap(fold[1], 2)]

    def fold_last(self, last):
        return [add(self.f[:2], last[1]), add(self.f[2:], last[0])]

    def fold_near(self, got, part):
        low, high = add(part[0], got[0]), add(part[1], got[1])
        return [low[0], high[0], jnp.stack([low[1], high[1]]).astype(BF16)]

    def near(self, fold):
        self.low, self.high, send = fold
        self.got = [self.net.swap(send, 4)]

    def fold_far(self, got):
        return [add(self.low, got[0][0]), add(self.high, got[0][1]).astype(BF16)]

    def far(self, fold):
        self.own, send = fold
        self.got = [self.net.swap(send, 8)]

    def result(self, got):
        return add(self.own, got[0])


def shards_16(
    activations,
    segment_ids,
    cotangent,
    querymat,
    keymat,
    valuemat,
    outmat,
    upmatrix,
    downmatrix,
    querybias,
    keybias,
    valuebias,
    outbias,
    upbias,
    downbias,
    firstgain,
    secondgain,
    thirdgain,
    fourthgain,
):
    net = Net(16)
    t, width = activations.shape
    rows = querymat.shape[0]
    hidden = upmatrix.shape[1]
    block = upbias.shape[0]
    half = width // 2
    me, core = net.me, net.core
    device = me * 2 + core
    where = jnp.stack([me, core]).astype(I32)

    dst = jnp.arange(width)
    place = (dst // rows) % 16
    chip = me ^ (place // 4 + 4 * (place % 4))
    src = chip * (2 * rows) + (core ^ (dst // half)) * rows + dst % rows
    order = (src[:, None] == jnp.arange(width)[None, :]).astype(BF16)
    slots = jnp.arange(t)
    segment = jnp.where(segment_ids >= 0, segment_ids, -1 - slots)
    col, row = segment[:, None], segment[None, :]
    valid = (segment_ids >= 0).astype(F32)[:, None]
    spots = positions_of(segment_ids).astype(F32)
    inverse = 10000.0 ** (-jnp.arange(HEAD // 2).astype(F32) * 2.0 / HEAD)
    angles = spots[:, None] * inverse[None, :]
    cosine = jnp.tile(jnp.cos(angles), (1, 4))
    sine = jnp.sin(angles)
    sine = jnp.tile(jnp.concatenate([-sine, sine], axis=1), (1, 2))

    ffn_shard = jnp.concatenate(
        [upmatrix.reshape(rows, 4, width).transpose(1, 0, 2), downmatrix.reshape(4, rows, width)]
    )
    ffn = lax.all_gather(ffn_shard, AXES, axis=0, tiled=False)
    qk = Gather(net, jnp.concatenate([querymat, keymat], axis=1))
    vo_shard = jnp.concatenate([valuemat, outmat], axis=1)
    nine = [querybias, keybias, valuebias, outbias, downbias, firstgain, secondgain, thirdgain, fourthgain]
    small = jnp.concatenate([jnp.pad(v[None], ((0, 0), (0, LANES - rows))) for v in nine] + [upbias[None]])
    buf = small[None]
    buf = jnp.concatenate([buf, net.sibling(buf)])
    for mask in (1, 2, 4, 8):
        buf = jnp.concatenate([buf, net.swap(buf, mask)])
    line, buf, vo_shard = after(qk.line, buf, vo_shard)
    qk.spread(line)
    vo = Gather(net, vo_shard)

    picks = (jnp.arange(32)[:, None] ^ device) == jnp.arange(32)[None, :]
    small_all = dot(picks.astype(BF16), buf.reshape(32, -1)).reshape(32, 10, LANES)
    b_q, b_k, b_v, b_o, b_d, g1, g2, g3, g4 = (
        small_all[:, i, :rows].reshape(1, width) for i in range(9)
    )
    b_up = small_all[:, 9].reshape(1, hidden)
    inputs = activations.astype(F32)
    normed = (inputs * inverse_rms(inputs) * g1).astype(BF16)
    turned = dot_t(order, normed).astype(BF16)
    x_own, x_sib = turned[:half], turned[half:]

    x, y, line = after(qk.x, qk.y, vo.line)
    qk.corner(x, y)
    vo.spread(line)
    d01, d23, x_sib, normed, tables, vectors = after(
        qk.d01,
        qk.d23,
        x_sib,
        normed,
        (cosine, sine, col, row, valid, order),
        (b_q, b_k, b_v, b_o, b_d, g2, g3, g4, b_up),
    )
    cosine, sine, col, row, valid, order = tables
    b_q, b_k, b_v, b_o, b_d, g2, g3, g4, b_up = vectors
    qk.finish(d01, d23)
    x_oth = net.sibling(x_sib)
    x, y = after(vo.x, vo.y)
    vo.corner(x, y)
    qk_pieces = qk.pieces()
    qk_rot = project(where, normed, qk_pieces, 2, jnp.concatenate([b_q, b_k], axis=1), (cosine, sine))
    d01, d23, qk_rot = after(vo.d01, vo.d23, qk_rot)
    vo.finish(d01, d23)
    vo_pieces = vo.pieces()
    v = project(where, normed, vo_pieces, 1, b_v)
    mixed, lse = attend(qk_rot, v, col, row)
    m_own, m_sib, att, mid, normed_mid, n_own, n_sib = out_project(
        where, mixed, order, activations, b_o, g2, g3, vo_pieces
    )
    m_oth = net.sibling(m_sib)
    n_oth = net.sibling(n_sib)
    a_own, a_sib, slope, layer_out, dc, down_sums, power = feed_forward(
        where, normed_mid, b_up, b_d, mid, cotangent, valid, g4, ffn
    )
    a_oth = net.sibling(a_sib)
    ffn_down = ffn.reshape(16, 2, 8, rows, width)

    dc_oth = net.sibling(dc)
    de, up_bias_sum = down_back(dc, slope, ffn_down)
    de, dc_oth, a_oth = after(de, dc_oth, a_oth)

    de_oth = net.sibling(de)
    slopes, de, de_oth = after(block_slopes(where, a_own, a_oth, dc, dc_oth), de, de_oth)

    down_sum = Scatter(net, slopes)
    down_sum.a()
    back = up_back(where, de, mid, att, cotangent, valid, g2, g3, ffn, vo_pieces)
    back, de, got, n_own, x23, y01 = after(back, de, down_sum.got, n_own, down_sum.x23, down_sum.y01)
    dmid, datt, dmix, mid_sums = back

    down_sum.c(x23, y01)
    fold = down_sum.fold_b(got)
    datt_oth = net.sibling(datt)
    slopes = row_slopes(n_own, n_oth, de, de_oth, 4)
    slopes, fold, datt_oth, datt, dmix, last = after(slopes, fold, datt_oth, datt, dmix, down_sum.last)

    down_sum.b(fold)
    part = down_sum.fold_last(last)
    steps = width // LANES // 2
    part_a = attend_back(qk_rot, v, dmix, lse, col, row, cosine, sine, 0, steps)
    part_a, dmix, slopes, got, part = after(part_a, dmix, slopes, down_sum.got, part)
    d_a, sums_a = part_a

    up_sum = Scatter(net, slopes)
    up_sum.a()
    fold = down_sum.fold_near(got, part)
    a_other = net.sibling(d_a)
    part_b = attend_back(qk_rot, v, dmix, lse, col, row, cosine, sine, steps, steps)
    part_b, datt, up_got, fold, a_other, m_own, x23, y01 = after(
        part_b, datt, up_sum.got, fold, a_other, m_own, up_sum.x23, up_sum.y01
    )
    d_b, sums_b = part_b

    up_sum.c(x23, y01)
    down_sum.near(fold)
    b_other = net.sibling(d_b)
    slopes = row_slopes(m_own, m_oth, datt, datt_oth, 1, 3)
    slopes, b_other, d_a, d_b, a_other, up_got = after(slopes, b_other, d_a, d_b, a_other, up_got)
    up_fold = up_sum.fold_b(up_got)
    slopes = qkv_slopes(x_own, x_oth, d_a, d_b, a_other, b_other, slopes)
    slopes, up_fold, up_last, got, d_a, d_b = after(
        slopes, up_fold, up_sum.last, down_sum.got, d_a, d_b
    )

    up_sum.b(up_fold)
    part = up_sum.fold_last(up_last)
    down_sum.far(down_sum.fold_far(got))
    input_gradient, first_sum = in_back(where, d_a, d_b, activations, dmid, g1, qk_pieces, vo_pieces)
    sums = jnp.concatenate([sums_a, sums_b], axis=1) + mid_sums + down_sums
    sums = jnp.concatenate(
        [
            sums,
            first_sum,
            up_bias_sum.reshape(4, width),
            jnp.pad(power, ((0, 2), (0, width - LANES))),
        ]
    )
    sums, slopes, up_got, part, down_got = after(sums, slopes, up_sum.got, part, down_sum.got)

    att_sum = Scatter(net, slopes)
    att_sum.a()
    up_sum.near(up_sum.fold_near(up_got, part))
    down_total = down_sum.result(down_got)
    sums = sums + net.sibling(sums)
    sums = sums + net.swap(sums, 1)
    sums, got, up_got, x23, y01 = after(sums, att_sum.got, up_sum.got, att_sum.x23, att_sum.y01)

    att_sum.c(x23, y01)
    up_sum.far(up_sum.fold_far(up_got))
    fold = att_sum.fold_b(got)
    sums = sums + net.swap(sums, 2)
    sums = sums + net.swap(sums, 4)
    fold, up_got, sums, last = after(fold, up_sum.got, sums, att_sum.last)

    att_sum.b(fold)
    part = att_sum.fold_last(last)
    sums = sums + net.swap(sums, 8)
    got, sums, part = after(att_sum.got, sums, part)

    att_sum.near(att_sum.fold_near(got, part))
    up_total = up_sum.result(up_got)
    own = lax.dynamic_slice_in_dim(sums[:9], device * rows, rows, 1)
    own_up = lax.dynamic_slice_in_dim(sums[9:13].reshape(-1), device * block, block, 0)
    got, own, own_up, power_sum = after(att_sum.got, own, own_up, sums[13, 0])

    att_sum.far(att_sum.fold_far(got))
    att_total = att_sum.result(att_sum.got)
    qkv_total = [att_total[:, i * width : (i + 1) * width] for i in range(3)]
    out_total = att_total[:, 3 * width :]

    output_power = power_sum / (t * 32)
    own = [own[i] for i in (0, 1, 2, 5, 7, 8, 4, 3, 6)]
    return (
        layer_out,
        input_gradient,
        *qkv_total,
        out_total,
        up_total,
        down_total,
        own[0],
        own[1],
        own[2],
        own[3],
        own_up,
        own[4],
        own[5],
        own[6],
        own[7],
        own[8],
        output_power,
    )


def shards(*args):
    rows, length = args[3].shape[0], args[0].shape[0]
    if lax.axis_size("wide") == 16 and rows == 32 and length == 512:
        return shards_16(*args)
    return shards_any(*args)


def solution(mesh):
    matrix = P(AXES, None)
    vector = P(AXES)
    return jax.shard_map(
        shards,
        mesh=mesh,
        in_specs=(matrix, vector, matrix) + (matrix,) * 6 + (vector,) * 10,
        out_specs=(matrix,) * 8 + (vector,) * 10 + (P(),),
        check_vma=False,
    )
```

```python
import jax
import jax.numpy as jnp
import functools

from jax import lax
from jax.experimental import pallas as pl
from jax.experimental.pallas import tpu as pltpu
from jax.sharding import PartitionSpec as P

HEAD = 64
AXES = ("wide", "narrow")


def rms_norm(values, gain):
    return values * lax.rsqrt(jnp.mean(values * values, axis=-1, keepdims=True) + 1e-06) * gain


def rotate(values, cosine, sine):
    midpoint = values.shape[-1] // 2
    first_half = values[..., :midpoint]
    second_half = values[..., midpoint:]
    return jnp.concatenate(
        [first_half * cosine - second_half * sine, first_half * sine + second_half * cosine],
        axis=-1,
    )


def positions_of(segment):
    places = jnp.arange(segment.shape[0])
    matching = segment[:, None] == segment[None, :]
    earlier = places[None, :] < places[:, None]
    return jnp.sum(jnp.logical_and(matching, earlier).astype(jnp.int32), axis=1)


def angle_tables(segment):
    places = positions_of(segment).astype(jnp.float32)
    midpoint = HEAD // 2
    inverse = 10000.0 ** (-jnp.arange(midpoint).astype(jnp.float32) * 2.0 / HEAD)
    angles = places[:, None] * inverse[None, :]
    return (jnp.cos(angles)[:, None, :], jnp.sin(angles)[:, None, :])


def key_mask(segment):
    places = jnp.arange(segment.shape[0])
    matching = segment[:, None] == segment[None, :]
    allowed = matching & (segment[None, :] >= 0) & (places[None, :] <= places[:, None])
    return allowed | (places[None, :] == places[:, None])


def contract_rows(left, right):
    return lax.dot_general(
        left, right, (((0,), (0,)), ((), ())), preferred_element_type=jnp.float32
    )


def times_transpose(left, right):
    return lax.dot_general(
        left, right, (((1,), (1,)), ((), ())), preferred_element_type=jnp.float32
    )


def product(left, right):
    return jnp.dot(left, right, preferred_element_type=jnp.float32)


def column_sums(values):
    return jnp.sum(values.astype(jnp.float32), axis=0)


def masked_scores(query_rot, key_rot, allowed):
    scores = (
        jnp.einsum("qhd,khd->hqk", query_rot, key_rot, preferred_element_type=jnp.float32) * 0.125
    )
    return jnp.where(allowed[None], scores, -1e30)


class Net:
    def __init__(self, wide):
        self.wide = wide
        self.me = lax.axis_index("wide")
        self.core = lax.axis_index("narrow")
        outer = []
        mask = wide // 2
        while mask > 2:
            outer.append(mask)
            mask //= 2
        self.outer = outer

    def swap(self, value, mask):
        pairs = [(d, d ^ mask) for d in range(self.wide)]
        return lax.ppermute(value, "wide", pairs)

    def sibling(self, value):
        return lax.ppermute(value, "narrow", [(0, 1), (1, 0)])

    def bit(self, mask):
        return (self.me & mask) != 0

    def grow(self, value, mask, axis):
        other = self.swap(value, mask)
        bit = self.bit(mask)
        low = jnp.where(bit, other, value)
        high = jnp.where(bit, value, other)
        return jnp.stack([low, high], axis=axis)

    def shrink(self, value, mask, axis):
        bit = self.bit(mask).astype(jnp.int32)
        mine = lax.dynamic_index_in_dim(value, bit, axis, keepdims=False)
        theirs = lax.dynamic_index_in_dim(value, 1 - bit, axis, keepdims=False)
        other = self.swap(theirs, mask)
        return (mine.astype(jnp.float32) + other.astype(jnp.float32)).astype(jnp.bfloat16)

    def gather(self, first, second):
        r, c = first.shape
        both = jnp.stack([first, second])[None]
        for mask in self.outer:
            both = self.grow(both, mask, 1).reshape(-1, 2, r, c)
        outer = both.shape[0]
        a = self.grow(both[:, 0], 1, 1)
        a = self.grow(a, 2, 1)
        b = self.grow(both[:, 1], 2, 1)
        b = self.grow(b, 1, 2)
        return jnp.stack([a, b], axis=3).reshape(outer * 4 * 2 * r, c)

    def scatter(self, full):
        rows, c = full.shape
        r = rows // (self.wide * 2)
        outer = self.wide // 4
        parts = full.reshape(outer, 2, 2, 2, r, c)
        a, b = parts[:, :, :, 0], parts[:, :, :, 1]
        a = self.shrink(self.shrink(a, 2, 1), 1, 1)
        b = self.shrink(self.shrink(b, 1, 2), 2, 1)
        both = jnp.stack([a, b], axis=1)
        for mask in reversed(self.outer):
            count = both.shape[0] // 2
            both = self.shrink(both.reshape(count, 2, 2, r, c), mask, 1)
        return both[0, 0], both[0, 1]

    def gather_small(self, value):
        other = self.sibling(value)
        core = self.core == 1
        buf = jnp.stack([jnp.where(core, other, value), jnp.where(core, value, other)])[None]
        for mask in [1, 2] + self.outer[::-1]:
            buf = self.grow(buf, mask, 0).reshape(1, -1, *value.shape)
        return buf[0]

    def total(self, value):
        value = value + self.sibling(value)
        for mask in [1, 2] + self.outer[::-1]:
            value = value + self.swap(value, mask)
        return value

    def pick(self, value, axis):
        mine = lax.dynamic_index_in_dim(value, self.core, axis, keepdims=False)
        theirs = lax.dynamic_index_in_dim(value, 1 - self.core, axis, keepdims=False)
        return mine, theirs

    def halves(self, mine, theirs):
        core = self.core == 1
        return jnp.where(core, theirs, mine), jnp.where(core, mine, theirs)

    def columns_in(self, shard):
        mine, theirs = self.pick(shard, 1)
        return self.halves(mine, self.sibling(theirs))

    def columns_out(self, first, second):
        mine, theirs = self.pick(jnp.stack([first, second]), 0)
        other = self.sibling(theirs)
        left, right = self.halves(mine, other)
        return jnp.stack([left, right], axis=1)


def shards_any(
    activations,
    segment_ids,
    cotangent,
    querymat,
    keymat,
    valuemat,
    outmat,
    upmatrix,
    downmatrix,
    querybias,
    keybias,
    valuebias,
    outbias,
    upbias,
    downbias,
    firstgain,
    secondgain,
    thirdgain,
    fourthgain,
):
    wide = lax.axis_size("wide")
    net = Net(wide)
    core = net.core
    length, width = activations.shape
    rows = querymat.shape[0]
    hidden = upmatrix.shape[1]
    block = hidden // (2 * wide)
    half = width // 2
    heads = width // HEAD
    f32 = jnp.float32
    bf16 = jnp.bfloat16

    nine = [querybias, keybias, valuebias, outbias, downbias, firstgain, secondgain, thirdgain, fourthgain]
    small = jnp.concatenate([jnp.concatenate(nine), upbias])
    qkv_shard = jnp.concatenate(
        [m.reshape(rows, 2, half) for m in (querymat, keymat, valuemat)], axis=2
    )
    up_shard = upmatrix.reshape(rows, wide, 2, block).transpose(0, 2, 1, 3).reshape(rows, 2, hidden // 2)
    out_shard = outmat.reshape(rows, 2, half)
    small_all = net.gather_small(small)
    qkv_mine = net.gather(*net.columns_in(qkv_shard))
    out_mine = net.gather(*net.columns_in(out_shard))
    up_mine = net.gather(*net.columns_in(up_shard))
    down_rows = downmatrix.shape[0]
    down_mine = net.gather(downmatrix[: down_rows // 2], downmatrix[down_rows // 2 :])
    qkv_theirs, out_theirs, up_theirs, down_theirs = map(
        net.sibling, (qkv_mine, out_mine, up_mine, down_mine)
    )

    vectors = small_all[:, : 9 * rows].reshape(-1, 9, rows).transpose(1, 0, 2).reshape(9, width)
    vectors = vectors.astype(f32)
    bias_query, bias_key, bias_value, bias_output, bias_down = (vectors[i] for i in range(5))
    gain_first, gain_second, gain_third, gain_fourth = (vectors[i] for i in range(5, 9))
    bias_up_pair = small_all[:, 9 * rows :].reshape(wide, 2, block).astype(f32)
    bias_up_mine, bias_up_theirs = (v.reshape(-1) for v in net.pick(bias_up_pair, 1))

    def natural(mine, theirs):
        return jnp.where(
            core == 1,
            jnp.concatenate([theirs, mine], axis=-1),
            jnp.concatenate([mine, theirs], axis=-1),
        )

    inputs = activations.astype(f32)
    cosine, sine = angle_tables(segment_ids)
    allowed = key_mask(segment_ids)
    valid_row = (segment_ids >= 0).astype(f32)
    normed_in, pull_first = jax.vjp(rms_norm, inputs, gain_first)
    normed_low = normed_in.astype(bf16)
    normed_low_theirs = net.sibling(normed_low)
    qkv_m = product(normed_low, qkv_mine)
    qkv_t = product(normed_low, qkv_theirs)
    queries, keys_pre, values_pre = (
        natural(qkv_m[:, i * half : (i + 1) * half], qkv_t[:, i * half : (i + 1) * half]) + b
        for i, b in enumerate((bias_query, bias_key, bias_value))
    )
    query_rot = rotate(queries.reshape(length, heads, HEAD), cosine, sine).astype(bf16)
    key_rot = rotate(keys_pre.reshape(length, heads, HEAD), cosine, sine).astype(bf16)
    value_low = values_pre.reshape(length, heads, HEAD).astype(bf16)
    scores = masked_scores(query_rot, key_rot, allowed)
    peak = jnp.max(scores, axis=-1, keepdims=True)
    exponent = jnp.exp(scores - peak)
    totals = jnp.sum(exponent, axis=-1, keepdims=True)
    logsum = peak + jnp.log(totals)
    probs = exponent / totals
    mixed = jnp.einsum(
        "hqk,khd->qhd", probs.astype(bf16), value_low, preferred_element_type=f32
    )
    mixed_low = mixed.reshape(length, width).astype(bf16)
    mixed_low_theirs = net.sibling(mixed_low)
    attended = natural(product(mixed_low, out_mine), product(mixed_low, out_theirs)) + bias_output
    normed_att, pull_second = jax.vjp(rms_norm, attended, gain_second)
    middle = inputs + normed_att
    normed_mid, pull_third = jax.vjp(rms_norm, middle, gain_third)
    normed_mid_low = normed_mid.astype(bf16)
    normed_mid_low_theirs = net.sibling(normed_mid_low)
    act_m_f, pull_gelu_m = jax.vjp(jax.nn.gelu, product(normed_mid_low, up_mine) + bias_up_mine)
    act_t_f, pull_gelu_t = jax.vjp(jax.nn.gelu, product(normed_mid_low, up_theirs) + bias_up_theirs)
    act_m = act_m_f.astype(bf16)
    act_t = act_t_f.astype(bf16)
    act_other = net.sibling(act_t)
    contracted = product(act_m, down_mine) + product(act_t, down_theirs) + bias_down
    local_power = jnp.sum(valid_row * jnp.mean(contracted * contracted, axis=-1))
    normed_out, pull_fourth = jax.vjp(rms_norm, contracted, gain_fourth)
    layer_out = (middle + normed_out).astype(bf16)

    seed = cotangent.astype(f32) * valid_row[:, None]
    d_contracted_f, fourth_slope = pull_fourth(seed)
    d_contracted = d_contracted_f.astype(bf16)
    d_contracted_theirs = net.sibling(d_contracted)
    down_bias_slope = column_sums(d_contracted)
    d_exp_m = pull_gelu_m(times_transpose(d_contracted, down_mine))[0].astype(bf16)
    d_exp_t = pull_gelu_t(times_transpose(d_contracted, down_theirs))[0].astype(bf16)
    d_exp_other = net.sibling(d_exp_t)

    def both_rows(a, b):
        return jnp.concatenate([a, b], axis=0)

    down_slope = contract_rows(
        both_rows(act_m, act_other), both_rows(d_contracted, d_contracted_theirs)
    ).astype(bf16)
    down_sum = net.scatter(down_slope)
    up_slope = contract_rows(
        both_rows(normed_mid_low, normed_mid_low_theirs), both_rows(d_exp_m, d_exp_other)
    ).astype(bf16)
    up_sum = net.scatter(up_slope)
    up_bias_m, up_bias_t = column_sums(d_exp_m), column_sums(d_exp_t)
    d_normed_mid = times_transpose(d_exp_m, up_mine) + times_transpose(d_exp_t, up_theirs)
    d_middle_part, third_slope = pull_third(d_normed_mid)
    d_middle = seed + d_middle_part
    d_attended_f, second_slope = pull_second(d_middle)
    d_attended = d_attended_f.astype(bf16)
    output_bias_slope = column_sums(d_attended)
    d_att_m, d_att_t = net.pick(d_attended.reshape(length, 2, half), 1)
    d_att_other = net.sibling(d_att_t)
    out_slope = contract_rows(
        both_rows(mixed_low, mixed_low_theirs), both_rows(d_att_m, d_att_other)
    ).astype(bf16)
    out_sum = net.scatter(out_slope)
    d_mixed = (
        (times_transpose(d_att_m, out_mine) + times_transpose(d_att_t, out_theirs))
        .astype(bf16)
        .reshape(length, heads, HEAD)
    )
    probs_again = jnp.exp(masked_scores(query_rot, key_rot, allowed) - logsum)
    d_values = jnp.einsum(
        "hqk,qhd->khd", probs_again.astype(bf16), d_mixed, preferred_element_type=f32
    )
    d_probs = jnp.einsum("qhd,khd->hqk", d_mixed, value_low, preferred_element_type=f32)
    row_terms = jnp.sum(probs_again * d_probs, axis=-1, keepdims=True)
    d_scores = (probs_again * (d_probs - row_terms)).astype(bf16)
    d_query_rot = (
        jnp.einsum("hqk,khd->qhd", d_scores, key_rot, preferred_element_type=f32) * 0.125
    )
    d_key_rot = (
        jnp.einsum("hqk,qhd->khd", d_scores, query_rot, preferred_element_type=f32) * 0.125
    )
    d_queries = rotate(d_query_rot, cosine, -sine).reshape(length, width).astype(bf16)
    d_keys = rotate(d_key_rot, cosine, -sine).reshape(length, width).astype(bf16)
    d_values_low = d_values.reshape(length, width).astype(bf16)
    pairs = [net.pick(v.reshape(length, 2, half), 1) for v in (d_queries, d_keys, d_values_low)]
    d_qkv_m = jnp.concatenate([p[0] for p in pairs], axis=1)
    d_qkv_t = jnp.concatenate([p[1] for p in pairs], axis=1)
    d_qkv_other = net.sibling(d_qkv_t)
    qkv_slope = contract_rows(
        both_rows(normed_low, normed_low_theirs), both_rows(d_qkv_m, d_qkv_other)
    ).astype(bf16)
    qkv_sum = net.scatter(qkv_slope)
    d_normed = times_transpose(d_qkv_m, qkv_mine) + times_transpose(d_qkv_t, qkv_theirs)
    d_inputs_part, first_slope = pull_first(d_normed)
    input_gradient = d_middle + d_inputs_part

    up_bias_low = jnp.where(core == 1, up_bias_t, up_bias_m).reshape(wide, 1, block)
    up_bias_high = jnp.where(core == 1, up_bias_m, up_bias_t).reshape(wide, 1, block)
    up_bias_slope = jnp.concatenate([up_bias_low, up_bias_high], axis=1).reshape(-1)
    small_slopes = jnp.concatenate(
        [
            column_sums(d_queries),
            column_sums(d_keys),
            column_sums(d_values_low),
            output_bias_slope,
            down_bias_slope,
            first_slope,
            second_slope,
            third_slope,
            fourth_slope,
            up_bias_slope,
            jnp.full((128,), local_power, f32),
        ]
    )
    sums = net.total(small_slopes)
    output_power = sums[-1] / (length * wide * 2)
    device = net.me * 2 + core
    own = lax.dynamic_slice_in_dim(sums[: 9 * width].reshape(9, width), device * rows, rows, 1)
    own_up = lax.dynamic_slice_in_dim(sums[9 * width : 9 * width + hidden], device * 2 * block // 2, block, 0)

    qkv_grad = net.columns_out(*qkv_sum).astype(f32)
    out_grad = net.columns_out(*out_sum).astype(f32).reshape(rows, width)
    up_grad = net.columns_out(*up_sum).astype(f32)
    up_grad = up_grad.reshape(rows, 2, wide, block).transpose(0, 2, 1, 3).reshape(rows, hidden)
    down_grad = jnp.concatenate(down_sum, axis=0).astype(f32)
    q_grad, k_grad, v_grad = (
        qkv_grad[:, :, i * half : (i + 1) * half].reshape(rows, width) for i in range(3)
    )
    return (
        layer_out,
        input_gradient,
        q_grad,
        k_grad,
        v_grad,
        out_grad,
        up_grad,
        down_grad,
        own[0],
        own[1],
        own[2],
        own[3],
        own_up,
        own[4],
        own[5],
        own[6],
        own[7],
        own[8],
        output_power,
    )


F32 = jnp.float32
BF16 = jnp.bfloat16
I32 = jnp.int32
EPS = 1e-06
VMEM_LIMIT = 60 * 1024 * 1024
LANES = 128
GELU_A = 0.7978845608028654
GELU_B = 0.044715
TILE = 128
DOWN_CHIPS = 4


def whole_spec():
    return pl.BlockSpec(memory_space=pltpu.VMEM)


def hbm_spec():
    return pl.BlockSpec(memory_space=pl.ANY)


def smem_spec():
    return pl.BlockSpec(memory_space=pltpu.SMEM)


def params():
    return pltpu.CompilerParams(vmem_limit_bytes=VMEM_LIMIT)


def shape(dims, dtype):
    return jax.ShapeDtypeStruct(dims, dtype)


def cost(flops, bytes_accessed):
    return pl.CostEstimate(flops=flops, bytes_accessed=bytes_accessed, transcendentals=0)


def dot(a, b):
    return lax.dot_general(a, b, (((1,), (0,)), ((), ())), preferred_element_type=F32)


def dot_t(a, b):
    return lax.dot_general(a, b, (((1,), (1,)), ((), ())), preferred_element_type=F32)


def t_dot(a, b):
    return lax.dot_general(a, b, (((0,), (0,)), ((), ())), preferred_element_type=F32)


def pair_mask(place):
    return place // 4 + 4 * (place % 4)


def assemble(where, pieces, target, sems, cols):
    copies = []
    for e in range(2):
        place = 0
        for piece in pieces[e * 5 : e * 5 + 5]:
            for j in range(piece.shape[0]):
                chip = where[0] ^ pair_mask(place)
                source = piece.at[j, :, pl.ds(*cols)]
                dest = target.at[chip, where[1] ^ e]
                copies.append(pltpu.make_async_copy(source, dest, sems.at[len(copies)]))
                place += 1
    for copy in copies:
        copy.start()
    return copies


def wait_all(copies):
    for copy in copies:
        copy.wait()


def fetch(sources, targets, sems, base=0):
    copies = [
        pltpu.make_async_copy(a, b, sems.at[base + i]) for i, (a, b) in enumerate(zip(sources, targets))
    ]
    for copy in copies:
        copy.start()
    return copies


def matrix(buf):
    return buf[...].reshape(-1, buf.shape[-1])


def inverse_rms(v):
    return lax.rsqrt(jnp.mean(v * v, axis=-1, keepdims=True) + EPS)


def place_rows(first, rows):
    n = rows[0].shape[1]
    at = lax.broadcasted_iota(I32, (8, n), 0)
    out = jnp.zeros((8, n), F32)
    for i, row in enumerate(rows):
        out = jnp.where(at == first + i, jnp.broadcast_to(row, (8, n)), out)
    return out


def rms_back(v, r, gain, e):
    ge = gain * e
    return r * ge - v * (r * r * r) * jnp.mean(v * ge, axis=-1, keepdims=True)


def row_sum(v):
    return jnp.sum(v, axis=0, keepdims=True)


def turn(v, cosine, sine):
    lane = lax.broadcasted_iota(I32, v.shape, 1)
    swapped = jnp.where((lane & 63) < 32, pltpu.roll(v, 96, 1), pltpu.roll(v, 32, 1))
    return v * cosine + swapped * sine


def project_kernel(parts, where, x, bias, *refs):
    pieces = refs[:10]
    tables = refs[10:-3]
    out, wbuf, sems = refs[-3:]
    width = x.shape[1]
    copies = [
        assemble(where, pieces, wbuf.at[i], sems.at[i], (i * width, width)) for i in range(parts)
    ]
    for i in range(parts):
        wait_all(copies[i])
        for c in range(0, width, 512):
            y = dot(x[...], wbuf[i, :, :, :, c : c + 512].reshape(width, 512))
            y = y + bias[:, i * width + c : i * width + c + 512]
            at = i * width + c
            if tables:
                cosine, sine = tables[0][...], tables[1][...]
                for b in range(0, 512, LANES):
                    z = turn(y[:, b : b + LANES], cosine, sine)
                    z = z * 0.125 if i == 0 else z
                    out[:, at + b : at + b + LANES] = z.astype(BF16)
            else:
                out[:, at : at + 512] = y.astype(BF16)


def project(where, x, pieces, parts, bias, tables=()):
    t, width = x.shape
    r = pieces[0].shape[1]
    return pl.pallas_call(
        functools.partial(project_kernel, parts),
        in_specs=[smem_spec(), whole_spec(), whole_spec()]
        + [hbm_spec()] * 10
        + [whole_spec()] * len(tables),
        out_specs=whole_spec(),
        out_shape=shape((t, parts * width), BF16),
        scratch_shapes=[
            pltpu.VMEM((parts, 16, 2, r, width), BF16),
            pltpu.SemaphoreType.DMA((parts, 32)),
        ],
        compiler_params=params(),
        cost_estimate=cost(2 * t * width * parts * width, 2 * parts * width * width),
        name="project",
    )(where, x, bias, *pieces, *tables)


def open_mask(col_ref, row_ref, open_ref):
    t = open_ref.shape[0]

    @pl.when(pl.program_id(0) == 0)
    def _():
        rows = lax.broadcasted_iota(I32, (t, t), 0)
        cols = lax.broadcasted_iota(I32, (t, t), 1)
        ok = (col_ref[...] == row_ref[...]) & (cols <= rows)
        open_ref[...] = jnp.where(ok, 0.0, -1e30)


def one_head(v, h):
    lane = lax.broadcasted_iota(I32, v.shape, 1)
    return jnp.where((lane < HEAD) == (h == 0), v, jnp.zeros_like(v))


def attend_kernel(q_ref, k_ref, v_ref, col_ref, row_ref, out_ref, lse_ref, open_ref):
    t = q_ref.shape[0]
    tile = TILE
    open_mask(col_ref, row_ref, open_ref)
    left = lax.broadcasted_iota(I32, (tile, LANES), 1) < HEAD
    spans = [(slice(i * tile, (i + 1) * tile), (i + 1) * tile) for i in range(t // tile)]
    pairs = [(rows, seen, h) for rows, seen in spans for h in range(2)]
    scores = [
        dot_t(one_head(q_ref[rows, :], h), k_ref[:seen, :]) + open_ref[rows, :seen]
        for rows, seen, h in pairs
    ]
    peaks = [jnp.max(s, axis=-1, keepdims=True) for s in scores]
    powers = [jnp.exp(s - peak) for s, peak in zip(scores, peaks)]
    totals = [jnp.sum(e, axis=-1, keepdims=True) for e in powers]
    outs = [
        dot(e.astype(BF16), v_ref[:seen, :]) / total
        for e, total, (rows, seen, h) in zip(powers, totals, pairs)
    ]
    sums = [peak + jnp.log(total) for peak, total in zip(peaks, totals)]
    for i, (rows, seen) in enumerate(spans):
        out_ref[rows, :] = jnp.where(left, outs[2 * i], outs[2 * i + 1]).astype(BF16)
        lse_ref[rows, :] = jnp.where(left, sums[2 * i], sums[2 * i + 1])


def attend(qk, v, col, row):
    t, width = v.shape
    steps = width // LANES
    block = lambda f: pl.BlockSpec((t, LANES), f)
    return pl.pallas_call(
        attend_kernel,
        grid=(steps,),
        in_specs=[
            block(lambda i: (0, i)),
            block(lambda i: (0, i + steps)),
            block(lambda i: (0, i)),
            pl.BlockSpec((t, 1), lambda i: (0, 0)),
            pl.BlockSpec((1, t), lambda i: (0, 0)),
        ],
        out_specs=[block(lambda i: (0, i))] * 2,
        out_shape=[shape((t, width), BF16), shape((t, width), F32)],
        scratch_shapes=[pltpu.VMEM((t, t), F32)],
        compiler_params=params(),
        cost_estimate=cost(4 * t * t * width, 10 * t * width),
        name="attend",
    )(qk, qk, v, col, row)


def attend_back_kernel(
    q_ref, k_ref, v_ref, dm_ref, lse_ref, col_ref, row_ref, cos_ref, sin_ref,
    d_ref, sum_ref, open_ref,
):
    t = q_ref.shape[0]
    tile = TILE
    open_mask(col_ref, row_ref, open_ref)
    left = lax.broadcasted_iota(I32, (tile, LANES), 1) < HEAD
    spans = [(slice(i * tile, (i + 1) * tile), (i + 1) * tile) for i in range(t // tile)]
    pairs = [(rows, seen, h) for rows, seen in spans for h in range(2)]
    scores = [
        dot_t(one_head(q_ref[rows, :], h), k_ref[:seen, :]) + open_ref[rows, :seen]
        for rows, seen, h in pairs
    ]
    d_probs = [dot_t(one_head(dm_ref[rows, :], h), v_ref[:seen, :]) for rows, seen, h in pairs]
    probs = [
        jnp.exp(s - lse_ref[rows, h * HEAD : h * HEAD + 1])
        for s, (rows, seen, h) in zip(scores, pairs)
    ]
    deltas = [jnp.sum(p * dp, axis=-1, keepdims=True) for p, dp in zip(probs, d_probs)]
    d_scores = [(p * (dp - d)).astype(BF16) for p, dp, d in zip(probs, d_probs, deltas)]
    probs = [p.astype(BF16) for p in probs]
    dq = [dot(ds, k_ref[:seen, :]) for ds, (rows, seen, h) in zip(d_scores, pairs)]
    total_q = jnp.zeros((1, LANES), F32)
    for i, (rows, seen) in enumerate(spans):
        v = jnp.where(left, dq[2 * i], dq[2 * i + 1]) * 0.125
        v = turn(v, cos_ref[rows, :], -sin_ref[rows, :]).astype(BF16)
        d_ref[0, rows, :] = v
        total_q += row_sum(v.astype(F32))
    totals = [total_q]
    for at, lhs, rhs in ((1, d_scores, q_ref), (2, probs, dm_ref)):
        total = jnp.zeros((1, LANES), F32)
        parts = [t_dot(a, rhs[rows, :]) for a, (rows, seen, h) in zip(lhs, pairs)]
        for i, (keys, _) in enumerate(spans):
            heads = [
                sum(parts[2 * j + h][keys] for j in range(i, len(spans))) for h in range(2)
            ]
            v = jnp.where(left, heads[0], heads[1])
            if at == 1:
                v = turn(v, cos_ref[keys, :], -sin_ref[keys, :])
            v = v.astype(BF16)
            d_ref[at, keys, :] = v
            total += row_sum(v.astype(F32))
        totals.append(total)
    sum_ref[...] = place_rows(0, totals)


def attend_back(qk, v, dm, lse, col, row, cosine, sine, first, steps):
    t, width = v.shape
    key = width // LANES
    part = steps * LANES
    block = lambda f: pl.BlockSpec((t, LANES), f)
    fixed = lambda a: pl.BlockSpec(a.shape, lambda i: (0, 0))
    here = block(lambda i: (0, i))
    read = block(lambda i: (0, i + first))
    return pl.pallas_call(
        attend_back_kernel,
        grid=(steps,),
        in_specs=[read, block(lambda i: (0, i + first + key)), read, read, read]
        + [fixed(a) for a in (col, row, cosine, sine)],
        out_specs=[
            pl.BlockSpec((3, t, LANES), lambda i: (0, 0, i)),
            pl.BlockSpec((8, LANES), lambda i: (0, i)),
        ],
        out_shape=[shape((3, t, part), BF16), shape((8, part), F32)],
        scratch_shapes=[pltpu.VMEM((t, t), F32)],
        compiler_params=params(),
        cost_estimate=cost(10 * t * t * part, 18 * t * part),
        name="attend_back",
    )(qk, qk, v, dm, lse, col, row, cosine, sine)


def out_kernel(where, mixed, order, x, bias, g2, g3, *refs):
    pieces = refs[:10]
    m_own, m_sib, att_ref, mid_ref, n_ref, n_own, n_sib, wbuf, sems = refs[10:]
    t, width = mixed.shape
    half = width // 2
    copies = assemble(where, pieces, wbuf, sems, (width, width))
    turned = dot_t(order[...], mixed[...]).astype(BF16)
    m_own[...] = turned[:half]
    m_sib[...] = turned[half:]
    wait_all(copies)
    w = matrix(wbuf)
    tile = 256
    for i in range(t // tile):
        rows = slice(i * tile, (i + 1) * tile)
        att = dot(mixed[rows, :], w) + bias[...]
        att_ref[rows, :] = att
        mid = x[rows, :].astype(F32) + att * inverse_rms(att) * g2[...]
        mid_ref[rows, :] = mid
        n_ref[rows, :] = (mid * inverse_rms(mid) * g3[...]).astype(BF16)
    turned = dot_t(order[...], n_ref[...]).astype(BF16)
    n_own[...] = turned[:half]
    n_sib[...] = turned[half:]


def out_project(where, mixed, order, x, bias, g2, g3, pieces):
    t, width = mixed.shape
    half = width // 2
    r = pieces[0].shape[1]
    halves = [shape((half, t), BF16)] * 2
    return pl.pallas_call(
        out_kernel,
        in_specs=[smem_spec()] + [whole_spec()] * 6 + [hbm_spec()] * 10,
        out_specs=[whole_spec()] * 7,
        out_shape=halves + [shape((t, width), F32)] * 2 + [shape((t, width), BF16)] + halves,
        scratch_shapes=[pltpu.VMEM((16, 2, r, width), BF16), pltpu.SemaphoreType.DMA((32,))],
        compiler_params=params(),
        cost_estimate=cost(6 * t * width * width, 16 * t * width),
        name="out_project",
    )(where, mixed, order, x, bias, g2, g3, *pieces)


def feed_kernel(
    where, x, b_up, w_up, w_down, b_down, valid, g4, mid_hbm, cot_hbm,
    a_own, a_sib, slope_ref, out_ref, dc_ref, sums_ref, power_ref, act_buf, acc, mid, cot, sems,
):
    step = pl.program_id(0)
    t, width = acc.shape
    first = where[1] == 0
    copies = [
        pltpu.make_async_copy(mid_hbm, mid, sems.at[0]),
        pltpu.make_async_copy(cot_hbm, cot, sems.at[1]),
    ]

    @pl.when(step == 0)
    def _():
        for copy in copies:
            copy.start()

    for j in range(w_up.shape[3] // 256):
        cols = slice(j * 256, (j + 1) * 256)
        y = dot(x[...], w_up[:, 0, :, cols].reshape(width, 256)) + b_up[:, cols]
        yy = y * y
        h = 0.5 * jnp.tanh(y * (GELU_A + (GELU_A * GELU_B) * yy)) + 0.5
        act = y * h
        slope = h + act * (1.0 - h) * (2 * GELU_A + (6 * GELU_A * GELU_B) * yy)
        act = act.astype(BF16)
        act_buf[:, cols] = act
        slope_ref[:, cols] = slope.astype(BF16)
        dst = slice(j * 128, (j + 1) * 128)
        a0, a1 = act[:, :128], act[:, 128:]
        a_own[:, dst] = jnp.where(first, a0, a1)
        a_sib[:, dst] = jnp.where(first, a1, a0)
    y = dot(act_buf[...], w_down[...].reshape(-1, width))

    @pl.when(step == 0)
    def _():
        acc[...] = y + b_down[...]

    @pl.when(step > 0)
    def _():
        acc[...] += y

    @pl.when(step == pl.num_programs(0) - 1)
    def _():
        wait_all(copies)
        tile = 128
        power = jnp.zeros((1, 1), F32)
        gain_sum = jnp.zeros((1, width), F32)
        bias_sum = jnp.zeros((1, width), F32)
        gain = g4[...]
        for i in range(t // tile):
            rows = slice(i * tile, (i + 1) * tile)
            v = acc[rows, :]
            ok = valid[rows, :]
            mean = jnp.mean(v * v, axis=-1, keepdims=True)
            power += row_sum(mean * ok)
            r = lax.rsqrt(mean + EPS)
            vr = v * r
            out_ref[rows, :] = (mid[rows, :] + vr * gain).astype(BF16)
            seed = cot[rows, :].astype(F32) * ok
            gain_sum += row_sum(vr * seed)
            dc = rms_back(v, r, gain, seed).astype(BF16)
            dc_ref[rows, :] = dc
            bias_sum += row_sum(dc.astype(F32))
        sums_ref[...] = place_rows(6, [gain_sum, bias_sum])
        power_ref[...] = jnp.broadcast_to(power, power_ref.shape)


def feed_forward(where, x, b_up, b_down, mid, cot, valid, g4, ffn):
    t, width = x.shape
    hidden = b_up.shape[1]
    devices, _, r, tn = ffn.shape
    steps = hidden // tn
    fixed = lambda a: pl.BlockSpec(a.shape, lambda i: (0, 0))
    tile = lambda n: pl.BlockSpec((t, n), lambda i: (0, i))
    return pl.pallas_call(
        feed_kernel,
        grid=(steps,),
        in_specs=[
            smem_spec(),
            fixed(x),
            pl.BlockSpec((1, tn), lambda i: (0, i)),
            pl.BlockSpec((devices, 1, r, tn), lambda i: (0, i, 0, 0)),
            pl.BlockSpec((devices // steps, 4, r, width), lambda i: (i, 1, 0, 0)),
            fixed(b_down),
            fixed(valid),
            fixed(g4),
            hbm_spec(),
            hbm_spec(),
        ],
        out_specs=[tile(tn // 2), tile(tn // 2), tile(tn)]
        + [pl.BlockSpec((t, width), lambda i: (0, 0))] * 2
        + [pl.BlockSpec((8, width), lambda i: (0, 0)), pl.BlockSpec((1, LANES), lambda i: (0, 0))],
        out_shape=[shape((t, hidden // 2), BF16)] * 2
        + [shape((t, hidden), BF16)]
        + [shape((t, width), BF16)] * 2
        + [shape((8, width), F32), shape((1, LANES), F32)],
        scratch_shapes=[
            pltpu.VMEM((t, tn), BF16),
            pltpu.VMEM((t, width), F32),
            pltpu.VMEM((t, width), F32),
            pltpu.VMEM((t, width), BF16),
            pltpu.SemaphoreType.DMA((2,)),
        ],
        compiler_params=params(),
        cost_estimate=cost(4 * t * width * hidden, 4 * width * hidden + 8 * t * hidden),
        name="feed_forward",
    )(where, x, b_up, ffn, ffn, b_down, valid, g4, mid, cot)


def block_at(ref, where, place):
    chip = where[0] ^ pair_mask(place)
    return ref.at[:, pl.ds(pl.multiple_of(chip * LANES, LANES), LANES)]


def down_back_kernel(dc, slope, w_ref, de_ref, sums_ref):
    width = dc.shape[1]
    for j in range(w_ref.shape[0]):
        cols = slice(j * 256, (j + 1) * 256)
        y = dot_t(dc[...], w_ref[j].reshape(256, width))
        d = (y * slope[:, cols].astype(F32)).astype(BF16)
        de_ref[:, cols] = d
        sums_ref[:, cols] = row_sum(d.astype(F32))


def down_back(dc, slope, ffn):
    t, width = dc.shape
    hidden = slope.shape[1]
    r = ffn.shape[3]
    chips = DOWN_CHIPS
    tn = chips * 256
    return pl.pallas_call(
        down_back_kernel,
        grid=(hidden // tn,),
        in_specs=[
            pl.BlockSpec((t, width), lambda i: (0, 0)),
            pl.BlockSpec((t, tn), lambda i: (0, i)),
            pl.BlockSpec((chips, 2, 4, r, width), lambda i: (i, 0, 1, 0, 0)),
        ],
        out_specs=[pl.BlockSpec((t, tn), lambda i: (0, i)), pl.BlockSpec((1, tn), lambda i: (0, i))],
        out_shape=[shape((t, hidden), BF16), shape((1, hidden), F32)],
        compiler_params=params(),
        cost_estimate=cost(2 * t * hidden * width, 2 * hidden * width),
        name="down_back",
    )(dc, slope, ffn)


GRAD_PLACES = {
    "d23": (14, 15),
    "d01": (12, 13),
    "x01": (4, 5),
    "y23": (10, 11),
    "x23": (6, 7),
    "y01": (8, 9),
    "f": (0, 1, 2, 3),
}


def runs_of(places):
    return [(at, places[at : at + 2]) for at in range(0, len(places), 2)]


def slope_kernel(parts, x_own, x_oth, *refs):
    dy_own, dy_oth = refs[:parts], refs[parts : 2 * parts]
    outs = refs[2 * parts :]
    for i in range(parts):
        n = dy_own[i].shape[1]
        y = dot(x_own[...], dy_own[i][...]) + dot(x_oth[...], dy_oth[i][...])
        y = y.astype(BF16)
        for places, out in zip(GRAD_PLACES.values(), outs):
            r = out.shape[1]
            for at, run in runs_of(places):
                part = y[run[0] * r : (run[-1] + 1) * r]
                out[at : at + 2, :, i * n : (i + 1) * n] = part.reshape(2, r, n)


def row_slopes(x_own, x_oth, dy_own, dy_oth, tiles, first=0):
    half, t = x_own.shape
    r = half // 16
    n = dy_own.shape[1] // tiles
    total = n * (first + tiles)
    fixed = pl.BlockSpec((half, t), lambda i: (0, 0))
    return pl.pallas_call(
        functools.partial(slope_kernel, 1),
        grid=(tiles,),
        in_specs=[fixed] * 2 + [pl.BlockSpec((t, n), lambda i: (0, i))] * 2,
        out_specs=[pl.BlockSpec((len(p), r, n), lambda i: (0, 0, i + first)) for p in GRAD_PLACES.values()],
        out_shape=[shape((len(p), r, total), BF16) for p in GRAD_PLACES.values()],
        compiler_params=params(),
        cost_estimate=cost(4 * t * half * n * tiles, 8 * t * n * tiles + 2 * half * n * tiles),
        name="row_slopes",
    )(x_own, x_oth, dy_own, dy_oth)


def qkv_slope_kernel(x_own, x_oth, a_own, b_own, a_oth, b_oth, *refs):
    outs = refs[len(GRAD_PLACES) :]
    n = a_own.shape[2]
    for i, (own, oth) in enumerate(((a_own, a_oth), (b_own, b_oth))):
        y = dot(x_own[...], own[0]) + dot(x_oth[...], oth[0])
        y = y.astype(BF16)
        for places, out in zip(GRAD_PLACES.values(), outs):
            r = out.shape[1]
            for at, run in runs_of(places):
                part = y[run[0] * r : (run[-1] + 1) * r]
                out[at : at + 2, :, i * n : (i + 1) * n] = part.reshape(2, r, n)


def qkv_slopes(x_own, x_oth, a_own, b_own, a_oth, b_oth, pieces):
    half, t = x_own.shape
    r = half // 16
    n = a_own.shape[2]
    fixed = pl.BlockSpec((half, t), lambda i: (0, 0))
    return pl.pallas_call(
        qkv_slope_kernel,
        grid=(3,),
        in_specs=[fixed] * 2
        + [pl.BlockSpec((1, t, n), lambda i: (i, 0, 0))] * 4
        + [hbm_spec()] * len(pieces),
        out_specs=[pl.BlockSpec((len(p), r, 2 * n), lambda i: (0, 0, i)) for p in GRAD_PLACES.values()],
        out_shape=[shape(p.shape, BF16) for p in pieces],
        input_output_aliases={6 + i: i for i in range(len(pieces))},
        compiler_params=params(),
        cost_estimate=cost(24 * t * half * n, 24 * t * n + 12 * half * n),
        name="qkv_slopes",
    )(x_own, x_oth, a_own, b_own, a_oth, b_oth, *pieces)


def block_slope_kernel(where, a_own, a_oth, dy_own, dy_oth, *refs):
    outs = refs[:7]
    stage, sems = refs[7:]
    sent = []
    for places, out in zip(GRAD_PLACES.values(), outs):
        for at, run in runs_of(places):
            i = len(sent)
            mine, other = (
                jnp.concatenate([block_at(act, where, p)[...] for p in run], axis=1)
                for act in (a_own, a_oth)
            )
            y = t_dot(mine, dy_own[...]) + t_dot(other, dy_oth[...])
            stage[i] = y.astype(BF16).reshape(2, LANES, y.shape[1])
            copy = pltpu.make_async_copy(stage.at[i], out.at[pl.ds(at, 2)], sems.at[i])
            copy.start()
            sent.append(copy)
    wait_all(sent)


def block_slopes(where, a_own, a_oth, dy_own, dy_oth):
    t, half = a_own.shape
    width = dy_own.shape[1]
    return pl.pallas_call(
        block_slope_kernel,
        in_specs=[smem_spec()] + [whole_spec()] * 4,
        out_specs=[hbm_spec()] * 7,
        out_shape=[shape((len(p), LANES, width), BF16) for p in GRAD_PLACES.values()],
        scratch_shapes=[pltpu.VMEM((8, 2, LANES, width), BF16), pltpu.SemaphoreType.DMA((8,))],
        compiler_params=params(),
        cost_estimate=cost(4 * t * half * width, 4 * t * (half + width) + 2 * half * width),
        name="block_slopes",
    )(where, a_own, a_oth, dy_own, dy_oth)


def up_back_kernel(where, de, valid, g2_ref, g3_ref, w_ref, mid_hbm, att_hbm, cot_hbm, *refs):
    pieces = refs[:10]
    dmid_hbm, datt_hbm, dmix_ref, sums_ref, acc, wbuf, mid_buf, att_buf, cot_buf, dmid_ref, datt_ref, sems = refs[10:]
    step = pl.program_id(0)
    t, width = acc.shape

    @pl.when(step == 0)
    def _():
        assemble(where, pieces, wbuf, sems, (width, width))
        fetch((mid_hbm, att_hbm, cot_hbm), (mid_buf, att_buf, cot_buf), sems, 32)

    y = dot_t(de[...], w_ref[:, 0].reshape(width, -1))

    @pl.when(step == 0)
    def _():
        acc[...] = y

    @pl.when(step > 0)
    def _():
        acc[...] += y

    @pl.when(step == pl.num_programs(0) - 1)
    def _():
        for i in range(32):
            pltpu.make_async_copy(pieces[0].at[0, :, pl.ds(width, width)], wbuf.at[0, 0], sems.at[i]).wait()
        for i, (a, b) in enumerate(((mid_hbm, mid_buf), (att_hbm, att_buf), (cot_hbm, cot_buf))):
            pltpu.make_async_copy(a, b, sems.at[32 + i]).wait()
        tile = 128
        g2, g3 = g2_ref[...], g3_ref[...]
        w = matrix(wbuf)
        sent = []
        sums = [jnp.zeros((1, width), F32)] * 3
        for i in range(t // tile):
            rows = slice(i * tile, (i + 1) * tile)
            e = acc[rows, :]
            mid = mid_buf[rows, :]
            r3 = inverse_rms(mid)
            dmid = cot_buf[rows, :].astype(F32) * valid[rows, :] + rms_back(mid, r3, g3, e)
            dmid_ref[rows, :] = dmid
            att = att_buf[rows, :]
            r2 = inverse_rms(att)
            datt = rms_back(att, r2, g2, dmid).astype(BF16)
            datt_ref[rows, :] = datt
            sums[0] += row_sum(mid * r3 * e)
            sums[1] += row_sum(att * r2 * dmid)
            sums[2] += row_sum(datt.astype(F32))
            for at, (a, b) in enumerate(((dmid_ref, dmid_hbm), (datt_ref, datt_hbm))):
                copy = pltpu.make_async_copy(a.at[rows, :], b.at[rows, :], sems.at[35 + 2 * i + at])
                copy.start()
                sent.append(copy)
        dmix_ref[...] = dot_t(datt_ref[...], w).astype(BF16)
        sums_ref[...] = place_rows(3, sums)
        wait_all(sent)


def up_back(where, de, mid, att, cot, valid, g2, g3, ffn, pieces):
    t, width = mid.shape
    hidden = de.shape[1]
    tk = ffn.shape[3]
    r = pieces[0].shape[1]
    fixed = lambda a: pl.BlockSpec(a.shape, lambda i: (0, 0))
    return pl.pallas_call(
        up_back_kernel,
        grid=(hidden // tk,),
        in_specs=[smem_spec(), pl.BlockSpec((t, tk), lambda i: (0, i))]
        + [fixed(a) for a in (valid, g2, g3)]
        + [pl.BlockSpec((ffn.shape[0], 1, ffn.shape[2], tk), lambda i: (0, i, 0, 0))]
        + [hbm_spec()] * 13,
        out_specs=[hbm_spec()] * 2
        + [pl.BlockSpec((t, width), lambda i: (0, 0)), pl.BlockSpec((8, width), lambda i: (0, 0))],
        out_shape=[shape((t, width), F32), shape((t, width), BF16), shape((t, width), BF16), shape((8, width), F32)],
        scratch_shapes=[
            pltpu.VMEM((t, width), F32),
            pltpu.VMEM((16, 2, r, width), BF16),
            pltpu.VMEM((t, width), F32),
            pltpu.VMEM((t, width), F32),
            pltpu.VMEM((t, width), BF16),
            pltpu.VMEM((t, width), F32),
            pltpu.VMEM((t, width), BF16),
            pltpu.SemaphoreType.DMA((43,)),
        ],
        compiler_params=params(),
        cost_estimate=cost(2 * t * width * hidden, 2 * width * hidden + 2 * t * hidden),
        name="up_back",
    )(where, de, valid, g2, g3, ffn, mid, att, cot, *pieces)


def in_back_kernel(where, *refs):
    d_a, d_b, x_hbm, dmid_hbm, g1_ref = refs[:5]
    qk, vo = refs[5:15], refs[15:25]
    out_ref, sums_ref, wbuf, x_buf, dmid_buf, sems = refs[25:]
    t, width = out_ref.shape
    half = width // 2
    copies = [
        assemble(where, pieces, wbuf.at[i], sems.at[i], (start, width))
        for i, (pieces, start) in enumerate(((qk, 0), (qk, width), (vo, 0)))
    ]
    late = fetch((x_hbm, dmid_hbm), (x_buf, dmid_buf), sems.at[3])
    e = None
    for i in range(3):
        wait_all(copies[i])
        d = jnp.concatenate([d_a[i], d_b[i]], axis=1)
        y = dot_t(d, wbuf[i].reshape(width, width))
        e = y if e is None else e + y
    wait_all(late)
    gain = g1_ref[...]
    tile = 128
    total = jnp.zeros((1, width), F32)
    for i in range(t // tile):
        rows = slice(i * tile, (i + 1) * tile)
        x = x_buf[rows, :].astype(F32)
        r = inverse_rms(x)
        out_ref[rows, :] = dmid_buf[rows, :] + rms_back(x, r, gain, e[rows, :])
        total += row_sum(x * r * e[rows, :])
    sums_ref[...] = total


def in_back(where, d_a, d_b, x, dmid, g1, qk_pieces, vo_pieces):
    t, width = x.shape
    r = qk_pieces[0].shape[1]
    return pl.pallas_call(
        in_back_kernel,
        in_specs=[smem_spec()] + [whole_spec()] * 2 + [hbm_spec()] * 2 + [whole_spec()] + [hbm_spec()] * 20,
        out_specs=[whole_spec()] * 2,
        out_shape=[shape((t, width), F32), shape((1, width), F32)],
        scratch_shapes=[
            pltpu.VMEM((3, 16, 2, r, width), BF16),
            pltpu.VMEM((t, width), BF16),
            pltpu.VMEM((t, width), F32),
            pltpu.SemaphoreType.DMA((4, 32)),
        ],
        compiler_params=params(),
        cost_estimate=cost(6 * t * width * width, 6 * width * width),
        name="in_back",
    )(where, d_a, d_b, x, dmid, g1, *qk_pieces, *vo_pieces)


def after(*values):
    return lax.optimization_barrier(values)


def add(*values):
    total = values[0].astype(F32)
    for v in values[1:]:
        total = total + v.astype(F32)
    return total


class Gather:
    def __init__(self, net, shard):
        self.net = net
        self.line = [shard] + [net.swap(shard, 4 * m) for m in (1, 2, 3)]

    def spread(self, line):
        net = self.net
        self.lines = jnp.stack(line)
        self.x = net.swap(self.lines, 1)
        self.y = net.swap(self.lines, 2)
        self.sib = [net.sibling(self.lines)]

    def corner(self, x, y):
        net = self.net
        self.x, self.y = x, y
        self.d01 = net.swap(x[:2], 2)
        self.d23 = net.swap(y[2:], 1)
        self.sib += [net.sibling(x), net.sibling(y)]

    def finish(self, d01, d23):
        net = self.net
        self.d01, self.d23 = d01, d23
        self.sib += [net.sibling(d01), net.sibling(d23)]

    def pieces(self):
        return [self.lines, self.x, self.y, self.d01, self.d23] + self.sib


class Scatter:
    def __init__(self, net, pieces):
        self.net = net
        self.d23, self.d01, self.x01, self.y23, self.x23, self.y01, self.f = pieces

    def a(self):
        self.got = [self.net.swap(self.d23, 1), self.net.swap(self.d01, 2)]

    def c(self, x23, y01):
        self.last = [self.net.swap(x23, 1), self.net.swap(y01, 2)]

    def fold_b(self, got):
        return [add(self.x01, got[1]).astype(BF16), add(self.y23, got[0]).astype(BF16)]

    def b(self, fold):
        self.got = [self.net.swap(fold[0], 1), self.net.swap(fold[1], 2)]

    def fold_last(self, last):
        return [add(self.f[:2], last[1]), add(self.f[2:], last[0])]

    def fold_near(self, got, part):
        low, high = add(part[0], got[0]), add(part[1], got[1])
        return [low[0], high[0], jnp.stack([low[1], high[1]]).astype(BF16)]

    def near(self, fold):
        self.low, self.high, send = fold
        self.got = [self.net.swap(send, 4)]

    def fold_far(self, got):
        return [add(self.low, got[0][0]), add(self.high, got[0][1]).astype(BF16)]

    def far(self, fold):
        self.own, send = fold
        self.got = [self.net.swap(send, 8)]

    def result(self, got):
        return add(self.own, got[0])


def shards_16(
    activations,
    segment_ids,
    cotangent,
    querymat,
    keymat,
    valuemat,
    outmat,
    upmatrix,
    downmatrix,
    querybias,
    keybias,
    valuebias,
    outbias,
    upbias,
    downbias,
    firstgain,
    secondgain,
    thirdgain,
    fourthgain,
):
    net = Net(16)
    t, width = activations.shape
    rows = querymat.shape[0]
    hidden = upmatrix.shape[1]
    block = upbias.shape[0]
    half = width // 2
    me, core = net.me, net.core
    device = me * 2 + core
    where = jnp.stack([me, core]).astype(I32)

    dst = jnp.arange(width)
    place = (dst // rows) % 16
    chip = me ^ (place // 4 + 4 * (place % 4))
    src = chip * (2 * rows) + (core ^ (dst // half)) * rows + dst % rows
    order = (src[:, None] == jnp.arange(width)[None, :]).astype(BF16)
    slots = jnp.arange(t)
    segment = jnp.where(segment_ids >= 0, segment_ids, -1 - slots)
    col, row = segment[:, None], segment[None, :]
    valid = (segment_ids >= 0).astype(F32)[:, None]
    spots = positions_of(segment_ids).astype(F32)
    inverse = 10000.0 ** (-jnp.arange(HEAD // 2).astype(F32) * 2.0 / HEAD)
    angles = spots[:, None] * inverse[None, :]
    cosine = jnp.tile(jnp.cos(angles), (1, 4))
    sine = jnp.sin(angles)
    sine = jnp.tile(jnp.concatenate([-sine, sine], axis=1), (1, 2))

    ffn_shard = jnp.concatenate(
        [upmatrix.reshape(rows, 4, width).transpose(1, 0, 2), downmatrix.reshape(4, rows, width)]
    )
    ffn = lax.all_gather(ffn_shard, AXES, axis=0, tiled=False)
    qk = Gather(net, jnp.concatenate([querymat, keymat], axis=1))
    vo_shard = jnp.concatenate([valuemat, outmat], axis=1)
    nine = [querybias, keybias, valuebias, outbias, downbias, firstgain, secondgain, thirdgain, fourthgain]
    small = jnp.concatenate([jnp.pad(v[None], ((0, 0), (0, LANES - rows))) for v in nine] + [upbias[None]])
    buf = small[None]
    buf = jnp.concatenate([buf, net.sibling(buf)])
    for mask in (1, 2, 4, 8):
        buf = jnp.concatenate([buf, net.swap(buf, mask)])
    line, buf, vo_shard = after(qk.line, buf, vo_shard)
    qk.spread(line)
    vo = Gather(net, vo_shard)

    picks = (jnp.arange(32)[:, None] ^ device) == jnp.arange(32)[None, :]
    small_all = dot(picks.astype(BF16), buf.reshape(32, -1)).reshape(32, 10, LANES)
    b_q, b_k, b_v, b_o, b_d, g1, g2, g3, g4 = (
        small_all[:, i, :rows].reshape(1, width) for i in range(9)
    )
    b_up = small_all[:, 9].reshape(1, hidden)
    inputs = activations.astype(F32)
    normed = (inputs * inverse_rms(inputs) * g1).astype(BF16)
    turned = dot_t(order, normed).astype(BF16)
    x_own, x_sib = turned[:half], turned[half:]

    x, y, line = after(qk.x, qk.y, vo.line)
    qk.corner(x, y)
    vo.spread(line)
    d01, d23, x_sib, normed, tables, vectors = after(
        qk.d01,
        qk.d23,
        x_sib,
        normed,
        (cosine, sine, col, row, valid, order),
        (b_q, b_k, b_v, b_o, b_d, g2, g3, g4, b_up),
    )
    cosine, sine, col, row, valid, order = tables
    b_q, b_k, b_v, b_o, b_d, g2, g3, g4, b_up = vectors
    qk.finish(d01, d23)
    x_oth = net.sibling(x_sib)
    x, y = after(vo.x, vo.y)
    vo.corner(x, y)
    qk_pieces = qk.pieces()
    qk_rot = project(where, normed, qk_pieces, 2, jnp.concatenate([b_q, b_k], axis=1), (cosine, sine))
    d01, d23, qk_rot = after(vo.d01, vo.d23, qk_rot)
    vo.finish(d01, d23)
    vo_pieces = vo.pieces()
    v = project(where, normed, vo_pieces, 1, b_v)
    mixed, lse = attend(qk_rot, v, col, row)
    m_own, m_sib, att, mid, normed_mid, n_own, n_sib = out_project(
        where, mixed, order, activations, b_o, g2, g3, vo_pieces
    )
    m_oth = net.sibling(m_sib)
    n_oth = net.sibling(n_sib)
    a_own, a_sib, slope, layer_out, dc, down_sums, power = feed_forward(
        where, normed_mid, b_up, b_d, mid, cotangent, valid, g4, ffn
    )
    a_oth = net.sibling(a_sib)
    ffn_down = ffn.reshape(16, 2, 8, rows, width)

    dc_oth = net.sibling(dc)
    de, up_bias_sum = down_back(dc, slope, ffn_down)
    de, dc_oth, a_oth = after(de, dc_oth, a_oth)

    de_oth = net.sibling(de)
    slopes, de, de_oth = after(block_slopes(where, a_own, a_oth, dc, dc_oth), de, de_oth)

    down_sum = Scatter(net, slopes)
    down_sum.a()
    back = up_back(where, de, mid, att, cotangent, valid, g2, g3, ffn, vo_pieces)
    back, de, got, n_own, x23, y01 = after(back, de, down_sum.got, n_own, down_sum.x23, down_sum.y01)
    dmid, datt, dmix, mid_sums = back

    down_sum.c(x23, y01)
    fold = down_sum.fold_b(got)
    datt_oth = net.sibling(datt)
    slopes = row_slopes(n_own, n_oth, de, de_oth, 4)
    slopes, fold, datt_oth, datt, dmix, last = after(slopes, fold, datt_oth, datt, dmix, down_sum.last)

    down_sum.b(fold)
    part = down_sum.fold_last(last)
    steps = width // LANES // 2
    part_a = attend_back(qk_rot, v, dmix, lse, col, row, cosine, sine, 0, steps)
    part_a, dmix, slopes, got, part = after(part_a, dmix, slopes, down_sum.got, part)
    d_a, sums_a = part_a

    up_sum = Scatter(net, slopes)
    up_sum.a()
    fold = down_sum.fold_near(got, part)
    a_other = net.sibling(d_a)
    part_b = attend_back(qk_rot, v, dmix, lse, col, row, cosine, sine, steps, steps)
    part_b, datt, up_got, fold, a_other, m_own, x23, y01 = after(
        part_b, datt, up_sum.got, fold, a_other, m_own, up_sum.x23, up_sum.y01
    )
    d_b, sums_b = part_b

    up_sum.c(x23, y01)
    down_sum.near(fold)
    b_other = net.sibling(d_b)
    slopes = row_slopes(m_own, m_oth, datt, datt_oth, 1, 3)
    slopes, b_other, d_a, d_b, a_other, up_got = after(slopes, b_other, d_a, d_b, a_other, up_got)
    up_fold = up_sum.fold_b(up_got)
    slopes = qkv_slopes(x_own, x_oth, d_a, d_b, a_other, b_other, slopes)
    slopes, up_fold, up_last, got, d_a, d_b = after(
        slopes, up_fold, up_sum.last, down_sum.got, d_a, d_b
    )

    up_sum.b(up_fold)
    part = up_sum.fold_last(up_last)
    down_sum.far(down_sum.fold_far(got))
    input_gradient, first_sum = in_back(where, d_a, d_b, activations, dmid, g1, qk_pieces, vo_pieces)
    sums = jnp.concatenate([sums_a, sums_b], axis=1) + mid_sums + down_sums
    sums = jnp.concatenate(
        [
            sums,
            first_sum,
            up_bias_sum.reshape(4, width),
            jnp.pad(power, ((0, 2), (0, width - LANES))),
        ]
    )
    sums, slopes, up_got, part, down_got = after(sums, slopes, up_sum.got, part, down_sum.got)

    att_sum = Scatter(net, slopes)
    att_sum.a()
    up_sum.near(up_sum.fold_near(up_got, part))
    down_total = down_sum.result(down_got)
    sums = sums + net.sibling(sums)
    sums = sums + net.swap(sums, 1)
    sums, got, up_got, x23, y01 = after(sums, att_sum.got, up_sum.got, att_sum.x23, att_sum.y01)

    att_sum.c(x23, y01)
    up_sum.far(up_sum.fold_far(up_got))
    fold = att_sum.fold_b(got)
    sums = sums + net.swap(sums, 2)
    sums = sums + net.swap(sums, 4)
    fold, up_got, sums, last = after(fold, up_sum.got, sums, att_sum.last)

    att_sum.b(fold)
    part = att_sum.fold_last(last)
    sums = sums + net.swap(sums, 8)
    got, sums, part = after(att_sum.got, sums, part)

    att_sum.near(att_sum.fold_near(got, part))
    up_total = up_sum.result(up_got)
    own = lax.dynamic_slice_in_dim(sums[:9], device * rows, rows, 1)
    own_up = lax.dynamic_slice_in_dim(sums[9:13].reshape(-1), device * block, block, 0)
    got, own, own_up, power_sum = after(att_sum.got, own, own_up, sums[13, 0])

    att_sum.far(att_sum.fold_far(got))
    att_total = att_sum.result(att_sum.got)
    qkv_total = [att_total[:, i * width : (i + 1) * width] for i in range(3)]
    out_total = att_total[:, 3 * width :]

    output_power = power_sum / (t * 32)
    own = [own[i] for i in (0, 1, 2, 5, 7, 8, 4, 3, 6)]
    return (
        layer_out,
        input_gradient,
        *qkv_total,
        out_total,
        up_total,
        down_total,
        own[0],
        own[1],
        own[2],
        own[3],
        own_up,
        own[4],
        own[5],
        own[6],
        own[7],
        own[8],
        output_power,
    )


def shards(*args):
    rows, length = args[3].shape[0], args[0].shape[0]
    if lax.axis_size("wide") == 16 and rows == 32 and length == 512:
        return shards_16(*args)
    return shards_any(*args)


def solution(mesh):
    matrix = P(AXES, None)
    vector = P(AXES)
    return jax.shard_map(
        shards,
        mesh=mesh,
        in_specs=(matrix, vector, matrix) + (matrix,) * 6 + (vector,) * 10,
        out_specs=(matrix,) * 8 + (vector,) * 10 + (P(),),
        check_vma=False,
    )
```

```python
import jax
import jax.numpy as jnp
import functools

from jax import lax
from jax.experimental import pallas as pl
from jax.experimental.pallas import tpu as pltpu
from jax.sharding import PartitionSpec as P

HEAD = 64
AXES = ("wide", "narrow")


def rms_norm(values, gain):
    return values * lax.rsqrt(jnp.mean(values * values, axis=-1, keepdims=True) + 1e-06) * gain


def rotate(values, cosine, sine):
    midpoint = values.shape[-1] // 2
    first_half = values[..., :midpoint]
    second_half = values[..., midpoint:]
    return jnp.concatenate(
        [first_half * cosine - second_half * sine, first_half * sine + second_half * cosine],
        axis=-1,
    )


def positions_of(segment):
    places = jnp.arange(segment.shape[0])
    matching = segment[:, None] == segment[None, :]
    earlier = places[None, :] < places[:, None]
    return jnp.sum(jnp.logical_and(matching, earlier).astype(jnp.int32), axis=1)


def angle_tables(segment):
    places = positions_of(segment).astype(jnp.float32)
    midpoint = HEAD // 2
    inverse = 10000.0 ** (-jnp.arange(midpoint).astype(jnp.float32) * 2.0 / HEAD)
    angles = places[:, None] * inverse[None, :]
    return (jnp.cos(angles)[:, None, :], jnp.sin(angles)[:, None, :])


def key_mask(segment):
    places = jnp.arange(segment.shape[0])
    matching = segment[:, None] == segment[None, :]
    allowed = matching & (segment[None, :] >= 0) & (places[None, :] <= places[:, None])
    return allowed | (places[None, :] == places[:, None])


def contract_rows(left, right):
    return lax.dot_general(
        left, right, (((0,), (0,)), ((), ())), preferred_element_type=jnp.float32
    )


def times_transpose(left, right):
    return lax.dot_general(
        left, right, (((1,), (1,)), ((), ())), preferred_element_type=jnp.float32
    )


def product(left, right):
    return jnp.dot(left, right, preferred_element_type=jnp.float32)


def column_sums(values):
    return jnp.sum(values.astype(jnp.float32), axis=0)


def masked_scores(query_rot, key_rot, allowed):
    scores = (
        jnp.einsum("qhd,khd->hqk", query_rot, key_rot, preferred_element_type=jnp.float32) * 0.125
    )
    return jnp.where(allowed[None], scores, -1e30)


class Net:
    def __init__(self, wide):
        self.wide = wide
        self.me = lax.axis_index("wide")
        self.core = lax.axis_index("narrow")
        outer = []
        mask = wide // 2
        while mask > 2:
            outer.append(mask)
            mask //= 2
        self.outer = outer

    def swap(self, value, mask):
        pairs = [(d, d ^ mask) for d in range(self.wide)]
        return lax.ppermute(value, "wide", pairs)

    def sibling(self, value):
        return lax.ppermute(value, "narrow", [(0, 1), (1, 0)])

    def bit(self, mask):
        return (self.me & mask) != 0

    def grow(self, value, mask, axis):
        other = self.swap(value, mask)
        bit = self.bit(mask)
        low = jnp.where(bit, other, value)
        high = jnp.where(bit, value, other)
        return jnp.stack([low, high], axis=axis)

    def shrink(self, value, mask, axis):
        bit = self.bit(mask).astype(jnp.int32)
        mine = lax.dynamic_index_in_dim(value, bit, axis, keepdims=False)
        theirs = lax.dynamic_index_in_dim(value, 1 - bit, axis, keepdims=False)
        other = self.swap(theirs, mask)
        return (mine.astype(jnp.float32) + other.astype(jnp.float32)).astype(jnp.bfloat16)

    def gather(self, first, second):
        r, c = first.shape
        both = jnp.stack([first, second])[None]
        for mask in self.outer:
            both = self.grow(both, mask, 1).reshape(-1, 2, r, c)
        outer = both.shape[0]
        a = self.grow(both[:, 0], 1, 1)
        a = self.grow(a, 2, 1)
        b = self.grow(both[:, 1], 2, 1)
        b = self.grow(b, 1, 2)
        return jnp.stack([a, b], axis=3).reshape(outer * 4 * 2 * r, c)

    def scatter(self, full):
        rows, c = full.shape
        r = rows // (self.wide * 2)
        outer = self.wide // 4
        parts = full.reshape(outer, 2, 2, 2, r, c)
        a, b = parts[:, :, :, 0], parts[:, :, :, 1]
        a = self.shrink(self.shrink(a, 2, 1), 1, 1)
        b = self.shrink(self.shrink(b, 1, 2), 2, 1)
        both = jnp.stack([a, b], axis=1)
        for mask in reversed(self.outer):
            count = both.shape[0] // 2
            both = self.shrink(both.reshape(count, 2, 2, r, c), mask, 1)
        return both[0, 0], both[0, 1]

    def gather_small(self, value):
        other = self.sibling(value)
        core = self.core == 1
        buf = jnp.stack([jnp.where(core, other, value), jnp.where(core, value, other)])[None]
        for mask in [1, 2] + self.outer[::-1]:
            buf = self.grow(buf, mask, 0).reshape(1, -1, *value.shape)
        return buf[0]

    def total(self, value):
        value = value + self.sibling(value)
        for mask in [1, 2] + self.outer[::-1]:
            value = value + self.swap(value, mask)
        return value

    def pick(self, value, axis):
        mine = lax.dynamic_index_in_dim(value, self.core, axis, keepdims=False)
        theirs = lax.dynamic_index_in_dim(value, 1 - self.core, axis, keepdims=False)
        return mine, theirs

    def halves(self, mine, theirs):
        core = self.core == 1
        return jnp.where(core, theirs, mine), jnp.where(core, mine, theirs)

    def columns_in(self, shard):
        mine, theirs = self.pick(shard, 1)
        return self.halves(mine, self.sibling(theirs))

    def columns_out(self, first, second):
        mine, theirs = self.pick(jnp.stack([first, second]), 0)
        other = self.sibling(theirs)
        left, right = self.halves(mine, other)
        return jnp.stack([left, right], axis=1)


def shards_any(
    activations,
    segment_ids,
    cotangent,
    querymat,
    keymat,
    valuemat,
    outmat,
    upmatrix,
    downmatrix,
    querybias,
    keybias,
    valuebias,
    outbias,
    upbias,
    downbias,
    firstgain,
    secondgain,
    thirdgain,
    fourthgain,
):
    wide = lax.axis_size("wide")
    net = Net(wide)
    core = net.core
    length, width = activations.shape
    rows = querymat.shape[0]
    hidden = upmatrix.shape[1]
    block = hidden // (2 * wide)
    half = width // 2
    heads = width // HEAD
    f32 = jnp.float32
    bf16 = jnp.bfloat16

    nine = [querybias, keybias, valuebias, outbias, downbias, firstgain, secondgain, thirdgain, fourthgain]
    small = jnp.concatenate([jnp.concatenate(nine), upbias])
    qkv_shard = jnp.concatenate(
        [m.reshape(rows, 2, half) for m in (querymat, keymat, valuemat)], axis=2
    )
    up_shard = upmatrix.reshape(rows, wide, 2, block).transpose(0, 2, 1, 3).reshape(rows, 2, hidden // 2)
    out_shard = outmat.reshape(rows, 2, half)
    small_all = net.gather_small(small)
    qkv_mine = net.gather(*net.columns_in(qkv_shard))
    out_mine = net.gather(*net.columns_in(out_shard))
    up_mine = net.gather(*net.columns_in(up_shard))
    down_rows = downmatrix.shape[0]
    down_mine = net.gather(downmatrix[: down_rows // 2], downmatrix[down_rows // 2 :])
    qkv_theirs, out_theirs, up_theirs, down_theirs = map(
        net.sibling, (qkv_mine, out_mine, up_mine, down_mine)
    )

    vectors = small_all[:, : 9 * rows].reshape(-1, 9, rows).transpose(1, 0, 2).reshape(9, width)
    vectors = vectors.astype(f32)
    bias_query, bias_key, bias_value, bias_output, bias_down = (vectors[i] for i in range(5))
    gain_first, gain_second, gain_third, gain_fourth = (vectors[i] for i in range(5, 9))
    bias_up_pair = small_all[:, 9 * rows :].reshape(wide, 2, block).astype(f32)
    bias_up_mine, bias_up_theirs = (v.reshape(-1) for v in net.pick(bias_up_pair, 1))

    def natural(mine, theirs):
        return jnp.where(
            core == 1,
            jnp.concatenate([theirs, mine], axis=-1),
            jnp.concatenate([mine, theirs], axis=-1),
        )

    inputs = activations.astype(f32)
    cosine, sine = angle_tables(segment_ids)
    allowed = key_mask(segment_ids)
    valid_row = (segment_ids >= 0).astype(f32)
    normed_in, pull_first = jax.vjp(rms_norm, inputs, gain_first)
    normed_low = normed_in.astype(bf16)
    normed_low_theirs = net.sibling(normed_low)
    qkv_m = product(normed_low, qkv_mine)
    qkv_t = product(normed_low, qkv_theirs)
    queries, keys_pre, values_pre = (
        natural(qkv_m[:, i * half : (i + 1) * half], qkv_t[:, i * half : (i + 1) * half]) + b
        for i, b in enumerate((bias_query, bias_key, bias_value))
    )
    query_rot = rotate(queries.reshape(length, heads, HEAD), cosine, sine).astype(bf16)
    key_rot = rotate(keys_pre.reshape(length, heads, HEAD), cosine, sine).astype(bf16)
    value_low = values_pre.reshape(length, heads, HEAD).astype(bf16)
    scores = masked_scores(query_rot, key_rot, allowed)
    peak = jnp.max(scores, axis=-1, keepdims=True)
    exponent = jnp.exp(scores - peak)
    totals = jnp.sum(exponent, axis=-1, keepdims=True)
    logsum = peak + jnp.log(totals)
    probs = exponent / totals
    mixed = jnp.einsum(
        "hqk,khd->qhd", probs.astype(bf16), value_low, preferred_element_type=f32
    )
    mixed_low = mixed.reshape(length, width).astype(bf16)
    mixed_low_theirs = net.sibling(mixed_low)
    attended = natural(product(mixed_low, out_mine), product(mixed_low, out_theirs)) + bias_output
    normed_att, pull_second = jax.vjp(rms_norm, attended, gain_second)
    middle = inputs + normed_att
    normed_mid, pull_third = jax.vjp(rms_norm, middle, gain_third)
    normed_mid_low = normed_mid.astype(bf16)
    normed_mid_low_theirs = net.sibling(normed_mid_low)
    act_m_f, pull_gelu_m = jax.vjp(jax.nn.gelu, product(normed_mid_low, up_mine) + bias_up_mine)
    act_t_f, pull_gelu_t = jax.vjp(jax.nn.gelu, product(normed_mid_low, up_theirs) + bias_up_theirs)
    act_m = act_m_f.astype(bf16)
    act_t = act_t_f.astype(bf16)
    act_other = net.sibling(act_t)
    contracted = product(act_m, down_mine) + product(act_t, down_theirs) + bias_down
    local_power = jnp.sum(valid_row * jnp.mean(contracted * contracted, axis=-1))
    normed_out, pull_fourth = jax.vjp(rms_norm, contracted, gain_fourth)
    layer_out = (middle + normed_out).astype(bf16)

    seed = cotangent.astype(f32) * valid_row[:, None]
    d_contracted_f, fourth_slope = pull_fourth(seed)
    d_contracted = d_contracted_f.astype(bf16)
    d_contracted_theirs = net.sibling(d_contracted)
    down_bias_slope = column_sums(d_contracted)
    d_exp_m = pull_gelu_m(times_transpose(d_contracted, down_mine))[0].astype(bf16)
    d_exp_t = pull_gelu_t(times_transpose(d_contracted, down_theirs))[0].astype(bf16)
    d_exp_other = net.sibling(d_exp_t)

    def both_rows(a, b):
        return jnp.concatenate([a, b], axis=0)

    down_slope = contract_rows(
        both_rows(act_m, act_other), both_rows(d_contracted, d_contracted_theirs)
    ).astype(bf16)
    down_sum = net.scatter(down_slope)
    up_slope = contract_rows(
        both_rows(normed_mid_low, normed_mid_low_theirs), both_rows(d_exp_m, d_exp_other)
    ).astype(bf16)
    up_sum = net.scatter(up_slope)
    up_bias_m, up_bias_t = column_sums(d_exp_m), column_sums(d_exp_t)
    d_normed_mid = times_transpose(d_exp_m, up_mine) + times_transpose(d_exp_t, up_theirs)
    d_middle_part, third_slope = pull_third(d_normed_mid)
    d_middle = seed + d_middle_part
    d_attended_f, second_slope = pull_second(d_middle)
    d_attended = d_attended_f.astype(bf16)
    output_bias_slope = column_sums(d_attended)
    d_att_m, d_att_t = net.pick(d_attended.reshape(length, 2, half), 1)
    d_att_other = net.sibling(d_att_t)
    out_slope = contract_rows(
        both_rows(mixed_low, mixed_low_theirs), both_rows(d_att_m, d_att_other)
    ).astype(bf16)
    out_sum = net.scatter(out_slope)
    d_mixed = (
        (times_transpose(d_att_m, out_mine) + times_transpose(d_att_t, out_theirs))
        .astype(bf16)
        .reshape(length, heads, HEAD)
    )
    probs_again = jnp.exp(masked_scores(query_rot, key_rot, allowed) - logsum)
    d_values = jnp.einsum(
        "hqk,qhd->khd", probs_again.astype(bf16), d_mixed, preferred_element_type=f32
    )
    d_probs = jnp.einsum("qhd,khd->hqk", d_mixed, value_low, preferred_element_type=f32)
    row_terms = jnp.sum(probs_again * d_probs, axis=-1, keepdims=True)
    d_scores = (probs_again * (d_probs - row_terms)).astype(bf16)
    d_query_rot = (
        jnp.einsum("hqk,khd->qhd", d_scores, key_rot, preferred_element_type=f32) * 0.125
    )
    d_key_rot = (
        jnp.einsum("hqk,qhd->khd", d_scores, query_rot, preferred_element_type=f32) * 0.125
    )
    d_queries = rotate(d_query_rot, cosine, -sine).reshape(length, width).astype(bf16)
    d_keys = rotate(d_key_rot, cosine, -sine).reshape(length, width).astype(bf16)
    d_values_low = d_values.reshape(length, width).astype(bf16)
    pairs = [net.pick(v.reshape(length, 2, half), 1) for v in (d_queries, d_keys, d_values_low)]
    d_qkv_m = jnp.concatenate([p[0] for p in pairs], axis=1)
    d_qkv_t = jnp.concatenate([p[1] for p in pairs], axis=1)
    d_qkv_other = net.sibling(d_qkv_t)
    qkv_slope = contract_rows(
        both_rows(normed_low, normed_low_theirs), both_rows(d_qkv_m, d_qkv_other)
    ).astype(bf16)
    qkv_sum = net.scatter(qkv_slope)
    d_normed = times_transpose(d_qkv_m, qkv_mine) + times_transpose(d_qkv_t, qkv_theirs)
    d_inputs_part, first_slope = pull_first(d_normed)
    input_gradient = d_middle + d_inputs_part

    up_bias_low = jnp.where(core == 1, up_bias_t, up_bias_m).reshape(wide, 1, block)
    up_bias_high = jnp.where(core == 1, up_bias_m, up_bias_t).reshape(wide, 1, block)
    up_bias_slope = jnp.concatenate([up_bias_low, up_bias_high], axis=1).reshape(-1)
    small_slopes = jnp.concatenate(
        [
            column_sums(d_queries),
            column_sums(d_keys),
            column_sums(d_values_low),
            output_bias_slope,
            down_bias_slope,
            first_slope,
            second_slope,
            third_slope,
            fourth_slope,
            up_bias_slope,
            jnp.full((128,), local_power, f32),
        ]
    )
    sums = net.total(small_slopes)
    output_power = sums[-1] / (length * wide * 2)
    device = net.me * 2 + core
    own = lax.dynamic_slice_in_dim(sums[: 9 * width].reshape(9, width), device * rows, rows, 1)
    own_up = lax.dynamic_slice_in_dim(sums[9 * width : 9 * width + hidden], device * 2 * block // 2, block, 0)

    qkv_grad = net.columns_out(*qkv_sum).astype(f32)
    out_grad = net.columns_out(*out_sum).astype(f32).reshape(rows, width)
    up_grad = net.columns_out(*up_sum).astype(f32)
    up_grad = up_grad.reshape(rows, 2, wide, block).transpose(0, 2, 1, 3).reshape(rows, hidden)
    down_grad = jnp.concatenate(down_sum, axis=0).astype(f32)
    q_grad, k_grad, v_grad = (
        qkv_grad[:, :, i * half : (i + 1) * half].reshape(rows, width) for i in range(3)
    )
    return (
        layer_out,
        input_gradient,
        q_grad,
        k_grad,
        v_grad,
        out_grad,
        up_grad,
        down_grad,
        own[0],
        own[1],
        own[2],
        own[3],
        own_up,
        own[4],
        own[5],
        own[6],
        own[7],
        own[8],
        output_power,
    )


F32 = jnp.float32
BF16 = jnp.bfloat16
I32 = jnp.int32
EPS = 1e-06
VMEM_LIMIT = 60 * 1024 * 1024
LANES = 128
GELU_A = 0.7978845608028654
GELU_B = 0.044715
TILE = 128
DOWN_CHIPS = 4


def whole_spec():
    return pl.BlockSpec(memory_space=pltpu.VMEM)


def hbm_spec():
    return pl.BlockSpec(memory_space=pl.ANY)


def smem_spec():
    return pl.BlockSpec(memory_space=pltpu.SMEM)


def params():
    return pltpu.CompilerParams(vmem_limit_bytes=VMEM_LIMIT)


def shape(dims, dtype):
    return jax.ShapeDtypeStruct(dims, dtype)


def cost(flops, bytes_accessed):
    return pl.CostEstimate(flops=flops, bytes_accessed=bytes_accessed, transcendentals=0)


def dot(a, b):
    return lax.dot_general(a, b, (((1,), (0,)), ((), ())), preferred_element_type=F32)


def dot_t(a, b):
    return lax.dot_general(a, b, (((1,), (1,)), ((), ())), preferred_element_type=F32)


def t_dot(a, b):
    return lax.dot_general(a, b, (((0,), (0,)), ((), ())), preferred_element_type=F32)


def pair_mask(place):
    return place // 4 + 4 * (place % 4)


def assemble(where, pieces, target, sems, cols):
    copies = []
    for e in range(2):
        place = 0
        for piece in pieces[e * 5 : e * 5 + 5]:
            for j in range(piece.shape[0]):
                chip = where[0] ^ pair_mask(place)
                source = piece.at[j, :, pl.ds(*cols)]
                dest = target.at[chip, where[1] ^ e]
                copies.append(pltpu.make_async_copy(source, dest, sems.at[len(copies)]))
                place += 1
    for copy in copies:
        copy.start()
    return copies


def wait_all(copies):
    for copy in copies:
        copy.wait()


def fetch(sources, targets, sems, base=0):
    copies = [
        pltpu.make_async_copy(a, b, sems.at[base + i]) for i, (a, b) in enumerate(zip(sources, targets))
    ]
    for copy in copies:
        copy.start()
    return copies


def matrix(buf):
    return buf[...].reshape(-1, buf.shape[-1])


def inverse_rms(v):
    return lax.rsqrt(jnp.mean(v * v, axis=-1, keepdims=True) + EPS)


def place_rows(first, rows):
    n = rows[0].shape[1]
    at = lax.broadcasted_iota(I32, (8, n), 0)
    out = jnp.zeros((8, n), F32)
    for i, row in enumerate(rows):
        out = jnp.where(at == first + i, jnp.broadcast_to(row, (8, n)), out)
    return out


def rms_back(v, r, gain, e):
    ge = gain * e
    return r * ge - v * (r * r * r) * jnp.mean(v * ge, axis=-1, keepdims=True)


def row_sum(v):
    return jnp.sum(v, axis=0, keepdims=True)


def turn(v, cosine, sine):
    lane = lax.broadcasted_iota(I32, v.shape, 1)
    swapped = jnp.where((lane & 63) < 32, pltpu.roll(v, 96, 1), pltpu.roll(v, 32, 1))
    return v * cosine + swapped * sine


def project_kernel(parts, where, x, bias, *refs):
    pieces = refs[:10]
    tables = refs[10:-3]
    out, wbuf, sems = refs[-3:]
    width = x.shape[1]
    copies = [
        assemble(where, pieces, wbuf.at[i], sems.at[i], (i * width, width)) for i in range(parts)
    ]
    for i in range(parts):
        wait_all(copies[i])
        for c in range(0, width, 512):
            y = dot(x[...], wbuf[i, :, :, :, c : c + 512].reshape(width, 512))
            y = y + bias[:, i * width + c : i * width + c + 512]
            at = i * width + c
            if tables:
                cosine, sine = tables[0][...], tables[1][...]
                for b in range(0, 512, LANES):
                    z = turn(y[:, b : b + LANES], cosine, sine)
                    z = z * 0.125 if i == 0 else z
                    out[:, at + b : at + b + LANES] = z.astype(BF16)
            else:
                out[:, at : at + 512] = y.astype(BF16)


def project(where, x, pieces, parts, bias, tables=()):
    t, width = x.shape
    r = pieces[0].shape[1]
    return pl.pallas_call(
        functools.partial(project_kernel, parts),
        in_specs=[smem_spec(), whole_spec(), whole_spec()]
        + [hbm_spec()] * 10
        + [whole_spec()] * len(tables),
        out_specs=whole_spec(),
        out_shape=shape((t, parts * width), BF16),
        scratch_shapes=[
            pltpu.VMEM((parts, 16, 2, r, width), BF16),
            pltpu.SemaphoreType.DMA((parts, 32)),
        ],
        compiler_params=params(),
        cost_estimate=cost(2 * t * width * parts * width, 2 * parts * width * width),
        name="project",
    )(where, x, bias, *pieces, *tables)


def open_mask(col_ref, row_ref, open_ref):
    t = open_ref.shape[0]

    @pl.when(pl.program_id(0) == 0)
    def _():
        rows = lax.broadcasted_iota(I32, (t, t), 0)
        cols = lax.broadcasted_iota(I32, (t, t), 1)
        ok = (col_ref[...] == row_ref[...]) & (cols <= rows)
        open_ref[...] = jnp.where(ok, 0.0, -1e30)


def one_head(v, h):
    lane = lax.broadcasted_iota(I32, v.shape, 1)
    return jnp.where((lane < HEAD) == (h == 0), v, jnp.zeros_like(v))


def attend_kernel(q_ref, k_ref, v_ref, col_ref, row_ref, out_ref, lse_ref, open_ref):
    t = q_ref.shape[0]
    tile = TILE
    open_mask(col_ref, row_ref, open_ref)
    left = lax.broadcasted_iota(I32, (tile, LANES), 1) < HEAD
    spans = [(slice(i * tile, (i + 1) * tile), (i + 1) * tile) for i in range(t // tile)]
    pairs = [(rows, seen, h) for rows, seen in spans for h in range(2)]
    scores = [
        dot_t(one_head(q_ref[rows, :], h), k_ref[:seen, :]) + open_ref[rows, :seen]
        for rows, seen, h in pairs
    ]
    peaks = [jnp.max(s, axis=-1, keepdims=True) for s in scores]
    powers = [jnp.exp(s - peak) for s, peak in zip(scores, peaks)]
    totals = [jnp.sum(e, axis=-1, keepdims=True) for e in powers]
    outs = [
        dot(e.astype(BF16), v_ref[:seen, :]) / total
        for e, total, (rows, seen, h) in zip(powers, totals, pairs)
    ]
    sums = [peak + jnp.log(total) for peak, total in zip(peaks, totals)]
    for i, (rows, seen) in enumerate(spans):
        out_ref[rows, :] = jnp.where(left, outs[2 * i], outs[2 * i + 1]).astype(BF16)
        lse_ref[rows, :] = jnp.where(left, sums[2 * i], sums[2 * i + 1])


def attend(qk, v, col, row):
    t, width = v.shape
    steps = width // LANES
    block = lambda f: pl.BlockSpec((t, LANES), f)
    return pl.pallas_call(
        attend_kernel,
        grid=(steps,),
        in_specs=[
            block(lambda i: (0, i)),
            block(lambda i: (0, i + steps)),
            block(lambda i: (0, i)),
            pl.BlockSpec((t, 1), lambda i: (0, 0)),
            pl.BlockSpec((1, t), lambda i: (0, 0)),
        ],
        out_specs=[block(lambda i: (0, i))] * 2,
        out_shape=[shape((t, width), BF16), shape((t, width), F32)],
        scratch_shapes=[pltpu.VMEM((t, t), F32)],
        compiler_params=params(),
        cost_estimate=cost(4 * t * t * width, 10 * t * width),
        name="attend",
    )(qk, qk, v, col, row)


def attend_back_kernel(
    q_ref, k_ref, v_ref, dm_ref, lse_ref, col_ref, row_ref, cos_ref, sin_ref,
    d_ref, sum_ref, open_ref,
):
    t = q_ref.shape[0]
    tile = TILE
    open_mask(col_ref, row_ref, open_ref)
    left = lax.broadcasted_iota(I32, (tile, LANES), 1) < HEAD
    spans = [(slice(i * tile, (i + 1) * tile), (i + 1) * tile) for i in range(t // tile)]
    pairs = [(rows, seen, h) for rows, seen in spans for h in range(2)]
    scores = [
        dot_t(one_head(q_ref[rows, :], h), k_ref[:seen, :]) + open_ref[rows, :seen]
        for rows, seen, h in pairs
    ]
    d_probs = [dot_t(one_head(dm_ref[rows, :], h), v_ref[:seen, :]) for rows, seen, h in pairs]
    probs = [
        jnp.exp(s - lse_ref[rows, h * HEAD : h * HEAD + 1])
        for s, (rows, seen, h) in zip(scores, pairs)
    ]
    deltas = [jnp.sum(p * dp, axis=-1, keepdims=True) for p, dp in zip(probs, d_probs)]
    d_scores = [(p * (dp - d)).astype(BF16) for p, dp, d in zip(probs, d_probs, deltas)]
    probs = [p.astype(BF16) for p in probs]
    dq = [dot(ds, k_ref[:seen, :]) for ds, (rows, seen, h) in zip(d_scores, pairs)]
    total_q = jnp.zeros((1, LANES), F32)
    for i, (rows, seen) in enumerate(spans):
        v = jnp.where(left, dq[2 * i], dq[2 * i + 1]) * 0.125
        v = turn(v, cos_ref[rows, :], -sin_ref[rows, :]).astype(BF16)
        d_ref[0, rows, :] = v
        total_q += row_sum(v.astype(F32))
    totals = [total_q]
    for at, lhs, rhs in ((1, d_scores, q_ref), (2, probs, dm_ref)):
        total = jnp.zeros((1, LANES), F32)
        parts = [t_dot(a, rhs[rows, :]) for a, (rows, seen, h) in zip(lhs, pairs)]
        for i, (keys, _) in enumerate(spans):
            heads = [
                sum(parts[2 * j + h][keys] for j in range(i, len(spans))) for h in range(2)
            ]
            v = jnp.where(left, heads[0], heads[1])
            if at == 1:
                v = turn(v, cos_ref[keys, :], -sin_ref[keys, :])
            v = v.astype(BF16)
            d_ref[at, keys, :] = v
            total += row_sum(v.astype(F32))
        totals.append(total)
    sum_ref[...] = place_rows(0, totals)


def attend_back(qk, v, dm, lse, col, row, cosine, sine, first, steps):
    t, width = v.shape
    key = width // LANES
    part = steps * LANES
    block = lambda f: pl.BlockSpec((t, LANES), f)
    fixed = lambda a: pl.BlockSpec(a.shape, lambda i: (0, 0))
    here = block(lambda i: (0, i))
    read = block(lambda i: (0, i + first))
    return pl.pallas_call(
        attend_back_kernel,
        grid=(steps,),
        in_specs=[read, block(lambda i: (0, i + first + key)), read, read, read]
        + [fixed(a) for a in (col, row, cosine, sine)],
        out_specs=[
            pl.BlockSpec((3, t, LANES), lambda i: (0, 0, i)),
            pl.BlockSpec((8, LANES), lambda i: (0, i)),
        ],
        out_shape=[shape((3, t, part), BF16), shape((8, part), F32)],
        scratch_shapes=[pltpu.VMEM((t, t), F32)],
        compiler_params=params(),
        cost_estimate=cost(10 * t * t * part, 18 * t * part),
        name="attend_back",
    )(qk, qk, v, dm, lse, col, row, cosine, sine)


def out_kernel(where, mixed, order, x, bias, g2, g3, *refs):
    pieces = refs[:10]
    m_own, m_sib, att_ref, mid_ref, n_ref, n_own, n_sib, wbuf, sems = refs[10:]
    t, width = mixed.shape
    half = width // 2
    copies = assemble(where, pieces, wbuf, sems, (width, width))
    turned = dot_t(order[...], mixed[...]).astype(BF16)
    m_own[...] = turned[:half]
    m_sib[...] = turned[half:]
    wait_all(copies)
    w = matrix(wbuf)
    tile = 256
    for i in range(t // tile):
        rows = slice(i * tile, (i + 1) * tile)
        att = dot(mixed[rows, :], w) + bias[...]
        att_ref[rows, :] = att
        mid = x[rows, :].astype(F32) + att * inverse_rms(att) * g2[...]
        mid_ref[rows, :] = mid
        n_ref[rows, :] = (mid * inverse_rms(mid) * g3[...]).astype(BF16)
    turned = dot_t(order[...], n_ref[...]).astype(BF16)
    n_own[...] = turned[:half]
    n_sib[...] = turned[half:]


def out_project(where, mixed, order, x, bias, g2, g3, pieces):
    t, width = mixed.shape
    half = width // 2
    r = pieces[0].shape[1]
    halves = [shape((half, t), BF16)] * 2
    return pl.pallas_call(
        out_kernel,
        in_specs=[smem_spec()] + [whole_spec()] * 6 + [hbm_spec()] * 10,
        out_specs=[whole_spec()] * 7,
        out_shape=halves + [shape((t, width), F32)] * 2 + [shape((t, width), BF16)] + halves,
        scratch_shapes=[pltpu.VMEM((16, 2, r, width), BF16), pltpu.SemaphoreType.DMA((32,))],
        compiler_params=params(),
        cost_estimate=cost(6 * t * width * width, 16 * t * width),
        name="out_project",
    )(where, mixed, order, x, bias, g2, g3, *pieces)


def feed_kernel(
    where, x, b_up, w_up, w_down, b_down, valid, g4, mid_hbm, cot_hbm,
    a_own, a_sib, slope_ref, out_ref, dc_ref, sums_ref, power_ref, act_buf, acc, mid, cot, sems,
):
    step = pl.program_id(0)
    t, width = acc.shape
    first = where[1] == 0
    copies = [
        pltpu.make_async_copy(mid_hbm, mid, sems.at[0]),
        pltpu.make_async_copy(cot_hbm, cot, sems.at[1]),
    ]

    @pl.when(step == 0)
    def _():
        for copy in copies:
            copy.start()

    for j in range(w_up.shape[3] // 256):
        cols = slice(j * 256, (j + 1) * 256)
        y = dot(x[...], w_up[:, 0, :, cols].reshape(width, 256)) + b_up[:, cols]
        yy = y * y
        h = 0.5 * jnp.tanh(y * (GELU_A + (GELU_A * GELU_B) * yy)) + 0.5
        act = y * h
        slope = h + act * (1.0 - h) * (2 * GELU_A + (6 * GELU_A * GELU_B) * yy)
        act = act.astype(BF16)
        act_buf[:, cols] = act
        slope_ref[:, cols] = slope.astype(BF16)
        dst = slice(j * 128, (j + 1) * 128)
        a0, a1 = act[:, :128], act[:, 128:]
        a_own[:, dst] = jnp.where(first, a0, a1)
        a_sib[:, dst] = jnp.where(first, a1, a0)
    y = dot(act_buf[...], w_down[...].reshape(-1, width))

    @pl.when(step == 0)
    def _():
        acc[...] = y + b_down[...]

    @pl.when(step > 0)
    def _():
        acc[...] += y

    @pl.when(step == pl.num_programs(0) - 1)
    def _():
        wait_all(copies)
        tile = 128
        power = jnp.zeros((1, 1), F32)
        gain_sum = jnp.zeros((1, width), F32)
        bias_sum = jnp.zeros((1, width), F32)
        gain = g4[...]
        for i in range(t // tile):
            rows = slice(i * tile, (i + 1) * tile)
            v = acc[rows, :]
            ok = valid[rows, :]
            mean = jnp.mean(v * v, axis=-1, keepdims=True)
            power += row_sum(mean * ok)
            r = lax.rsqrt(mean + EPS)
            vr = v * r
            out_ref[rows, :] = (mid[rows, :] + vr * gain).astype(BF16)
            seed = cot[rows, :].astype(F32) * ok
            gain_sum += row_sum(vr * seed)
            dc = rms_back(v, r, gain, seed).astype(BF16)
            dc_ref[rows, :] = dc
            bias_sum += row_sum(dc.astype(F32))
        sums_ref[...] = place_rows(6, [gain_sum, bias_sum])
        power_ref[...] = jnp.broadcast_to(power, power_ref.shape)


def feed_forward(where, x, b_up, b_down, mid, cot, valid, g4, ffn):
    t, width = x.shape
    hidden = b_up.shape[1]
    devices, _, r, tn = ffn.shape
    steps = hidden // tn
    fixed = lambda a: pl.BlockSpec(a.shape, lambda i: (0, 0))
    tile = lambda n: pl.BlockSpec((t, n), lambda i: (0, i))
    return pl.pallas_call(
        feed_kernel,
        grid=(steps,),
        in_specs=[
            smem_spec(),
            fixed(x),
            pl.BlockSpec((1, tn), lambda i: (0, i)),
            pl.BlockSpec((devices, 1, r, tn), lambda i: (0, i, 0, 0)),
            pl.BlockSpec((devices // steps, 4, r, width), lambda i: (i, 1, 0, 0)),
            fixed(b_down),
            fixed(valid),
            fixed(g4),
            hbm_spec(),
            hbm_spec(),
        ],
        out_specs=[tile(tn // 2), tile(tn // 2), tile(tn)]
        + [pl.BlockSpec((t, width), lambda i: (0, 0))] * 2
        + [pl.BlockSpec((8, width), lambda i: (0, 0)), pl.BlockSpec((1, LANES), lambda i: (0, 0))],
        out_shape=[shape((t, hidden // 2), BF16)] * 2
        + [shape((t, hidden), BF16)]
        + [shape((t, width), BF16)] * 2
        + [shape((8, width), F32), shape((1, LANES), F32)],
        scratch_shapes=[
            pltpu.VMEM((t, tn), BF16),
            pltpu.VMEM((t, width), F32),
            pltpu.VMEM((t, width), F32),
            pltpu.VMEM((t, width), BF16),
            pltpu.SemaphoreType.DMA((2,)),
        ],
        compiler_params=params(),
        cost_estimate=cost(4 * t * width * hidden, 4 * width * hidden + 8 * t * hidden),
        name="feed_forward",
    )(where, x, b_up, ffn, ffn, b_down, valid, g4, mid, cot)


def block_at(ref, where, place):
    chip = where[0] ^ pair_mask(place)
    return ref.at[:, pl.ds(pl.multiple_of(chip * LANES, LANES), LANES)]


def down_back_kernel(dc, slope, w_ref, de_ref, sums_ref):
    width = dc.shape[1]
    for j in range(w_ref.shape[0]):
        cols = slice(j * 256, (j + 1) * 256)
        y = dot_t(dc[...], w_ref[j].reshape(256, width))
        d = (y * slope[:, cols].astype(F32)).astype(BF16)
        de_ref[:, cols] = d
        sums_ref[:, cols] = row_sum(d.astype(F32))


def down_back(dc, slope, ffn):
    t, width = dc.shape
    hidden = slope.shape[1]
    r = ffn.shape[3]
    chips = DOWN_CHIPS
    tn = chips * 256
    return pl.pallas_call(
        down_back_kernel,
        grid=(hidden // tn,),
        in_specs=[
            pl.BlockSpec((t, width), lambda i: (0, 0)),
            pl.BlockSpec((t, tn), lambda i: (0, i)),
            pl.BlockSpec((chips, 2, 4, r, width), lambda i: (i, 0, 1, 0, 0)),
        ],
        out_specs=[pl.BlockSpec((t, tn), lambda i: (0, i)), pl.BlockSpec((1, tn), lambda i: (0, i))],
        out_shape=[shape((t, hidden), BF16), shape((1, hidden), F32)],
        compiler_params=params(),
        cost_estimate=cost(2 * t * hidden * width, 2 * hidden * width),
        name="down_back",
    )(dc, slope, ffn)


GRAD_PLACES = {
    "d23": (14, 15),
    "d01": (12, 13),
    "x01": (4, 5),
    "y23": (10, 11),
    "x23": (6, 7),
    "y01": (8, 9),
    "f": (0, 1, 2, 3),
}


def runs_of(places):
    return [(at, places[at : at + 2]) for at in range(0, len(places), 2)]


def slope_kernel(parts, x_own, x_oth, *refs):
    dy_own, dy_oth = refs[:parts], refs[parts : 2 * parts]
    outs = refs[2 * parts :]
    for i in range(parts):
        n = dy_own[i].shape[1]
        y = dot(x_own[...], dy_own[i][...]) + dot(x_oth[...], dy_oth[i][...])
        y = y.astype(BF16)
        for places, out in zip(GRAD_PLACES.values(), outs):
            r = out.shape[1]
            for at, run in runs_of(places):
                part = y[run[0] * r : (run[-1] + 1) * r]
                out[at : at + 2, :, i * n : (i + 1) * n] = part.reshape(2, r, n)


def row_slopes(x_own, x_oth, dy_own, dy_oth, tiles, first=0):
    half, t = x_own.shape
    r = half // 16
    n = dy_own.shape[1] // tiles
    total = n * (first + tiles)
    fixed = pl.BlockSpec((half, t), lambda i: (0, 0))
    return pl.pallas_call(
        functools.partial(slope_kernel, 1),
        grid=(tiles,),
        in_specs=[fixed] * 2 + [pl.BlockSpec((t, n), lambda i: (0, i))] * 2,
        out_specs=[pl.BlockSpec((len(p), r, n), lambda i: (0, 0, i + first)) for p in GRAD_PLACES.values()],
        out_shape=[shape((len(p), r, total), BF16) for p in GRAD_PLACES.values()],
        compiler_params=params(),
        cost_estimate=cost(4 * t * half * n * tiles, 8 * t * n * tiles + 2 * half * n * tiles),
        name="row_slopes",
    )(x_own, x_oth, dy_own, dy_oth)


def qkv_slope_kernel(x_own, x_oth, a_own, b_own, a_oth, b_oth, *refs):
    outs = refs[len(GRAD_PLACES) :]
    n = a_own.shape[2]
    for i, (own, oth) in enumerate(((a_own, a_oth), (b_own, b_oth))):
        y = dot(x_own[...], own[0]) + dot(x_oth[...], oth[0])
        y = y.astype(BF16)
        for places, out in zip(GRAD_PLACES.values(), outs):
            r = out.shape[1]
            for at, run in runs_of(places):
                part = y[run[0] * r : (run[-1] + 1) * r]
                out[at : at + 2, :, i * n : (i + 1) * n] = part.reshape(2, r, n)


def qkv_slopes(x_own, x_oth, a_own, b_own, a_oth, b_oth, pieces):
    half, t = x_own.shape
    r = half // 16
    n = a_own.shape[2]
    fixed = pl.BlockSpec((half, t), lambda i: (0, 0))
    return pl.pallas_call(
        qkv_slope_kernel,
        grid=(3,),
        in_specs=[fixed] * 2
        + [pl.BlockSpec((1, t, n), lambda i: (i, 0, 0))] * 4
        + [hbm_spec()] * len(pieces),
        out_specs=[pl.BlockSpec((len(p), r, 2 * n), lambda i: (0, 0, i)) for p in GRAD_PLACES.values()],
        out_shape=[shape(p.shape, BF16) for p in pieces],
        input_output_aliases={6 + i: i for i in range(len(pieces))},
        compiler_params=params(),
        cost_estimate=cost(24 * t * half * n, 24 * t * n + 12 * half * n),
        name="qkv_slopes",
    )(x_own, x_oth, a_own, b_own, a_oth, b_oth, *pieces)


def block_slope_kernel(where, a_own, a_oth, dy_own, dy_oth, *refs):
    outs = refs[:7]
    stage, sems = refs[7:]
    sent = []
    for places, out in zip(GRAD_PLACES.values(), outs):
        for at, run in runs_of(places):
            i = len(sent)
            mine, other = (
                jnp.concatenate([block_at(act, where, p)[...] for p in run], axis=1)
                for act in (a_own, a_oth)
            )
            y = t_dot(mine, dy_own[...]) + t_dot(other, dy_oth[...])
            stage[i] = y.astype(BF16).reshape(2, LANES, y.shape[1])
            copy = pltpu.make_async_copy(stage.at[i], out.at[pl.ds(at, 2)], sems.at[i])
            copy.start()
            sent.append(copy)
    wait_all(sent)


def block_slopes(where, a_own, a_oth, dy_own, dy_oth):
    t, half = a_own.shape
    width = dy_own.shape[1]
    return pl.pallas_call(
        block_slope_kernel,
        in_specs=[smem_spec()] + [whole_spec()] * 4,
        out_specs=[hbm_spec()] * 7,
        out_shape=[shape((len(p), LANES, width), BF16) for p in GRAD_PLACES.values()],
        scratch_shapes=[pltpu.VMEM((8, 2, LANES, width), BF16), pltpu.SemaphoreType.DMA((8,))],
        compiler_params=params(),
        cost_estimate=cost(4 * t * half * width, 4 * t * (half + width) + 2 * half * width),
        name="block_slopes",
    )(where, a_own, a_oth, dy_own, dy_oth)


def up_back_kernel(where, de, valid, g2_ref, g3_ref, w_ref, mid_hbm, att_hbm, cot_hbm, *refs):
    pieces = refs[:10]
    dmid_hbm, datt_hbm, dmix_ref, sums_ref, acc, wbuf, mid_buf, att_buf, cot_buf, dmid_ref, datt_ref, sems = refs[10:]
    step = pl.program_id(0)
    t, width = acc.shape

    @pl.when(step == 0)
    def _():
        assemble(where, pieces, wbuf, sems, (width, width))
        fetch((mid_hbm, att_hbm, cot_hbm), (mid_buf, att_buf, cot_buf), sems, 32)

    y = dot_t(de[...], w_ref[:, 0].reshape(width, -1))

    @pl.when(step == 0)
    def _():
        acc[...] = y

    @pl.when(step > 0)
    def _():
        acc[...] += y

    @pl.when(step == pl.num_programs(0) - 1)
    def _():
        for i in range(32):
            pltpu.make_async_copy(pieces[0].at[0, :, pl.ds(width, width)], wbuf.at[0, 0], sems.at[i]).wait()
        for i, (a, b) in enumerate(((mid_hbm, mid_buf), (att_hbm, att_buf), (cot_hbm, cot_buf))):
            pltpu.make_async_copy(a, b, sems.at[32 + i]).wait()
        tile = 128
        g2, g3 = g2_ref[...], g3_ref[...]
        w = matrix(wbuf)
        sent = []
        sums = [jnp.zeros((1, width), F32)] * 3
        for i in range(t // tile):
            rows = slice(i * tile, (i + 1) * tile)
            e = acc[rows, :]
            mid = mid_buf[rows, :]
            r3 = inverse_rms(mid)
            dmid = cot_buf[rows, :].astype(F32) * valid[rows, :] + rms_back(mid, r3, g3, e)
            dmid_ref[rows, :] = dmid
            att = att_buf[rows, :]
            r2 = inverse_rms(att)
            datt = rms_back(att, r2, g2, dmid).astype(BF16)
            datt_ref[rows, :] = datt
            sums[0] += row_sum(mid * r3 * e)
            sums[1] += row_sum(att * r2 * dmid)
            sums[2] += row_sum(datt.astype(F32))
            for at, (a, b) in enumerate(((dmid_ref, dmid_hbm), (datt_ref, datt_hbm))):
                copy = pltpu.make_async_copy(a.at[rows, :], b.at[rows, :], sems.at[35 + 2 * i + at])
                copy.start()
                sent.append(copy)
        dmix_ref[...] = dot_t(datt_ref[...], w).astype(BF16)
        sums_ref[...] = place_rows(3, sums)
        wait_all(sent)


def up_back(where, de, mid, att, cot, valid, g2, g3, ffn, pieces):
    t, width = mid.shape
    hidden = de.shape[1]
    tk = ffn.shape[3]
    r = pieces[0].shape[1]
    fixed = lambda a: pl.BlockSpec(a.shape, lambda i: (0, 0))
    return pl.pallas_call(
        up_back_kernel,
        grid=(hidden // tk,),
        in_specs=[smem_spec(), pl.BlockSpec((t, tk), lambda i: (0, i))]
        + [fixed(a) for a in (valid, g2, g3)]
        + [pl.BlockSpec((ffn.shape[0], 1, ffn.shape[2], tk), lambda i: (0, i, 0, 0))]
        + [hbm_spec()] * 13,
        out_specs=[hbm_spec()] * 2
        + [pl.BlockSpec((t, width), lambda i: (0, 0)), pl.BlockSpec((8, width), lambda i: (0, 0))],
        out_shape=[shape((t, width), F32), shape((t, width), BF16), shape((t, width), BF16), shape((8, width), F32)],
        scratch_shapes=[
            pltpu.VMEM((t, width), F32),
            pltpu.VMEM((16, 2, r, width), BF16),
            pltpu.VMEM((t, width), F32),
            pltpu.VMEM((t, width), F32),
            pltpu.VMEM((t, width), BF16),
            pltpu.VMEM((t, width), F32),
            pltpu.VMEM((t, width), BF16),
            pltpu.SemaphoreType.DMA((43,)),
        ],
        compiler_params=params(),
        cost_estimate=cost(2 * t * width * hidden, 2 * width * hidden + 2 * t * hidden),
        name="up_back",
    )(where, de, valid, g2, g3, ffn, mid, att, cot, *pieces)


def in_back_kernel(where, *refs):
    d_a, d_b, x_hbm, dmid_hbm, g1_ref = refs[:5]
    qk, vo = refs[5:15], refs[15:25]
    out_ref, sums_ref, wbuf, x_buf, dmid_buf, sems = refs[25:]
    t, width = out_ref.shape
    half = width // 2
    copies = [
        assemble(where, pieces, wbuf.at[i], sems.at[i], (start, width))
        for i, (pieces, start) in enumerate(((qk, 0), (qk, width), (vo, 0)))
    ]
    late = fetch((x_hbm, dmid_hbm), (x_buf, dmid_buf), sems.at[3])
    e = None
    for i in range(3):
        wait_all(copies[i])
        d = jnp.concatenate([d_a[i], d_b[i]], axis=1)
        y = dot_t(d, wbuf[i].reshape(width, width))
        e = y if e is None else e + y
    wait_all(late)
    gain = g1_ref[...]
    tile = 128
    total = jnp.zeros((1, width), F32)
    for i in range(t // tile):
        rows = slice(i * tile, (i + 1) * tile)
        x = x_buf[rows, :].astype(F32)
        r = inverse_rms(x)
        out_ref[rows, :] = dmid_buf[rows, :] + rms_back(x, r, gain, e[rows, :])
        total += row_sum(x * r * e[rows, :])
    sums_ref[...] = total


def in_back(where, d_a, d_b, x, dmid, g1, qk_pieces, vo_pieces):
    t, width = x.shape
    r = qk_pieces[0].shape[1]
    return pl.pallas_call(
        in_back_kernel,
        in_specs=[smem_spec()] + [whole_spec()] * 2 + [hbm_spec()] * 2 + [whole_spec()] + [hbm_spec()] * 20,
        out_specs=[whole_spec()] * 2,
        out_shape=[shape((t, width), F32), shape((1, width), F32)],
        scratch_shapes=[
            pltpu.VMEM((3, 16, 2, r, width), BF16),
            pltpu.VMEM((t, width), BF16),
            pltpu.VMEM((t, width), F32),
            pltpu.SemaphoreType.DMA((4, 32)),
        ],
        compiler_params=params(),
        cost_estimate=cost(6 * t * width * width, 6 * width * width),
        name="in_back",
    )(where, d_a, d_b, x, dmid, g1, *qk_pieces, *vo_pieces)


def after(*values):
    return lax.optimization_barrier(values)


def add(*values):
    total = values[0].astype(F32)
    for v in values[1:]:
        total = total + v.astype(F32)
    return total


class Gather:
    def __init__(self, net, shard):
        self.net = net
        self.line = [shard] + [net.swap(shard, 4 * m) for m in (1, 2, 3)]

    def spread(self, line):
        net = self.net
        self.lines = jnp.stack(line)
        self.x = net.swap(self.lines, 1)
        self.y = net.swap(self.lines, 2)
        self.sib = [net.sibling(self.lines)]

    def corner(self, x, y):
        net = self.net
        self.x, self.y = x, y
        self.d01 = net.swap(x[:2], 2)
        self.d23 = net.swap(y[2:], 1)
        self.sib += [net.sibling(x), net.sibling(y)]

    def finish(self, d01, d23):
        net = self.net
        self.d01, self.d23 = d01, d23
        self.sib += [net.sibling(d01), net.sibling(d23)]

    def pieces(self):
        return [self.lines, self.x, self.y, self.d01, self.d23] + self.sib


class Scatter:
    def __init__(self, net, pieces):
        self.net = net
        self.d23, self.d01, self.x01, self.y23, self.x23, self.y01, self.f = pieces

    def a(self):
        self.got = [self.net.swap(self.d23, 1), self.net.swap(self.d01, 2)]

    def c(self, x23, y01):
        self.last = [self.net.swap(x23, 1), self.net.swap(y01, 2)]

    def fold_b(self, got):
        return [add(self.x01, got[1]).astype(BF16), add(self.y23, got[0]).astype(BF16)]

    def b(self, fold):
        self.got = [self.net.swap(fold[0], 1), self.net.swap(fold[1], 2)]

    def fold_last(self, last):
        return [add(self.f[:2], last[1]), add(self.f[2:], last[0])]

    def fold_near(self, got, part):
        low, high = add(part[0], got[0]), add(part[1], got[1])
        return [low[0], high[0], jnp.stack([low[1], high[1]]).astype(BF16)]

    def near(self, fold):
        self.low, self.high, send = fold
        self.got = [self.net.swap(send, 4)]

    def fold_far(self, got):
        return [add(self.low, got[0][0]), add(self.high, got[0][1]).astype(BF16)]

    def far(self, fold):
        self.own, send = fold
        self.got = [self.net.swap(send, 8)]

    def result(self, got):
        return add(self.own, got[0])


def shards_16(
    activations,
    segment_ids,
    cotangent,
    querymat,
    keymat,
    valuemat,
    outmat,
    upmatrix,
    downmatrix,
    querybias,
    keybias,
    valuebias,
    outbias,
    upbias,
    downbias,
    firstgain,
    secondgain,
    thirdgain,
    fourthgain,
):
    net = Net(16)
    t, width = activations.shape
    rows = querymat.shape[0]
    hidden = upmatrix.shape[1]
    block = upbias.shape[0]
    half = width // 2
    me, core = net.me, net.core
    device = me * 2 + core
    where = jnp.stack([me, core]).astype(I32)

    dst = jnp.arange(width)
    place = (dst // rows) % 16
    chip = me ^ (place // 4 + 4 * (place % 4))
    src = chip * (2 * rows) + (core ^ (dst // half)) * rows + dst % rows
    order = (src[:, None] == jnp.arange(width)[None, :]).astype(BF16)
    slots = jnp.arange(t)
    segment = jnp.where(segment_ids >= 0, segment_ids, -1 - slots)
    col, row = segment[:, None], segment[None, :]
    valid = (segment_ids >= 0).astype(F32)[:, None]
    spots = positions_of(segment_ids).astype(F32)
    inverse = 10000.0 ** (-jnp.arange(HEAD // 2).astype(F32) * 2.0 / HEAD)
    angles = spots[:, None] * inverse[None, :]
    cosine = jnp.tile(jnp.cos(angles), (1, 4))
    sine = jnp.sin(angles)
    sine = jnp.tile(jnp.concatenate([-sine, sine], axis=1), (1, 2))

    ffn_shard = jnp.concatenate(
        [upmatrix.reshape(rows, 4, width).transpose(1, 0, 2), downmatrix.reshape(4, rows, width)]
    )
    ffn = lax.all_gather(ffn_shard, AXES, axis=0, tiled=False)
    qk = Gather(net, jnp.concatenate([querymat, keymat], axis=1))
    vo_shard = jnp.concatenate([valuemat, outmat], axis=1)
    nine = [querybias, keybias, valuebias, outbias, downbias, firstgain, secondgain, thirdgain, fourthgain]
    small = jnp.concatenate([jnp.pad(v[None], ((0, 0), (0, LANES - rows))) for v in nine] + [upbias[None]])
    buf = small[None]
    buf = jnp.concatenate([buf, net.sibling(buf)])
    for mask in (1, 2, 4, 8):
        buf = jnp.concatenate([buf, net.swap(buf, mask)])
    line, buf, vo_shard = after(qk.line, buf, vo_shard)
    qk.spread(line)
    vo = Gather(net, vo_shard)

    picks = (jnp.arange(32)[:, None] ^ device) == jnp.arange(32)[None, :]
    small_all = dot(picks.astype(BF16), buf.reshape(32, -1)).reshape(32, 10, LANES)
    b_q, b_k, b_v, b_o, b_d, g1, g2, g3, g4 = (
        small_all[:, i, :rows].reshape(1, width) for i in range(9)
    )
    b_up = small_all[:, 9].reshape(1, hidden)
    inputs = activations.astype(F32)
    normed = (inputs * inverse_rms(inputs) * g1).astype(BF16)
    turned = dot_t(order, normed).astype(BF16)
    x_own, x_sib = turned[:half], turned[half:]

    x, y, line = after(qk.x, qk.y, vo.line)
    qk.corner(x, y)
    vo.spread(line)
    d01, d23, x_sib, normed, tables, vectors = after(
        qk.d01,
        qk.d23,
        x_sib,
        normed,
        (cosine, sine, col, row, valid, order),
        (b_q, b_k, b_v, b_o, b_d, g2, g3, g4, b_up),
    )
    cosine, sine, col, row, valid, order = tables
    b_q, b_k, b_v, b_o, b_d, g2, g3, g4, b_up = vectors
    qk.finish(d01, d23)
    x_oth = net.sibling(x_sib)
    x, y = after(vo.x, vo.y)
    vo.corner(x, y)
    qk_pieces = qk.pieces()
    qk_rot = project(where, normed, qk_pieces, 2, jnp.concatenate([b_q, b_k], axis=1), (cosine, sine))
    d01, d23, qk_rot = after(vo.d01, vo.d23, qk_rot)
    vo.finish(d01, d23)
    vo_pieces = vo.pieces()
    v = project(where, normed, vo_pieces, 1, b_v)
    mixed, lse = attend(qk_rot, v, col, row)
    m_own, m_sib, att, mid, normed_mid, n_own, n_sib = out_project(
        where, mixed, order, activations, b_o, g2, g3, vo_pieces
    )
    m_oth = net.sibling(m_sib)
    n_oth = net.sibling(n_sib)
    a_own, a_sib, slope, layer_out, dc, down_sums, power = feed_forward(
        where, normed_mid, b_up, b_d, mid, cotangent, valid, g4, ffn
    )
    a_oth = net.sibling(a_sib)
    ffn_down = ffn.reshape(16, 2, 8, rows, width)

    dc_oth = net.sibling(dc)
    de, up_bias_sum = down_back(dc, slope, ffn_down)
    de, dc_oth, a_oth = after(de, dc_oth, a_oth)

    de_oth = net.sibling(de)
    slopes, de, de_oth = after(block_slopes(where, a_own, a_oth, dc, dc_oth), de, de_oth)

    down_sum = Scatter(net, slopes)
    down_sum.a()
    back = up_back(where, de, mid, att, cotangent, valid, g2, g3, ffn, vo_pieces)
    back, de, got, n_own, x23, y01 = after(back, de, down_sum.got, n_own, down_sum.x23, down_sum.y01)
    dmid, datt, dmix, mid_sums = back

    down_sum.c(x23, y01)
    fold = down_sum.fold_b(got)
    datt_oth = net.sibling(datt)
    slopes = row_slopes(n_own, n_oth, de, de_oth, 4)
    slopes, fold, datt_oth, datt, dmix, last = after(slopes, fold, datt_oth, datt, dmix, down_sum.last)

    down_sum.b(fold)
    part = down_sum.fold_last(last)
    steps = width // LANES // 2
    part_a = attend_back(qk_rot, v, dmix, lse, col, row, cosine, sine, 0, steps)
    part_a, dmix, slopes, got, part = after(part_a, dmix, slopes, down_sum.got, part)
    d_a, sums_a = part_a

    up_sum = Scatter(net, slopes)
    up_sum.a()
    fold = down_sum.fold_near(got, part)
    a_other = net.sibling(d_a)
    part_b = attend_back(qk_rot, v, dmix, lse, col, row, cosine, sine, steps, steps)
    part_b, datt, up_got, fold, a_other, m_own, x23, y01 = after(
        part_b, datt, up_sum.got, fold, a_other, m_own, up_sum.x23, up_sum.y01
    )
    d_b, sums_b = part_b

    up_sum.c(x23, y01)
    down_sum.near(fold)
    b_other = net.sibling(d_b)
    slopes = row_slopes(m_own, m_oth, datt, datt_oth, 1, 3)
    slopes, b_other, d_a, d_b, a_other, up_got = after(slopes, b_other, d_a, d_b, a_other, up_got)
    up_fold = up_sum.fold_b(up_got)
    slopes = qkv_slopes(x_own, x_oth, d_a, d_b, a_other, b_other, slopes)
    slopes, up_fold, up_last, got, d_a, d_b = after(
        slopes, up_fold, up_sum.last, down_sum.got, d_a, d_b
    )

    up_sum.b(up_fold)
    att_sum = Scatter(net, slopes)
    att_sum.a()
    part = up_sum.fold_last(up_last)
    down_sum.far(down_sum.fold_far(got))
    input_gradient, first_sum = in_back(where, d_a, d_b, activations, dmid, g1, qk_pieces, vo_pieces)
    sums = jnp.concatenate([sums_a, sums_b], axis=1) + mid_sums + down_sums
    sums = jnp.concatenate(
        [
            sums,
            first_sum,
            up_bias_sum.reshape(4, width),
            jnp.pad(power, ((0, 2), (0, width - LANES))),
        ]
    )
    sums, up_got, part, down_got, got, x23, y01 = after(
        sums, up_sum.got, part, down_sum.got, att_sum.got, att_sum.x23, att_sum.y01
    )

    att_sum.c(x23, y01)
    up_sum.near(up_sum.fold_near(up_got, part))
    fold = att_sum.fold_b(got)
    down_total = down_sum.result(down_got)
    sums = sums + net.sibling(sums)
    sums = sums + net.swap(sums, 1)
    sums, up_got, fold, last = after(sums, up_sum.got, fold, att_sum.last)

    att_sum.b(fold)
    up_sum.far(up_sum.fold_far(up_got))
    part = att_sum.fold_last(last)
    sums = sums + net.swap(sums, 2)
    sums = sums + net.swap(sums, 4)
    got, sums, part, up_got = after(att_sum.got, sums, part, up_sum.got)

    att_sum.near(att_sum.fold_near(got, part))
    up_total = up_sum.result(up_got)
    sums = sums + net.swap(sums, 8)
    own = lax.dynamic_slice_in_dim(sums[:9], device * rows, rows, 1)
    own_up = lax.dynamic_slice_in_dim(sums[9:13].reshape(-1), device * block, block, 0)
    got, own, own_up, power_sum = after(att_sum.got, own, own_up, sums[13, 0])

    att_sum.far(att_sum.fold_far(got))
    att_total = att_sum.result(att_sum.got)
    qkv_total = [att_total[:, i * width : (i + 1) * width] for i in range(3)]
    out_total = att_total[:, 3 * width :]

    output_power = power_sum / (t * 32)
    own = [own[i] for i in (0, 1, 2, 5, 7, 8, 4, 3, 6)]
    return (
        layer_out,
        input_gradient,
        *qkv_total,
        out_total,
        up_total,
        down_total,
        own[0],
        own[1],
        own[2],
        own[3],
        own_up,
        own[4],
        own[5],
        own[6],
        own[7],
        own[8],
        output_power,
    )


def shards(*args):
    rows, length = args[3].shape[0], args[0].shape[0]
    if lax.axis_size("wide") == 16 and rows == 32 and length == 512:
        return shards_16(*args)
    return shards_any(*args)


def solution(mesh):
    matrix = P(AXES, None)
    vector = P(AXES)
    return jax.shard_map(
        shards,
        mesh=mesh,
        in_specs=(matrix, vector, matrix) + (matrix,) * 6 + (vector,) * 10,
        out_specs=(matrix,) * 8 + (vector,) * 10 + (P(),),
        check_vma=False,
    )
```
